32 devices in a mesh: grp: 2 (over y), visit: 16 (over z, x, core).
Axes of the slice: x: 2, y: 2, z: 4, core: 2. Of those that a mesh axis runs over, the one named last changes fastest.
Arguments:
- science: float32 [8192, 1024], P(('grp', 'visit')), parts along dimension 0, may hold values from -6 to 6
- patches: float32 [256, 256, 256], P(('grp', 'visit')), parts along dimension 0, may hold values from -6 to 6
- margin: int32 [128, 3], P('grp'), parts along dimension 0, may hold values from 0 to 255, as said below
- kernel_coef: float32 [27, 128], P(None, ('grp', 'visit')), parts along dimension 1, may hold values from -4 to 4
- ccd_first: int32 [32], P('grp'), parts along dimension 0, may hold values 0 or 1
Outputs:
- patch_mean: float32 [256, 256, 256], P(('grp', 'visit')), parts along dimension 0
The draws below stay inside these ranges and needn't reach their ends.
There are 2 independent parts, one for each index of `grp`. The reference program is written for one: setup_inputs(seed, part) draws one part's arguments, and reference() takes and returns one part's arrays. A program takes and returns all parts, laid end to end along the dimension named above; each array names one. Nothing has to cross between parts.
Inputs may be any that keep to these rules, and one draw needn't show every extreme that they name: `margin`: column 0 is a patch id, columns 1 and 2 are offsets below 256. A tile of strip d names a patch owned by strip d - 1, d or d + 1. Among the 4 tiles of one strip at most 2 name patches of one owner (patch id // 8), and in every strip some owner is named exactly 2 times.
All inputs are finite; a program needn't handle non-finite values.
Results may differ from the reference program's by a relative error of at most 0.004.
Values may be sent and summed in bfloat16 or wider, within the bound.
No kernel may reach another device: no remote copies, remote signals or barrier semaphores. Data moves between devices by JAX's collectives and lax.ppermute only.
A program may use at most 64 MiB of HBM per device.

```python
import jax
import jax.numpy as jnp
from jax import lax

TILE = 256
RADIUS = 10
SIGMAS = 3
ORDERS = 3
NBASIS = 27
TILES_DEV = 4
PATCH_DEV = 8
OWNERS = 16
CAP = 2
TILES = 64
PATCHES = 128
ROWS = 4096
STRIP = 1024


def draw_margin(key, part):
    keys = jax.random.split(key, 6)
    strips = jnp.arange(OWNERS)
    first_pick = jax.random.randint(keys[0], (OWNERS,), 0, 3) - 1
    end_pick = jax.random.randint(keys[1], (OWNERS,), 0, 2)
    favored = jnp.where(strips == 0, end_pick, jnp.where(strips == OWNERS - 1, end_pick - 1, first_pick))
    pick_other = jax.random.randint(keys[2], (OWNERS, TILES_DEV), 0, 2)
    lower_other = jnp.where(favored == -1, 0, -1)
    upper_other = jnp.where(favored == 1, 0, 1)
    middle_other = jnp.where(pick_other == 0, lower_other[:, None], upper_other[:, None])
    end_other = jnp.where(strips == 0, 1 - favored, -1 - favored)
    at_end = (strips == 0) | (strips == OWNERS - 1)
    other = jnp.where(at_end[:, None], end_other[:, None], middle_other)
    positions = jnp.arange(TILES_DEV)
    offset_grid = jnp.where(positions[None, :] < CAP, favored[:, None], other)
    shuffle_keys = jax.random.randint(keys[3], (OWNERS, TILES_DEV), 0, 1048576) * TILES_DEV + positions[None, :]
    order = jnp.argsort(shuffle_keys, axis=1)
    offset_grid = jnp.take_along_axis(offset_grid, order, axis=1)
    owners_drawn = strips[:, None] + offset_grid
    local_patch = jax.random.randint(keys[4], (OWNERS, TILES_DEV), 0, PATCH_DEV)
    patch_ids = (owners_drawn * PATCH_DEV + local_patch).reshape(TILES, 1)
    offsets = jax.random.randint(keys[5], (TILES, 2), 0, TILE)
    return jnp.concatenate([patch_ids, offsets], axis=1).astype(jnp.int32)


def with_ends(entries, key, smallest, largest):
    extent = entries.shape
    spot = [jax.random.randint(jax.random.fold_in(key, axis), (), 0, extent[axis]) for axis in range(len(extent))]
    entries = entries.at[tuple(spot)].set(smallest)
    longest = extent.index(max(extent))
    spot[longest] = (spot[longest] + 1) % extent[longest]
    return entries.at[tuple(spot)].set(largest)


def levels(stream_key, shape, cuts, least, top_value):
    level, own = 1.0, jax.random.fold_in(stream_key, 6)
    for axis_at, blocks in cuts:
        draws = jnp.exp(jax.random.uniform(jax.random.fold_in(own, axis_at), (blocks,), jnp.float32, least / len(cuts), top_value / len(cuts)))
        level = level * jnp.repeat(draws, shape[axis_at] // blocks).reshape([-1 if axis == axis_at else 1 for axis in range(len(shape))])
    return level


def scatter_about(stream_key, extent, scale, reach, cuts=(), dtype=jnp.bfloat16):
    factor_of = levels(stream_key, extent, cuts, -0.22, 0.18) if cuts else 1.0
    array = jax.random.normal(stream_key, extent, jnp.float32) * scale * factor_of
    return jnp.minimum(jnp.maximum(array, -reach), reach).astype(dtype)


def setup_inputs(seed: int = 0, part: int = 0) -> dict:
    splits = jax.random.split(jax.random.key(seed), 6)
    part_splits = jax.random.split(jax.random.fold_in(splits[5], part), 6)
    science = scatter_about(part_splits[0], (ROWS, STRIP), 1.0, 6.0, ((0, 16),), jnp.float32)
    patches = scatter_about(part_splits[1], (PATCHES, TILE, TILE), 1.0, 6.0, ((0, 16),), jnp.float32)
    margin = draw_margin(jax.random.fold_in(jax.random.fold_in(splits[5], part), 71), part)
    kernel_coef = scatter_about(part_splits[3], (NBASIS, TILES), 1.0, 4.0, ((1, 16),), jnp.float32)
    ccd_first = with_ends((jax.random.randint(part_splits[4], (OWNERS,), 0, 4) < 1).astype(jnp.int32), jax.random.fold_in(part_splits[4], 1), 0, 1)
    return {"science": science, "patches": patches, "margin": margin, "kernel_coef": kernel_coef, "ccd_first": ccd_first}


def basis_table():
    width = TILE + 2 * RADIUS
    offsets = (jnp.arange(width)[None, :] - jnp.arange(TILE)[:, None] - RADIUS).astype(jnp.float32)
    inside = jnp.abs(offsets) <= RADIUS
    taps = jnp.arange(-RADIUS, RADIUS + 1).astype(jnp.float32)
    tables = []
    for sigma_index in range(SIGMAS):
        sigma = 0.75 * 2.0 ** sigma_index
        normal_sum = jnp.sum(jnp.exp(-taps * taps / (2.0 * sigma * sigma)))
        profile = jnp.where(inside, jnp.exp(-offsets * offsets / (2.0 * sigma * sigma)) / normal_sum, 0.0)
        tables.append(jnp.stack([profile * (offsets / sigma) ** order_index for order_index in range(ORDERS)]))
    return jnp.stack(tables)


def shift_tiles(stack, down, right):
    span = stack.shape[1]
    positions = jnp.arange(span)
    row_source = (positions[None, :] - down[:, None]) % span
    moved = jnp.take_along_axis(stack, row_source[:, :, None], axis=1)
    col_source = (positions[None, :] - right[:, None]) % span
    return jnp.take_along_axis(moved, col_source[:, None, :], axis=2)


def match_strip(extended, science_strip, weights):
    table = basis_table()
    width = TILE + 2 * RADIUS
    starts = jnp.arange(TILES_DEV)[:, None] * TILE + jnp.arange(width)[None, :]
    windows = jnp.take(extended, starts, axis=1)
    mixing = weights.reshape(SIGMAS, ORDERS, ORDERS, TILES_DEV)
    mixed = jnp.einsum('spqt,sqij->tspij', mixing, table, precision=lax.Precision.HIGHEST).astype(jnp.bfloat16)
    vertical = jnp.einsum('tspij,jtk->tspik', mixed.astype(jnp.float32), windows.astype(jnp.float32),
                          precision=lax.Precision.HIGHEST).astype(jnp.bfloat16)
    across = jnp.swapaxes(table, 2, 3).astype(jnp.bfloat16)
    matched = jnp.einsum('tspik,spkl->til', vertical.astype(jnp.float32), across.astype(jnp.float32),
                         precision=lax.Precision.HIGHEST)
    science_tiles = science_strip.reshape(TILE, TILES_DEV, TILE).transpose(1, 0, 2)
    return science_tiles - matched


def reference(science, patches, margin, kernel_coef, ccd_first):
    templ16 = patches.astype(jnp.bfloat16)
    patch_ids = margin[:, 0]
    down = margin[:, 1]
    right = margin[:, 2]
    aligned = shift_tiles(jnp.take(templ16, patch_ids, axis=0), down, right)
    strips = aligned.reshape(OWNERS, TILES_DEV, TILE, TILE).transpose(0, 2, 1, 3).reshape(OWNERS, TILE, STRIP)
    device_ids = jnp.arange(OWNERS)
    keep_top = (device_ids > 0) & (ccd_first == 0)
    next_first = jnp.concatenate([ccd_first[1:], jnp.ones((1,), jnp.int32)])
    keep_bottom = next_first == 0
    zero_rows = jnp.zeros((1, RADIUS, STRIP), jnp.bfloat16)
    above = jnp.concatenate([zero_rows, strips[:-1, TILE - RADIUS:, :]], axis=0)
    below = jnp.concatenate([strips[1:, :RADIUS, :], zero_rows], axis=0)
    above = jnp.where(keep_top[:, None, None], above, jnp.zeros_like(above))
    below = jnp.where(keep_bottom[:, None, None], below, jnp.zeros_like(below))
    extended = jnp.concatenate([above, strips, below], axis=1)
    extended = jnp.pad(extended, ((0, 0), (0, 0), (RADIUS, RADIUS)))
    science_blocks = science.reshape(OWNERS, TILE, STRIP)
    coef_blocks = kernel_coef.reshape(NBASIS, OWNERS, TILES_DEV).transpose(1, 0, 2)
    diffs = lax.map(lambda items: match_strip(items[0], items[1], items[2]),
                    (extended, science_blocks, coef_blocks))
    diffs = diffs.reshape(TILES, TILE, TILE)
    back = shift_tiles(diffs, -down, -right)
    sums = jax.ops.segment_sum(back, patch_ids, num_segments=PATCHES)
    counts = jax.ops.segment_sum(jnp.ones((TILES,), jnp.float32), patch_ids, num_segments=PATCHES)
    return sums / jnp.maximum(counts, 1.0)[:, None, None]
```

```python
import functools

import jax
import jax.numpy as jnp
import numpy as np
from jax import lax
from jax.experimental import pallas as pl
from jax.experimental.pallas import tpu as pltpu
from jax.sharding import PartitionSpec as P

TILE = 256
HALF = 128
RADIUS = 10
SIGMAS = 3
ORDERS = 3
EDGE = 16
CAP = 2
STRIPS = 3
SLOTS = STRIPS * CAP
KINDS = 4
TOP, BOTTOM, LEFT, RIGHT = range(KINDS)
PIECES = SLOTS * KINDS
FRAME_ROWS = PIECES * EDGE
COEF_ROWS = 32


def owned_slots(margin, owner, strips, per_strip, owned):
    slots = []
    for q in range(STRIPS):
        strip = owner - 1 + q
        inside = (strip >= 0) & (strip < strips)
        base = jnp.clip(strip, 0, strips - 1) * per_strip
        count = jnp.int32(0)
        found = [jnp.int32(-1) for _ in range(CAP)]
        for s in range(per_strip):
            mine = inside & (lax.div(margin[(base + s) * 3], owned) == owner)
            for j in range(CAP):
                found[j] = jnp.where(mine & (count == j), base + s, found[j])
            count = count + jnp.where(mine, 1, 0)
        slots.extend(found)
    return slots


def partner_sign(owner):
    return 1 - 2 * lax.rem(owner, 2)


def pack_kernel(sizes, margin, coef, patches, science, aligned, to_chip, to_next, to_far, own_coef,
                patch_buf, science_buf, slot_of, patch_sem, science_sem):
    strips, per_strip, owned = sizes
    owner = lax.axis_index("visit")
    sign = partner_sign(owner)
    slots = owned_slots(margin, owner, strips, per_strip, owned)
    for k in range(SLOTS):
        slot_of[k] = slots[k]

        @pl.when(slots[k] >= 0)
        def _(k=k):
            local = lax.rem(margin[jnp.maximum(slots[k], 0) * 3], owned)
            pltpu.make_async_copy(patches.at[local], patch_buf.at[k], patch_sem.at[k]).start()

    whole = pltpu.make_async_copy(science, science_buf, science_sem)
    whole.start()

    def slot_step(k, carry):
        tile = slot_of[k]

        @pl.when(tile >= 0)
        def _():
            down = margin[tile * 3 + 1]
            right = margin[tile * 3 + 2]
            local = lax.rem(margin[tile * 3], owned)
            pltpu.make_async_copy(patches.at[local], patch_buf.at[k], patch_sem.at[k]).wait()
            moved = pltpu.roll(pltpu.roll(patch_buf[k], down, 0), right, 1)
            moved16 = moved.astype(jnp.bfloat16)
            aligned[k] = moved16
            row = k * KINDS * EDGE
            to_chip[pl.ds(row + TOP * EDGE, EDGE), :] = moved16[:EDGE]
            to_chip[pl.ds(row + BOTTOM * EDGE, EDGE), :] = moved16[TILE - EDGE :]
            left = jnp.transpose(moved[:, :HALF])[:EDGE]
            right_edge = jnp.transpose(moved[:, TILE - HALF :])[HALF - EDGE :]
            to_chip[pl.ds(row + LEFT * EDGE, EDGE), :] = left.astype(jnp.bfloat16)
            to_chip[pl.ds(row + RIGHT * EDGE, EDGE), :] = right_edge.astype(jnp.bfloat16)

        return carry

    lax.fori_loop(0, SLOTS, slot_step, 0)

    @pl.when(sign < 0)
    def _():
        for j in range(CAP):
            source = (((STRIPS - 1) * CAP + j) * KINDS + BOTTOM) * EDGE
            to_far[j * EDGE : (j + 1) * EDGE, :] = to_chip[source : source + EDGE, :]

    @pl.when(sign > 0)
    def _():
        for j in range(CAP):
            source = (j * KINDS + TOP) * EDGE
            to_far[j * EDGE : (j + 1) * EDGE, :] = to_chip[source : source + EDGE, :]

    lane4 = lax.broadcasted_iota(jnp.int32, coef.shape, 1)
    lanes = lax.broadcasted_iota(jnp.int32, (COEF_ROWS, TILE), 1)
    bases = coef.shape[0]
    coefs = coef[...]

    def coef_block(offset):
        block = jnp.zeros((COEF_ROWS, TILE), jnp.float32)
        count = jnp.int32(0)
        for s in range(per_strip):
            tile = owner * per_strip + s
            match = lax.div(margin[tile * 3], owned) == owner + offset
            column = jnp.sum(jnp.where(lane4 == s, coefs, 0.0), axis=1, keepdims=True)
            column = jnp.concatenate([column, jnp.zeros((COEF_ROWS - bases, 1), jnp.float32)], axis=0)
            high = column.astype(jnp.bfloat16).astype(jnp.float32)
            rest = column - high
            middle = rest.astype(jnp.bfloat16).astype(jnp.float32)
            low = rest - middle
            for part, value in enumerate((high, middle, low)):
                block = block + jnp.where(match & (lanes == count * 3 + part), value, 0.0)
            count = count + jnp.where(match, 1, 0)
        return block.astype(jnp.bfloat16)

    own_coef[...] = coef_block(0)
    chip_rows = FRAME_ROWS + CAP * TILE
    to_chip[chip_rows : chip_rows + COEF_ROWS, :] = coef_block(sign)
    to_next[CAP * TILE : CAP * TILE + COEF_ROWS, :] = coef_block(-sign)
    whole.wait()
    for ref, offset, first in ((to_chip, sign, FRAME_ROWS), (to_next, -sign, 0)):
        count = jnp.int32(0)
        for s in range(per_strip):
            match = lax.div(margin[(owner * per_strip + s) * 3], owned) == owner + offset

            @pl.when(match)
            def _(ref=ref, first=first, count=count, s=s):
                start = pl.multiple_of(first + count * TILE, EDGE)
                ref[pl.ds(start, TILE), :] = science_buf[:, s * TILE : (s + 1) * TILE].astype(jnp.bfloat16)

            count = count + jnp.where(match, 1, 0)


def profile(u, sigma, order):
    taps = np.arange(-RADIUS, RADIUS + 1).astype(np.float32)
    total = float(np.sum(np.exp(-taps * taps / np.float32(2.0 * sigma * sigma)), dtype=np.float32))
    shape = jnp.where(jnp.abs(u) <= RADIUS, jnp.exp(-u * u / (2.0 * sigma * sigma)) / total, 0.0)
    for _ in range(order):
        shape = shape * (u / sigma)
    return shape


def match_kernel(sizes, margin, ccd_first, aligned, from_chip, frames_next, science_next, frames_across, from_far,
                 own_frames, own_coef, science, out,
                 frames, aligned_buf, far_buf, science_buf, coefs, local_science, window, spread, mixes, table, across,
                 total, slot_of, sems):
    strips, per_strip, owned = sizes
    owner = lax.axis_index("visit")
    sign = partner_sign(owner)
    copies = [
        (own_frames.at[pl.ds(0, FRAME_ROWS)], frames.at[3]),
        (from_chip.at[pl.ds(0, FRAME_ROWS)], frames.at[4]),
        (frames_next.at[pl.ds(0, FRAME_ROWS)], frames.at[2]),
        (frames_next.at[pl.ds(FRAME_ROWS, FRAME_ROWS)], frames.at[1]),
        (frames_across.at[pl.ds(0, FRAME_ROWS)], frames.at[5]),
        (frames_across.at[pl.ds(FRAME_ROWS, FRAME_ROWS)], frames.at[6]),
        (from_far, far_buf),
        (own_coef, coefs.at[1]),
        (from_chip.at[pl.ds(FRAME_ROWS + CAP * TILE, COEF_ROWS)], coefs.at[2]),
        (science_next.at[pl.ds(CAP * TILE, COEF_ROWS)], coefs.at[0]),
        (from_chip.at[pl.ds(FRAME_ROWS, CAP * TILE)], science_buf.at[1]),
        (science_next.at[pl.ds(0, CAP * TILE)], science_buf.at[0]),
        (science, local_science),
        (aligned, aligned_buf),
    ]
    started = [pltpu.make_async_copy(a, b, sems.at[n]) for n, (a, b) in enumerate(copies)]
    for copy in started:
        copy.start()

    slots = owned_slots(margin, owner, strips, per_strip, owned)
    ids = [jnp.where(t >= 0, margin[jnp.maximum(t, 0) * 3], -1) for t in slots]
    for k in range(SLOTS):
        slot_of[k] = slots[k]
        slot_of[SLOTS + k] = sum(jnp.where(other == ids[k], 1, 0) for other in ids)

    u = (lax.broadcasted_iota(jnp.int32, (HALF, TILE), 1) - lax.broadcasted_iota(jnp.int32, (HALF, TILE), 0) - EDGE)
    u = u.astype(jnp.float32)
    w = lax.broadcasted_iota(jnp.int32, (TILE, HALF), 0) - lax.broadcasted_iota(jnp.int32, (TILE, HALF), 1)
    w = jnp.where(w > HALF, w - TILE, w).astype(jnp.float32)
    for g in range(SIGMAS):
        sigma = 0.75 * 2.0**g
        for k in range(ORDERS):
            n = g * ORDERS + k
            table[n] = profile(u, sigma, k)
            across[:, n * HALF : (n + 1) * HALF] = profile(w, sigma, k).astype(jnp.bfloat16)
    window_rows = TILE + 2 * EDGE
    for n in range(SIGMAS * ORDERS):
        spread[n, window_rows:, :] = jnp.zeros((HALF + TILE - window_rows, TILE), jnp.bfloat16)
    out[...] = jnp.zeros(out.shape, jnp.float32)
    for copy in started:
        copy.wait()
    far_strip = jnp.where(sign > 0, STRIPS - 1, 0)
    far_kind = jnp.where(sign > 0, BOTTOM, TOP)
    for j in range(CAP):
        start = pl.multiple_of(((far_strip * CAP + j) * KINDS + far_kind) * EDGE, EDGE)
        frames[0, pl.ds(start, EDGE), :] = far_buf[j * EDGE : (j + 1) * EDGE, :]

    def piece(strip, position, kind, allowed):
        inside = (strip >= 0) & (strip < strips) & (position >= 0) & (position < per_strip) & allowed
        base = jnp.clip(strip, 0, strips - 1) * per_strip
        where = jnp.clip(position, 0, per_strip - 1)
        its_owner = lax.div(margin[(base + where) * 3], owned)
        rank = jnp.int32(0)
        for s in range(per_strip):
            same = lax.div(margin[(base + s) * 3], owned) == its_owner
            rank = rank + jnp.where(same & (s < where), 1, 0)
        relative = jnp.clip(strip, 0, strips - 1) - its_owner + 1
        member = jnp.clip((its_owner - owner) * sign + 3, 0, 6)
        row = jnp.clip((relative * CAP + rank) * KINDS + kind, 0, PIECES - 1) * EDGE
        value = frames[member, pl.ds(pl.multiple_of(row, EDGE), EDGE), :]
        return jnp.where(inside, value, jnp.zeros_like(value))

    def slot_step(k, carry):
        tile = slot_of[k]

        @pl.when(tile >= 0)
        def _():
            q = lax.div(k, CAP)
            j = lax.rem(k, CAP)
            strip = owner - 1 + q
            position = tile - strip * per_strip
            down = margin[tile * 3 + 1]
            right = margin[tile * 3 + 2]
            local = lax.rem(margin[tile * 3], owned)
            yes = owner >= 0
            keep_top = (strip > 0) & (ccd_first[strip] == 0)
            keep_bottom = (strip < strips - 1) & (ccd_first[jnp.minimum(strip + 1, strips - 1)] == 0)

            from_right = piece(strip, position + 1, LEFT, yes).astype(jnp.float32)
            from_left = piece(strip, position - 1, RIGHT, yes).astype(jnp.float32)
            sides = jnp.concatenate(
                [from_right, jnp.zeros((HALF - 2 * EDGE, TILE), jnp.float32), from_left], axis=0
            )
            sides = jnp.transpose(sides).astype(jnp.bfloat16)

            def place(first, rows, middle_a, middle_b, left_b, right_a):
                low = lax.broadcasted_iota(jnp.int32, (rows, HALF), 1) < HALF // 2
                window[0, first : first + rows, :HALF] = middle_a
                window[0, first : first + rows, HALF:] = jnp.where(low, middle_b, left_b)
                window[1, first : first + rows, :HALF] = middle_b
                window[1, first : first + rows, HALF:] = jnp.where(low, right_a, middle_a)

            center = aligned_buf[k]
            place(EDGE, TILE, center[:, :HALF], center[:, HALF:], sides, sides)
            for first, neighbour, kind, keep in (
                (0, strip - 1, BOTTOM, keep_top),
                (EDGE + TILE, strip + 1, TOP, keep_bottom),
            ):
                middle = piece(neighbour, position, kind, keep)
                left = piece(neighbour, position - 1, kind, keep)
                right_piece = piece(neighbour, position + 1, kind, keep)
                place(first, EDGE, middle[:, :HALF], middle[:, HALF:], left[:, HALF:], right_piece[:, :HALF])

            columns = SIGMAS * ORDERS
            for c in range(2):
                for n in range(0, columns, 2):
                    wide = min(2, columns - n)
                    h = jnp.dot(
                        window[c], across[:, n * HALF : (n + wide) * HALF], preferred_element_type=jnp.float32
                    ).astype(jnp.bfloat16)
                    for m in range(wide):
                        spread[n + m, :window_rows, c * HALF : (c + 1) * HALF] = h[:, m * HALF : (m + 1) * HALF]

            member = (q - 1) * sign + 1
            block = coefs[member].astype(jnp.float32)
            lanes = lax.broadcasted_iota(jnp.int32, block.shape, 1)
            mine = (lanes >= j * 3) & (lanes < j * 3 + 3)
            column = jnp.sum(jnp.where(mine, block, 0.0), axis=1, keepdims=True)
            for g in range(SIGMAS):
                for h in range(ORDERS):
                    mix = jnp.zeros((HALF, TILE), jnp.float32)
                    for v in range(ORDERS):
                        n = (g * ORDERS + h) * ORDERS + v
                        mix = mix + column[n : n + 1, :] * table[g * ORDERS + v]
                    mixes[g * ORDERS + h] = mix.astype(jnp.bfloat16)
            for r in range(2):
                acc = jnp.zeros((HALF, TILE), jnp.float32)
                for n in range(columns):
                    acc = acc + jnp.dot(
                        mixes[n], spread[n, r * HALF : r * HALF + TILE, :], preferred_element_type=jnp.float32
                    )
                total[r * HALF : (r + 1) * HALF, :] = acc

            @pl.when(q == 1)
            def _():
                start = pl.multiple_of(position * TILE, TILE)
                total[...] = local_science[:, pl.ds(start, TILE)] - total[...]

            @pl.when(q != 1)
            def _():
                start = pl.multiple_of(j * TILE, TILE)
                arrived = science_buf[lax.div(member, 2), pl.ds(start, TILE), :]
                total[...] = arrived.astype(jnp.float32) - total[...]

            back = pltpu.roll(pltpu.roll(total[...], lax.rem(TILE - down, TILE), 0), lax.rem(TILE - right, TILE), 1)
            count = slot_of[SLOTS + k]
            share = jnp.float32(1.0)
            for n in range(2, SLOTS + 1):
                share = jnp.where(count == n, jnp.float32(1.0 / n), share)
            out[local] = out[local] + back * share

        return carry

    lax.fori_loop(0, SLOTS, slot_step, 0)


def body(science, patches, margin, kernel_coef, ccd_first):
    strips = lax.axis_size("visit")
    owned = patches.shape[0]
    per_strip = science.shape[1] // TILE
    sizes = (strips, per_strip, owned)
    flat = margin.reshape(-1)
    smem = pl.BlockSpec(memory_space=pltpu.SMEM)
    vmem = pl.BlockSpec(memory_space=pltpu.VMEM)
    hbm = pl.BlockSpec(memory_space=pl.ANY)
    bf16 = jnp.bfloat16
    f32 = jnp.float32
    chip_rows = FRAME_ROWS + CAP * TILE + COEF_ROWS
    next_rows = CAP * TILE + COEF_ROWS
    far_rows = CAP * EDGE
    aligned, to_chip, to_next, to_far, own_coef = pl.pallas_call(
        functools.partial(pack_kernel, sizes),
        out_shape=(
            jax.ShapeDtypeStruct((SLOTS, TILE, TILE), bf16),
            jax.ShapeDtypeStruct((chip_rows, TILE), bf16),
            jax.ShapeDtypeStruct((next_rows, TILE), bf16),
            jax.ShapeDtypeStruct((far_rows, TILE), bf16),
            jax.ShapeDtypeStruct((COEF_ROWS, TILE), bf16),
        ),
        in_specs=[smem, vmem, hbm, hbm],
        out_specs=(vmem, vmem, vmem, vmem, vmem),
        scratch_shapes=[
            pltpu.VMEM((SLOTS, TILE, TILE), f32),
            pltpu.VMEM((TILE, per_strip * TILE), f32),
            pltpu.SMEM((SLOTS,), jnp.int32),
            pltpu.SemaphoreType.DMA((SLOTS,)),
            pltpu.SemaphoreType.DMA,
        ],
        name="pack",
    )(flat, kernel_coef, patches, science)

    on_chip = [(i, i ^ 1) for i in range(strips)]
    next_chip = [p for i in range(1, strips - 1, 2) for p in ((i, i + 1), (i + 1, i))]
    far = [p for i in range(1, strips - 3, 2) for p in ((i, i + 3), (i + 3, i))]
    from_far = lax.ppermute(to_far, "visit", far)
    from_chip = lax.ppermute(to_chip, "visit", on_chip)
    both = jnp.concatenate([to_chip[:FRAME_ROWS], from_chip[:FRAME_ROWS]], axis=0)
    frames_next = lax.ppermute(both, "visit", next_chip)
    science_next = lax.ppermute(to_next, "visit", next_chip)
    frames_across = lax.ppermute(frames_next, "visit", on_chip)

    columns = SIGMAS * ORDERS
    return pl.pallas_call(
        functools.partial(match_kernel, sizes),
        out_shape=jax.ShapeDtypeStruct(patches.shape, f32),
        in_specs=[smem, smem] + [hbm] * 9,
        out_specs=vmem,
        scratch_shapes=[
            pltpu.VMEM((7, FRAME_ROWS, TILE), bf16),
            pltpu.VMEM((SLOTS, TILE, TILE), bf16),
            pltpu.VMEM((far_rows, TILE), bf16),
            pltpu.VMEM((2, CAP * TILE, TILE), bf16),
            pltpu.VMEM((3, COEF_ROWS, TILE), bf16),
            pltpu.VMEM((TILE, per_strip * TILE), f32),
            pltpu.VMEM((2, TILE + 2 * EDGE, TILE), bf16),
            pltpu.VMEM((columns, TILE + HALF, TILE), bf16),
            pltpu.VMEM((columns, HALF, TILE), bf16),
            pltpu.VMEM((columns, HALF, TILE), f32),
            pltpu.VMEM((TILE, columns * HALF), bf16),
            pltpu.VMEM((TILE, TILE), f32),
            pltpu.SMEM((2 * SLOTS,), jnp.int32),
            pltpu.SemaphoreType.DMA((14,)),
        ],
        name="match",
    )(flat, ccd_first, aligned, from_chip, frames_next, science_next, frames_across, from_far, to_chip, own_coef, science)


def solution(mesh):
    in_specs = (
        P(("grp", "visit"), None),
        P(("grp", "visit"), None, None),
        P("grp", None),
        P(None, ("grp", "visit")),
        P("grp"),
    )
    out_specs = P(("grp", "visit"), None, None)
    return jax.shard_map(body, mesh=mesh, in_specs=in_specs, out_specs=out_specs, check_vma=False)
```

```python
import functools

import jax
import jax.numpy as jnp
import numpy as np
from jax import lax
from jax.experimental import pallas as pl
from jax.experimental.pallas import tpu as pltpu
from jax.sharding import PartitionSpec as P

TILE = 256
HALF = 128
RADIUS = 10
SIGMAS = 3
ORDERS = 3
EDGE = 16
CAP = 2
STRIPS = 3
SLOTS = STRIPS * CAP
KINDS = 4
TOP, BOTTOM, LEFT, RIGHT = range(KINDS)
PIECES = SLOTS * KINDS
COEF_ROWS = 16
NEAR = 8
PIECE_ROWS = CAP * EDGE
NEAR_ROWS = COEF_ROWS + NEAR * PIECE_ROWS
RECORD = COEF_ROWS + PIECES * EDGE


def owned_slots(margin, owner, strips, per_strip, owned):
    slots = []
    for q in range(STRIPS):
        strip = owner - 1 + q
        inside = (strip >= 0) & (strip < strips)
        base = jnp.clip(strip, 0, strips - 1) * per_strip
        count = jnp.int32(0)
        found = [jnp.int32(-1) for _ in range(CAP)]
        for s in range(per_strip):
            mine = inside & (lax.div(margin[0, base + s], owned) == owner)
            for j in range(CAP):
                found[j] = jnp.where(mine & (count == j), base + s, found[j])
            count = count + jnp.where(mine, 1, 0)
        slots.extend(found)
    return slots


def sign_of(owner):
    return 1 - 2 * lax.rem(owner, 2)


def piece_position(relative, kind, sign):
    along = relative * sign
    facing = jnp.where(sign > 0, kind, jnp.where(kind == TOP, BOTTOM, jnp.where(kind == BOTTOM, TOP, kind)))
    middle = jnp.where(facing == TOP, 4, jnp.where(facing == BOTTOM, 11, facing + 3))
    return jnp.where(along < 0, facing, jnp.where(along > 0, 7 + facing, middle))


def pack_kernel(sizes, margin_hbm, coef_hbm, patches, science, aligned, to_chip, to_next, to_far,
                margin, coef, patch_buf, science_buf, slot_of, patch_sem, science_sem, small_sem):
    strips, per_strip, owned = sizes
    tables = [
        pltpu.make_async_copy(a, b, small_sem.at[n]) for n, (a, b) in enumerate(((margin_hbm, margin), (coef_hbm, coef)))
    ]
    for copy in tables:
        copy.start()
    whole = pltpu.make_async_copy(science, science_buf, science_sem)
    whole.start()
    for copy in tables:
        copy.wait()
    owner = lax.axis_index("visit")
    sign = sign_of(owner)
    slots = owned_slots(margin, owner, strips, per_strip, owned)
    for k in range(SLOTS):
        slot_of[k] = slots[k]

        @pl.when(slots[k] >= 0)
        def _(k=k):
            local = lax.rem(margin[0, jnp.maximum(slots[k], 0)], owned)
            pltpu.make_async_copy(patches.at[local], patch_buf.at[k], patch_sem.at[k]).start()

    values = coef[...]
    bases = values.shape[1]
    high = values.astype(jnp.bfloat16).astype(jnp.float32)
    middle = (values - high).astype(jnp.bfloat16).astype(jnp.float32)
    low = values - high - middle
    parts = jnp.concatenate([high, middle, low, jnp.zeros_like(low)], axis=0).astype(jnp.bfloat16)
    to_chip[:COEF_ROWS, :bases] = parts
    to_next[:COEF_ROWS, :bases] = parts

    def slot_step(k, carry):
        tile = slot_of[k]

        @pl.when(tile >= 0)
        def _():
            down = margin[1, tile]
            right = margin[2, tile]
            local = lax.rem(margin[0, tile], owned)
            pltpu.make_async_copy(patches.at[local], patch_buf.at[k], patch_sem.at[k]).wait()
            moved = pltpu.roll(pltpu.roll(patch_buf[k], down, 0), right, 1)
            moved16 = moved.astype(jnp.bfloat16)
            aligned[k] = moved16
            relative = lax.div(k, CAP) - 1
            j = lax.rem(k, CAP)
            left = jnp.transpose(moved[:, :HALF])[:EDGE]
            right_edge = jnp.transpose(moved[:, TILE - HALF :])[HALF - EDGE :]
            edges = (moved16[:EDGE], moved16[TILE - EDGE :], left.astype(jnp.bfloat16), right_edge.astype(jnp.bfloat16))
            for kind in range(KINDS):
                position = piece_position(relative, jnp.int32(kind), sign)
                row = pl.multiple_of(COEF_ROWS + (position * CAP + j) * EDGE, EDGE)
                to_chip[pl.ds(row, EDGE), :] = edges[kind]

                @pl.when(position < NEAR)
                def _(kind=kind, row=row):
                    to_next[pl.ds(row, EDGE), :] = edges[kind]

                @pl.when(position == 0)
                def _(kind=kind):
                    to_far[pl.ds(pl.multiple_of(j * EDGE, EDGE), EDGE), :] = edges[kind]

        return carry

    lax.fori_loop(0, SLOTS, slot_step, 0)
    whole.wait()
    counts = [jnp.int32(0), jnp.int32(0)]
    for s in range(per_strip):
        tile = owner * per_strip + s
        offset = lax.div(margin[0, tile], owned) - owner

        @pl.when(offset != 0)
        def _(s=s, tile=tile, offset=offset, counts=tuple(counts)):
            up = lax.rem(TILE - margin[1, tile], TILE)
            back = lax.rem(TILE - margin[2, tile], TILE)
            moved = pltpu.roll(pltpu.roll(science_buf[:, s * TILE : (s + 1) * TILE], up, 0), back, 1)
            moved16 = moved.astype(jnp.bfloat16)

            @pl.when(offset == sign)
            def _():
                to_chip[pl.ds(pl.multiple_of(RECORD + counts[0] * TILE, EDGE), TILE), :] = moved16

            @pl.when(offset != sign)
            def _():
                to_next[pl.ds(pl.multiple_of(NEAR_ROWS + counts[1] * TILE, EDGE), TILE), :] = moved16

        counts[0] = counts[0] + jnp.where(offset == sign, 1, 0)
        counts[1] = counts[1] + jnp.where(offset == -sign, 1, 0)


def profile(u, sigma, order):
    taps = np.arange(-RADIUS, RADIUS + 1).astype(np.float32)
    total = float(np.sum(np.exp(-taps * taps / np.float32(2.0 * sigma * sigma)), dtype=np.float32))
    shape = jnp.where(jnp.abs(u) <= RADIUS, jnp.exp(-u * u / (2.0 * sigma * sigma)) / total, 0.0)
    for _ in range(order):
        shape = shape * (u / sigma)
    return shape


def match_kernel(sizes, margin, ccd_first, aligned, own_record, from_chip, from_next, from_two, from_across, from_far,
                 science, out,
                 frames, window, spread, mixes, table, across, total, slot_of):
    strips, per_strip, owned = sizes
    owner = lax.axis_index("visit")
    sign = sign_of(owner)
    near = pl.ds(0, NEAR_ROWS)
    relayed = pl.ds(NEAR_ROWS, RECORD - NEAR_ROWS)
    frames[3] = own_record[:RECORD, :]
    frames[4] = from_chip[:RECORD, :]
    frames[2, near] = from_next[near, :]
    frames[1, relayed] = from_two[...]
    frames[5, near] = from_across[near, :]
    frames[6, relayed] = from_across[relayed, :]
    frames[0, pl.ds(COEF_ROWS, PIECE_ROWS)] = from_far[...]

    slots = owned_slots(margin, owner, strips, per_strip, owned)
    ids = [jnp.where(t >= 0, margin[0, jnp.maximum(t, 0)], -1) for t in slots]
    for k in range(SLOTS):
        slot_of[k] = slots[k]
        slot_of[SLOTS + k] = sum(jnp.where(other == ids[k], 1, 0) for other in ids)

    u = (lax.broadcasted_iota(jnp.int32, (HALF, TILE), 1) - lax.broadcasted_iota(jnp.int32, (HALF, TILE), 0) - EDGE)
    u = u.astype(jnp.float32)
    w = lax.broadcasted_iota(jnp.int32, (TILE, HALF), 0) - lax.broadcasted_iota(jnp.int32, (TILE, HALF), 1)
    w = jnp.where(w > HALF, w - TILE, w).astype(jnp.float32)
    for g in range(SIGMAS):
        sigma = 0.75 * 2.0**g
        for k in range(ORDERS):
            n = g * ORDERS + k
            table[n] = profile(u, sigma, k)
            across[:, n * HALF : (n + 1) * HALF] = profile(w, sigma, k).astype(jnp.bfloat16)
    window_rows = TILE + 2 * EDGE
    for n in range(SIGMAS * ORDERS):
        spread[n, window_rows:, :] = jnp.zeros((HALF + TILE - window_rows, TILE), jnp.bfloat16)
    out[...] = jnp.zeros(out.shape, jnp.float32)
    def piece(strip, position, kind, allowed):
        inside = (strip >= 0) & (strip < strips) & (position >= 0) & (position < per_strip) & allowed
        base = jnp.clip(strip, 0, strips - 1) * per_strip
        where = jnp.clip(position, 0, per_strip - 1)
        its_owner = lax.div(margin[0, base + where], owned)
        rank = jnp.int32(0)
        for s in range(per_strip):
            same = lax.div(margin[0, base + s], owned) == its_owner
            rank = rank + jnp.where(same & (s < where), 1, 0)
        relative = jnp.clip(strip, 0, strips - 1) - its_owner
        member = jnp.clip((its_owner - owner) * sign + 3, 0, 6)
        place = piece_position(relative, jnp.int32(kind), sign_of(its_owner)) * CAP + rank
        row = COEF_ROWS + jnp.clip(place, 0, PIECES - 1) * EDGE
        value = frames[member, pl.ds(pl.multiple_of(row, EDGE), EDGE), :]
        return jnp.where(inside, value, jnp.zeros_like(value))

    def slot_step(k, carry):
        tile = slot_of[k]

        @pl.when(tile >= 0)
        def _():
            q = lax.div(k, CAP)
            j = lax.rem(k, CAP)
            strip = owner - 1 + q
            position = tile - strip * per_strip
            down = margin[1, tile]
            right = margin[2, tile]
            local = lax.rem(margin[0, tile], owned)
            yes = owner >= 0
            keep_top = (strip > 0) & (ccd_first[strip] == 0)
            keep_bottom = (strip < strips - 1) & (ccd_first[jnp.minimum(strip + 1, strips - 1)] == 0)

            from_right = piece(strip, position + 1, LEFT, yes).astype(jnp.float32)
            from_left = piece(strip, position - 1, RIGHT, yes).astype(jnp.float32)
            sides = jnp.concatenate(
                [from_right, jnp.zeros((HALF - 2 * EDGE, TILE), jnp.float32), from_left], axis=0
            )
            sides = jnp.transpose(sides).astype(jnp.bfloat16)

            def place(first, rows, middle_a, middle_b, left_b, right_a):
                low = lax.broadcasted_iota(jnp.int32, (rows, HALF), 1) < HALF // 2
                window[0, first : first + rows, :HALF] = middle_a
                window[0, first : first + rows, HALF:] = jnp.where(low, middle_b, left_b)
                window[1, first : first + rows, :HALF] = middle_b
                window[1, first : first + rows, HALF:] = jnp.where(low, right_a, middle_a)

            center = aligned[k]
            place(EDGE, TILE, center[:, :HALF], center[:, HALF:], sides, sides)
            for first, neighbour, kind, keep in (
                (0, strip - 1, BOTTOM, keep_top),
                (EDGE + TILE, strip + 1, TOP, keep_bottom),
            ):
                middle = piece(neighbour, position, kind, keep)
                left = piece(neighbour, position - 1, kind, keep)
                right_piece = piece(neighbour, position + 1, kind, keep)
                place(first, EDGE, middle[:, :HALF], middle[:, HALF:], left[:, HALF:], right_piece[:, :HALF])

            columns = SIGMAS * ORDERS
            for c in range(2):
                for n in range(0, columns, 2):
                    wide = min(2, columns - n)
                    h = jnp.dot(
                        window[c], across[:, n * HALF : (n + wide) * HALF], preferred_element_type=jnp.float32
                    ).astype(jnp.bfloat16)
                    for m in range(wide):
                        spread[n + m, :window_rows, c * HALF : (c + 1) * HALF] = h[:, m * HALF : (m + 1) * HALF]

            member = (q - 1) * sign
            block = frames[member + 3, :COEF_ROWS, :HALF].astype(jnp.float32)
            rows = lax.broadcasted_iota(jnp.int32, block.shape, 0)
            mine = (lax.rem(rows, per_strip) == position) & (rows < 3 * per_strip)
            weights = jnp.sum(jnp.where(mine, block, 0.0), axis=0, keepdims=True)
            for g in range(SIGMAS):
                for h in range(ORDERS):
                    mix = jnp.zeros((HALF, TILE), jnp.float32)
                    for v in range(ORDERS):
                        n = (g * ORDERS + h) * ORDERS + v
                        mix = mix + weights[:, n : n + 1] * table[g * ORDERS + v]
                    mixes[g * ORDERS + h] = mix.astype(jnp.bfloat16)
            for r in range(2):
                acc = jnp.zeros((HALF, TILE), jnp.float32)
                for n in range(columns):
                    acc = acc - jnp.dot(
                        mixes[n], spread[n, r * HALF : r * HALF + TILE, :], preferred_element_type=jnp.float32
                    )
                total[r * HALF : (r + 1) * HALF, :] = acc

            @pl.when(q == 1)
            def _():
                start = pl.multiple_of(position * TILE, TILE)
                total[...] = total[...] + science[:, pl.ds(start, TILE)]

            total[...] = pltpu.roll(
                pltpu.roll(total[...], lax.rem(TILE - down, TILE), 0), lax.rem(TILE - right, TILE), 1
            )

            @pl.when(member == 1)
            def _():
                start = pl.multiple_of(RECORD + j * TILE, EDGE)
                total[...] = total[...] + from_chip[pl.ds(start, TILE), :].astype(jnp.float32)

            @pl.when(member == -1)
            def _():
                start = pl.multiple_of(NEAR_ROWS + j * TILE, EDGE)
                total[...] = total[...] + from_next[pl.ds(start, TILE), :].astype(jnp.float32)

            count = slot_of[SLOTS + k]
            share = jnp.float32(1.0)
            for n in range(2, SLOTS + 1):
                share = jnp.where(count == n, jnp.float32(1.0 / n), share)
            out[local] = out[local] + total[...] * share

        return carry

    lax.fori_loop(0, SLOTS, slot_step, 0)


def body(science, patches, margin, kernel_coef, ccd_first):
    strips = lax.axis_size("visit")
    owned = patches.shape[0]
    per_strip = science.shape[1] // TILE
    sizes = (strips, per_strip, owned)
    margin = margin.T
    smem = pl.BlockSpec(memory_space=pltpu.SMEM)
    vmem = pl.BlockSpec(memory_space=pltpu.VMEM)
    hbm = pl.BlockSpec(memory_space=pl.ANY)
    stays = pl.BlockSpec(memory_space=pltpu.HBM)
    bf16 = jnp.bfloat16
    f32 = jnp.float32
    aligned, to_chip, to_next, to_far = pl.pallas_call(
        functools.partial(pack_kernel, sizes),
        out_shape=(
            jax.ShapeDtypeStruct((SLOTS, TILE, TILE), bf16),
            jax.ShapeDtypeStruct((RECORD + CAP * TILE, TILE), bf16),
            jax.ShapeDtypeStruct((NEAR_ROWS + CAP * TILE, TILE), bf16),
            jax.ShapeDtypeStruct((PIECE_ROWS, TILE), bf16),
        ),
        in_specs=[stays] * 4,
        out_specs=(vmem, vmem, vmem, vmem),
        scratch_shapes=[
            pltpu.SMEM(margin.shape, jnp.int32),
            pltpu.VMEM(kernel_coef.shape[::-1], f32),
            pltpu.VMEM((SLOTS, TILE, TILE), f32),
            pltpu.VMEM((TILE, per_strip * TILE), f32),
            pltpu.SMEM((SLOTS,), jnp.int32),
            pltpu.SemaphoreType.DMA((SLOTS,)),
            pltpu.SemaphoreType.DMA,
            pltpu.SemaphoreType.DMA((2,)),
        ],
        compiler_params=pltpu.CompilerParams(vmem_limit_bytes=52 * 2**20),
        name="pack",
    )(margin, kernel_coef.T, patches, science)

    on_chip = [(i, i ^ 1) for i in range(strips)]
    next_chip = [p for i in range(1, strips - 1, 2) for p in ((i, i + 1), (i + 1, i))]
    far = [p for i in range(1, strips - 3, 2) for p in ((i, i + 3), (i + 3, i))]
    two = [p for i in range(0, strips - 2, 2) for p in ((i, i + 2), (i + 3, i + 1))]
    from_next = lax.ppermute(to_next, "visit", next_chip)
    from_two = lax.ppermute(to_chip[NEAR_ROWS:RECORD], "visit", two)
    from_far = lax.ppermute(to_far, "visit", far)
    from_chip = lax.ppermute(to_chip, "visit", on_chip)
    from_next, from_two, from_far, from_chip = lax.optimization_barrier((from_next, from_two, from_far, from_chip))
    relay = jnp.concatenate([from_next[:NEAR_ROWS], from_two], axis=0)
    from_across = lax.ppermute(relay, "visit", on_chip)

    columns = SIGMAS * ORDERS
    return pl.pallas_call(
        functools.partial(match_kernel, sizes),
        out_shape=jax.ShapeDtypeStruct(patches.shape, f32),
        in_specs=[smem, smem] + [vmem] * 8,
        out_specs=vmem,
        scratch_shapes=[
            pltpu.VMEM((7, RECORD, TILE), bf16),
            pltpu.VMEM((2, TILE + 2 * EDGE, TILE), bf16),
            pltpu.VMEM((columns, TILE + HALF, TILE), bf16),
            pltpu.VMEM((columns, HALF, TILE), bf16),
            pltpu.VMEM((columns, HALF, TILE), f32),
            pltpu.VMEM((TILE, columns * HALF), bf16),
            pltpu.VMEM((TILE, TILE), f32),
            pltpu.SMEM((2 * SLOTS,), jnp.int32),
        ],
        compiler_params=pltpu.CompilerParams(vmem_limit_bytes=24 * 2**20),
        name="match",
    )(margin, ccd_first, aligned, to_chip, from_chip, from_next, from_two, from_across, from_far, science)


def solution(mesh):
    in_specs = (
        P(("grp", "visit"), None),
        P(("grp", "visit"), None, None),
        P("grp", None),
        P(None, ("grp", "visit")),
        P("grp"),
    )
    out_specs = P(("grp", "visit"), None, None)
    return jax.shard_map(body, mesh=mesh, in_specs=in_specs, out_specs=out_specs, check_vma=False)
```

```python
import functools

import jax
import jax.numpy as jnp
import numpy as np
from jax import lax
from jax.experimental import pallas as pl
from jax.experimental.pallas import tpu as pltpu
from jax.sharding import PartitionSpec as P

TILE = 256
HALF = 128
RADIUS = 10
SIGMAS = 3
ORDERS = 3
EDGE = 16
CAP = 2
STRIPS = 3
SLOTS = STRIPS * CAP
KINDS = 4
TOP, BOTTOM, LEFT, RIGHT = range(KINDS)
PIECES = SLOTS * KINDS
COEF_ROWS = 16
NEAR = 8
PIECE_ROWS = CAP * EDGE
NEAR_ROWS = COEF_ROWS + NEAR * PIECE_ROWS
RECORD = COEF_ROWS + PIECES * EDGE
MEMBERS = 7
ENTRY = 16
HEAD = 2
REACH = HALF + 2 * EDGE
CORNER = HALF - 2 * EDGE


def owned_slots(margin, owner, strips, per_strip, owned):
    slots = []
    for q in range(STRIPS):
        strip = owner - 1 + q
        inside = (strip >= 0) & (strip < strips)
        base = jnp.clip(strip, 0, strips - 1) * per_strip
        count = jnp.int32(0)
        found = [jnp.int32(-1) for _ in range(CAP)]
        for s in range(per_strip):
            mine = inside & (lax.div(margin[0, base + s], owned) == owner)
            for j in range(CAP):
                found[j] = jnp.where(mine & (count == j), base + s, found[j])
            count = count + jnp.where(mine, 1, 0)
        slots.extend(found)
    return slots


def sign_of(owner):
    return 1 - 2 * lax.rem(owner, 2)


def piece_position(relative, kind, sign):
    along = relative * sign
    facing = jnp.where(sign > 0, kind, jnp.where(kind == TOP, BOTTOM, jnp.where(kind == BOTTOM, TOP, kind)))
    middle = jnp.where(facing == TOP, 4, jnp.where(facing == BOTTOM, 11, facing + 3))
    return jnp.where(along < 0, facing, jnp.where(along > 0, 7 + facing, middle))


def pack_kernel(sizes, margin_hbm, coef_hbm, patches, science, aligned, to_chip, to_next, to_far,
                margin, coef, patch_buf, science_buf, slot_of, patch_sem, science_sem, small_sem):
    strips, per_strip, owned = sizes
    tables = [
        pltpu.make_async_copy(a, b, small_sem.at[n]) for n, (a, b) in enumerate(((margin_hbm, margin), (coef_hbm, coef)))
    ]
    for copy in tables:
        copy.start()
    whole = pltpu.make_async_copy(science, science_buf, science_sem)
    whole.start()
    for copy in tables:
        copy.wait()
    owner = lax.axis_index("visit")
    sign = sign_of(owner)
    slots = owned_slots(margin, owner, strips, per_strip, owned)
    for k in range(SLOTS):
        slot_of[k] = slots[k]

        @pl.when(slots[k] >= 0)
        def _(k=k):
            local = lax.rem(margin[0, jnp.maximum(slots[k], 0)], owned)
            pltpu.make_async_copy(patches.at[local], patch_buf.at[k], patch_sem.at[k]).start()

    values = coef[...]
    bases = values.shape[1]
    high = values.astype(jnp.bfloat16).astype(jnp.float32)
    middle = (values - high).astype(jnp.bfloat16).astype(jnp.float32)
    low = values - high - middle
    parts = jnp.concatenate([high, middle, low, jnp.zeros_like(low)], axis=0).astype(jnp.bfloat16)
    to_chip[:COEF_ROWS, :bases] = parts
    to_next[:COEF_ROWS, :bases] = parts

    def slot_step(k, carry):
        tile = slot_of[k]

        @pl.when(tile >= 0)
        def _():
            down = margin[1, tile]
            right = margin[2, tile]
            local = lax.rem(margin[0, tile], owned)
            pltpu.make_async_copy(patches.at[local], patch_buf.at[k], patch_sem.at[k]).wait()
            moved = pltpu.roll(pltpu.roll(patch_buf[k], down, 0), right, 1)
            moved16 = moved.astype(jnp.bfloat16)
            aligned[k] = moved16
            relative = lax.div(k, CAP) - 1
            j = lax.rem(k, CAP)
            left = jnp.transpose(moved[:, :HALF])[:EDGE]
            right_edge = jnp.transpose(moved[:, TILE - HALF :])[HALF - EDGE :]
            edges = (moved16[:EDGE], moved16[TILE - EDGE :], left.astype(jnp.bfloat16), right_edge.astype(jnp.bfloat16))
            for kind in range(KINDS):
                position = piece_position(relative, jnp.int32(kind), sign)
                row = pl.multiple_of(COEF_ROWS + (position * CAP + j) * EDGE, EDGE)
                to_chip[pl.ds(row, EDGE), :] = edges[kind]

                @pl.when(position < NEAR)
                def _(kind=kind, row=row):
                    to_next[pl.ds(row, EDGE), :] = edges[kind]

                @pl.when(position == 0)
                def _(kind=kind):
                    to_far[pl.ds(pl.multiple_of(j * EDGE, EDGE), EDGE), :] = edges[kind]

        return carry

    lax.fori_loop(0, SLOTS, slot_step, 0)
    whole.wait()
    counts = [jnp.int32(0), jnp.int32(0)]
    for s in range(per_strip):
        tile = owner * per_strip + s
        offset = lax.div(margin[0, tile], owned) - owner

        @pl.when(offset != 0)
        def _(s=s, tile=tile, offset=offset, counts=tuple(counts)):
            up = lax.rem(TILE - margin[1, tile], TILE)
            back = lax.rem(TILE - margin[2, tile], TILE)
            moved = pltpu.roll(pltpu.roll(science_buf[:, s * TILE : (s + 1) * TILE], up, 0), back, 1)
            moved16 = moved.astype(jnp.bfloat16)

            @pl.when(offset == sign)
            def _():
                to_chip[pl.ds(pl.multiple_of(RECORD + counts[0] * TILE, EDGE), TILE), :] = moved16

            @pl.when(offset != sign)
            def _():
                to_next[pl.ds(pl.multiple_of(NEAR_ROWS + counts[1] * TILE, EDGE), TILE), :] = moved16

        counts[0] = counts[0] + jnp.where(offset == sign, 1, 0)
        counts[1] = counts[1] + jnp.where(offset == -sign, 1, 0)


def profile(u, sigma, order):
    taps = np.arange(-RADIUS, RADIUS + 1).astype(np.float32)
    total = float(np.sum(np.exp(-taps * taps / np.float32(2.0 * sigma * sigma)), dtype=np.float32))
    shape = jnp.where(jnp.abs(u) <= RADIUS, jnp.exp(-u * u / (2.0 * sigma * sigma)) / total, 0.0)
    for _ in range(order):
        shape = shape * (u / sigma)
    return shape


def plan_kernel(sizes, margin, ccd_first, from_far, from_chip, science, plan, across, table, corner, first):
    strips, per_strip, owned = sizes
    owner = lax.axis_index("visit")
    sign = sign_of(owner)
    slots = owned_slots(margin, owner, strips, per_strip, owned)
    ids = [jnp.where(t >= 0, margin[0, jnp.maximum(t, 0)], -1) for t in slots]
    counts = [sum(jnp.where(other == mine, 1, 0) for other in ids) for mine in ids]
    entry = jnp.int32(0)
    places = []
    for k in range(SLOTS):
        places.append(entry)
        entry = entry + jnp.where(slots[k] >= 0, 1, 0)
        plan[k] = slots[k]
        plan[SLOTS + k] = counts[k]
        plan[2 * SLOTS + k] = places[k]
    plan[3 * SLOTS] = entry

    def piece_row(strip, position, kind, allowed):
        inside = (strip >= 0) & (strip < strips) & (position >= 0) & (position < per_strip) & allowed
        base = jnp.clip(strip, 0, strips - 1) * per_strip
        where = jnp.clip(position, 0, per_strip - 1)
        its_owner = lax.div(margin[0, base + where], owned)
        rank = jnp.int32(0)
        for s in range(per_strip):
            same = lax.div(margin[0, base + s], owned) == its_owner
            rank = rank + jnp.where(same & (s < where), 1, 0)
        relative = jnp.clip(strip, 0, strips - 1) - its_owner
        member = (its_owner - owner) * sign + 3
        place = piece_position(relative, jnp.int32(kind), sign_of(its_owner)) * CAP + rank
        row = member * RECORD + COEF_ROWS + place * EDGE
        return jnp.where(inside, row, MEMBERS * RECORD)

    def fill(k, carry):
        tile = plan[k]

        @pl.when(tile >= 0)
        def _():
            q = lax.div(k, CAP)
            j = lax.rem(k, CAP)
            strip = owner - 1 + q
            position = tile - strip * per_strip
            local = lax.rem(margin[0, tile], owned)
            up = lax.rem(TILE - margin[1, tile], TILE)
            back = lax.rem(TILE - margin[2, tile], TILE)
            yes = owner >= 0
            keep_top = (strip > 0) & (ccd_first[strip] == 0)
            keep_bottom = (strip < strips - 1) & (ccd_first[jnp.minimum(strip + 1, strips - 1)] == 0)
            at = ENTRY * (plan[2 * SLOTS + k] + HEAD)
            member = (q - 1) * sign
            pieces = (
                (strip, position + 1, LEFT, yes),
                (strip, position - 1, RIGHT, yes),
                (strip - 1, position, BOTTOM, keep_top),
                (strip - 1, position - 1, BOTTOM, keep_top),
                (strip - 1, position + 1, BOTTOM, keep_top),
                (strip + 1, position, TOP, keep_bottom),
                (strip + 1, position - 1, TOP, keep_bottom),
                (strip + 1, position + 1, TOP, keep_bottom),
            )
            for n, args in enumerate(pieces):
                plan[at + n] = piece_row(*args)
            plan[at + 8] = k
            plan[at + 9] = up
            plan[at + 10] = back
            plan[at + 11] = local
            plan[at + 12] = plan[SLOTS + k]
            plan[at + 13] = member + 3
            plan[at + 14] = position
            share = share_of(plan[SLOTS + k])

            @pl.when(member == 0)
            def _():
                start = pl.multiple_of(position * TILE, TILE)
                moved = pltpu.roll(pltpu.roll(science[:, pl.ds(start, TILE)], up, 0), back, 1)
                first[local] = first[local] + moved * share

            @pl.when(member == 1)
            def _():
                start = pl.multiple_of(RECORD + j * TILE, EDGE)
                first[local] = first[local] + from_chip[pl.ds(start, TILE), :].astype(jnp.float32) * share

        return carry

    first[...] = jnp.zeros(first.shape, jnp.float32)
    lax.fori_loop(0, SLOTS, fill, 0)

    row = lax.broadcasted_iota(jnp.int32, (HALF, TILE), 0)
    u = (lax.broadcasted_iota(jnp.int32, (HALF, TILE), 1) - row - EDGE).astype(jnp.float32)
    w = lax.broadcasted_iota(jnp.int32, (TILE, HALF), 0) - lax.broadcasted_iota(jnp.int32, (TILE, HALF), 1)
    w = jnp.where(w > HALF, w - TILE, w).astype(jnp.float32)
    for g in range(SIGMAS):
        sigma = 0.75 * 2.0**g
        for k in range(ORDERS):
            n = g * ORDERS + k
            table[n] = profile(u[:, :HALF], sigma, k)
            corner[n] = profile(u[CORNER:, HALF:], sigma, k)
            across[:, n * HALF : (n + 1) * HALF] = profile(w, sigma, k).astype(jnp.bfloat16)


def share_of(count):
    share = jnp.float32(1.0)
    for n in range(2, SLOTS + 1):
        share = jnp.where(count == n, jnp.float32(1.0 / n), share)
    return share


def match_kernel(per_strip, plan, aligned, own_record, from_chip, from_next, from_two, from_across, from_far,
                 across, table, corner, first, out,
                 frames, window, spread, mixes, total):
    def put(member, start, rows, value):
        frames[member * RECORD + start : member * RECORD + start + rows, :] = value

    relayed = RECORD - NEAR_ROWS
    put(0, COEF_ROWS, PIECE_ROWS, from_far[...])
    put(1, NEAR_ROWS, relayed, from_two[...])
    put(2, 0, NEAR_ROWS, from_next[:NEAR_ROWS, :])
    put(3, 0, RECORD, own_record[:RECORD, :])
    put(4, 0, RECORD, from_chip[:RECORD, :])
    put(5, 0, NEAR_ROWS, from_across[:NEAR_ROWS, :])
    put(6, NEAR_ROWS, relayed, from_across[NEAR_ROWS:, :])
    put(MEMBERS, 0, EDGE, jnp.zeros((EDGE, TILE), jnp.bfloat16))
    columns = SIGMAS * ORDERS
    window_rows = TILE + 2 * EDGE
    mixes[:, :CORNER, HALF:] = jnp.zeros((columns, CORNER, REACH - HALF), jnp.bfloat16)
    out[...] = first[...]
    total[...] = jnp.zeros(total.shape, jnp.float32)
    strip_lanes = per_strip

    def base(k):
        return ENTRY * (k + HEAD)

    def build(k, half):
        at = base(k)

        def piece(n):
            return frames[pl.ds(pl.multiple_of(plan[at + n], EDGE), EDGE), :]

        sides = jnp.concatenate(
            [piece(0).astype(jnp.float32), jnp.zeros((HALF - 2 * EDGE, TILE), jnp.float32), piece(1).astype(jnp.float32)],
            axis=0,
        )
        sides = jnp.transpose(sides).astype(jnp.bfloat16)

        def place(start, rows, middle_a, middle_b, left_b, right_a):
            low = lax.broadcasted_iota(jnp.int32, (rows, HALF), 1) < HALF // 2
            window[half, start : start + rows, :HALF] = middle_a
            window[half, start : start + rows, HALF:] = jnp.where(low, middle_b, left_b)
            second = window_rows + start
            window[half, second : second + rows, :HALF] = middle_b
            window[half, second : second + rows, HALF:] = jnp.where(low, right_a, middle_a)

        center = aligned[plan[at + 8]]
        place(EDGE, TILE, center[:, :HALF], center[:, HALF:], sides, sides)
        for start, n in ((0, 2), (EDGE + TILE, 5)):
            middle, left, right = piece(n), piece(n + 1), piece(n + 2)
            place(start, EDGE, middle[:, :HALF], middle[:, HALF:], left[:, HALF:], right[:, :HALF])

    def finish(k, half, share):
        at = base(k)
        local = plan[at + 11]
        back = pltpu.roll(pltpu.roll(total[half], plan[at + 9], 0), plan[at + 10], 1)
        out[local] = out[local] - back * share

    count = plan[3 * SLOTS]

    for k in range(SLOTS):
        @pl.when((plan[k] >= 0) & (plan[base(plan[2 * SLOTS + k]) + 13] == 2))
        def _(k=k):
            at = base(plan[2 * SLOTS + k])
            local = plan[at + 11]
            start = NEAR_ROWS + (k % CAP) * TILE
            arrived = from_next[start : start + TILE, :].astype(jnp.float32)
            out[local] = out[local] + arrived * share_of(plan[at + 12])

    @pl.when(count > 0)
    def _():
        build(0, 0)

    def step(k, carry):
        half = lax.rem(k, 2)
        at = base(k)
        coef_row = pl.multiple_of(plan[at + 13] * RECORD, EDGE)
        block = frames[pl.ds(coef_row, COEF_ROWS), :HALF].astype(jnp.float32)
        rows = lax.broadcasted_iota(jnp.int32, block.shape, 0)
        mine = (lax.rem(rows, strip_lanes) == plan[at + 14]) & (rows < 3 * strip_lanes)
        weights = jnp.sum(jnp.where(mine, block, 0.0), axis=0, keepdims=True)
        build(jnp.minimum(k + 1, count - 1), 1 - half)
        for n in range(0, columns, 2):
            wide = min(2, columns - n)
            h = jnp.dot(window[half], across[:, n * HALF : (n + wide) * HALF], preferred_element_type=jnp.float32)
            h = h.astype(jnp.bfloat16)
            for m in range(wide):
                for c in range(2):
                    spread[n + m, :window_rows, c * HALF : (c + 1) * HALF] = h[
                        c * window_rows : (c + 1) * window_rows, m * HALF : (m + 1) * HALF
                    ]
            for c in range(n, n + wide):
                g = c // ORDERS
                mix = jnp.zeros((HALF, HALF), jnp.float32)
                edge = jnp.zeros((HALF - CORNER, REACH - HALF), jnp.float32)
                for v in range(ORDERS):
                    weight = weights[:, c * ORDERS + v : c * ORDERS + v + 1]
                    mix = mix + weight * table[g * ORDERS + v]
                    edge = edge + weight * corner[g * ORDERS + v, :, : REACH - HALF]
                mixes[c, :, :HALF] = mix.astype(jnp.bfloat16)
                mixes[c, CORNER:, HALF:] = edge.astype(jnp.bfloat16)
        finish(jnp.maximum(k - 1, 0), 1 - half, jnp.where(k > 0, share_of(plan[base(jnp.maximum(k - 1, 0)) + 12]), 0.0))
        for r in range(2):
            acc = jnp.zeros((HALF, TILE), jnp.float32)
            for n in range(columns):
                acc = acc + jnp.dot(
                    mixes[n], spread[n, r * HALF : r * HALF + REACH, :], preferred_element_type=jnp.float32
                )
            total[half, r * HALF : (r + 1) * HALF, :] = acc
        return carry

    lax.fori_loop(0, count, step, 0)

    @pl.when(count > 0)
    def _():
        finish(count - 1, lax.rem(count - 1, 2), share_of(plan[base(count - 1) + 12]))


def body(science, patches, margin, kernel_coef, ccd_first):
    strips = lax.axis_size("visit")
    owned = patches.shape[0]
    per_strip = science.shape[1] // TILE
    sizes = (strips, per_strip, owned)
    margin = margin.T
    smem = pl.BlockSpec(memory_space=pltpu.SMEM)
    vmem = pl.BlockSpec(memory_space=pltpu.VMEM)
    hbm = pl.BlockSpec(memory_space=pl.ANY)
    stays = pl.BlockSpec(memory_space=pltpu.HBM)
    bf16 = jnp.bfloat16
    f32 = jnp.float32
    aligned, to_chip, to_next, to_far = pl.pallas_call(
        functools.partial(pack_kernel, sizes),
        out_shape=(
            jax.ShapeDtypeStruct((SLOTS, TILE, TILE), bf16),
            jax.ShapeDtypeStruct((RECORD + CAP * TILE, TILE), bf16),
            jax.ShapeDtypeStruct((NEAR_ROWS + CAP * TILE, TILE), bf16),
            jax.ShapeDtypeStruct((PIECE_ROWS, TILE), bf16),
        ),
        in_specs=[stays] * 4,
        out_specs=(vmem, vmem, vmem, vmem),
        scratch_shapes=[
            pltpu.SMEM(margin.shape, jnp.int32),
            pltpu.VMEM(kernel_coef.shape[::-1], f32),
            pltpu.VMEM((SLOTS, TILE, TILE), f32),
            pltpu.VMEM((TILE, per_strip * TILE), f32),
            pltpu.SMEM((SLOTS,), jnp.int32),
            pltpu.SemaphoreType.DMA((SLOTS,)),
            pltpu.SemaphoreType.DMA,
            pltpu.SemaphoreType.DMA((2,)),
        ],
        compiler_params=pltpu.CompilerParams(vmem_limit_bytes=52 * 2**20),
        name="pack",
    )(margin, kernel_coef.T, patches, science)

    on_chip = [(i, i ^ 1) for i in range(strips)]
    next_chip = [p for i in range(1, strips - 1, 2) for p in ((i, i + 1), (i + 1, i))]
    far = [p for i in range(1, strips - 3, 2) for p in ((i, i + 3), (i + 3, i))]
    two = [p for i in range(0, strips - 2, 2) for p in ((i, i + 2), (i + 3, i + 1))]
    from_next = lax.ppermute(to_next, "visit", next_chip)
    from_two = lax.ppermute(to_chip[NEAR_ROWS:RECORD], "visit", two)
    from_far = lax.ppermute(to_far, "visit", far)
    from_chip = lax.ppermute(to_chip, "visit", on_chip)
    columns = SIGMAS * ORDERS
    planned = pl.pallas_call(
        functools.partial(plan_kernel, sizes),
        out_shape=(
            jax.ShapeDtypeStruct((ENTRY * (HEAD + SLOTS),), jnp.int32),
            jax.ShapeDtypeStruct((TILE, columns * HALF), bf16),
            jax.ShapeDtypeStruct((columns, HALF, HALF), f32),
            jax.ShapeDtypeStruct((columns, HALF - CORNER, HALF), f32),
            jax.ShapeDtypeStruct(patches.shape, f32),
        ),
        in_specs=[smem, smem] + [vmem] * 3,
        out_specs=(smem, vmem, vmem, vmem, vmem),
        compiler_params=pltpu.CompilerParams(vmem_limit_bytes=12 * 2**20),
        name="plan",
    )(margin, ccd_first, from_far, from_chip, science)
    from_next, from_two, from_far, planned = lax.optimization_barrier((from_next, from_two, from_far, planned))
    plan, *tables = planned
    relay = jnp.concatenate([from_next[:NEAR_ROWS], from_two], axis=0)
    from_across = lax.ppermute(relay, "visit", on_chip)

    return pl.pallas_call(
        functools.partial(match_kernel, per_strip),
        out_shape=jax.ShapeDtypeStruct(patches.shape, f32),
        in_specs=[smem] + [vmem] * 11,
        out_specs=vmem,
        scratch_shapes=[
            pltpu.VMEM((MEMBERS * RECORD + EDGE, TILE), bf16),
            pltpu.VMEM((2, 2 * (TILE + 2 * EDGE), TILE), bf16),
            pltpu.VMEM((columns, TILE + 2 * EDGE, TILE), bf16),
            pltpu.VMEM((columns, HALF, REACH), bf16),
            pltpu.VMEM((2, TILE, TILE), f32),
        ],
        compiler_params=pltpu.CompilerParams(vmem_limit_bytes=24 * 2**20),
        name="match",
    )(plan, aligned, to_chip, from_chip, from_next, from_two, from_across, from_far, *tables)


def solution(mesh):
    in_specs = (
        P(("grp", "visit"), None),
        P(("grp", "visit"), None, None),
        P("grp", None),
        P(None, ("grp", "visit")),
        P("grp"),
    )
    out_specs = P(("grp", "visit"), None, None)
    return jax.shard_map(body, mesh=mesh, in_specs=in_specs, out_specs=out_specs, check_vma=False)
```

```python
import functools

import jax
import jax.numpy as jnp
import numpy as np
from jax import lax
from jax.experimental import pallas as pl
from jax.experimental.pallas import tpu as pltpu
from jax.sharding import PartitionSpec as P

TILE = 256
HALF = 128
RADIUS = 10
SIGMAS = 3
ORDERS = 3
EDGE = 16
CAP = 2
STRIPS = 3
SLOTS = STRIPS * CAP
KINDS = 4
TOP, BOTTOM, LEFT, RIGHT = range(KINDS)
PIECES = SLOTS * KINDS
COEF_ROWS = 16
NEAR = 8
PIECE_ROWS = CAP * EDGE
NEAR_ROWS = COEF_ROWS + NEAR * CAP * RADIUS
TWO_ROWS = (STRIPS * KINDS - NEAR) * CAP * RADIUS
RECORD = COEF_ROWS + PIECES * EDGE
MEMBERS = 7
ENTRY = 16
HEAD = 2
REACH = HALF + 2 * EDGE


def owned_slots(margin, owner, strips, per_strip, owned):
    slots = []
    for q in range(STRIPS):
        strip = owner - 1 + q
        inside = (strip >= 0) & (strip < strips)
        base = jnp.clip(strip, 0, strips - 1) * per_strip
        count = jnp.int32(0)
        found = [jnp.int32(-1) for _ in range(CAP)]
        for s in range(per_strip):
            mine = inside & (owner_of(margin[0, base + s], owned) == owner)
            for j in range(CAP):
                found[j] = jnp.where(mine & (count == j), base + s, found[j])
            count = count + jnp.where(mine, 1, 0)
        slots.extend(found)
    return slots


def sign_of(owner):
    return 1 - 2 * lax.rem(owner, 2)


def piece_position(relative, kind, sign):
    along = relative * sign
    facing = jnp.where(sign > 0, kind, jnp.where(kind == TOP, BOTTOM, jnp.where(kind == BOTTOM, TOP, kind)))
    middle = jnp.where(facing == TOP, 4, jnp.where(facing == BOTTOM, 11, facing + 3))
    return jnp.where(along < 0, facing, jnp.where(along > 0, 7 + facing, middle))


def owner_of(patch, owned):
    if owned & (owned - 1) == 0:
        return lax.shift_right_logical(patch, jnp.int32(owned.bit_length() - 1))
    return lax.div(patch, owned)


def packed(record, first, count):
    rows = record[COEF_ROWS + first * EDGE : COEF_ROWS + (first + count) * EDGE, :].astype(jnp.float32)
    return jnp.concatenate([rows[n * EDGE : n * EDGE + RADIUS] for n in range(count)], axis=0).astype(jnp.bfloat16)


def spaced(rows):
    rows = rows.astype(jnp.float32)
    empty = jnp.zeros((EDGE - RADIUS, TILE), jnp.float32)
    pieces = []
    for n in range(rows.shape[0] // RADIUS):
        pieces += [rows[n * RADIUS : (n + 1) * RADIUS], empty]
    return jnp.concatenate(pieces, axis=0).astype(jnp.bfloat16)


def pack_kernel(sizes, margin_hbm, coef_hbm, patches, science, aligned, to_chip, to_next, to_two, to_far,
                margin, coef, patch_buf, science_buf, slot_of, patch_sem, science_sem, small_sem):
    strips, per_strip, owned = sizes
    tables = [
        pltpu.make_async_copy(a, b, small_sem.at[n]) for n, (a, b) in enumerate(((margin_hbm, margin), (coef_hbm, coef)))
    ]
    for copy in tables:
        copy.start()
    whole = pltpu.make_async_copy(science, science_buf, science_sem)
    whole.start()
    to_chip[COEF_ROWS:RECORD, :] = jnp.zeros((RECORD - COEF_ROWS, TILE), jnp.bfloat16)
    to_far[...] = jnp.zeros(to_far.shape, jnp.bfloat16)
    for copy in tables:
        copy.wait()
    owner = lax.axis_index("visit")
    sign = sign_of(owner)
    slots = owned_slots(margin, owner, strips, per_strip, owned)
    for k in range(SLOTS):
        slot_of[k] = slots[k]

        @pl.when(slots[k] >= 0)
        def _(k=k):
            local = lax.rem(margin[0, jnp.maximum(slots[k], 0)], owned)
            pltpu.make_async_copy(patches.at[local], patch_buf.at[k], patch_sem.at[k]).start()

    values = coef[...]
    bases = values.shape[1]
    high = values.astype(jnp.bfloat16).astype(jnp.float32)
    middle = (values - high).astype(jnp.bfloat16).astype(jnp.float32)
    low = values - high - middle
    parts = jnp.concatenate([high, middle, low, jnp.zeros_like(low)], axis=0).astype(jnp.bfloat16)
    to_chip[:COEF_ROWS, :bases] = parts
    to_next[:COEF_ROWS, :bases] = parts

    whole.wait()
    counts = [jnp.int32(0), jnp.int32(0)]
    for s in range(per_strip):
        tile = owner * per_strip + s
        offset = lax.div(margin[0, tile], owned) - owner

        @pl.when(offset != 0)
        def _(s=s, tile=tile, offset=offset, counts=tuple(counts)):
            up = lax.rem(TILE - margin[1, tile], TILE)
            back = lax.rem(TILE - margin[2, tile], TILE)
            moved = pltpu.roll(pltpu.roll(science_buf[:, s * TILE : (s + 1) * TILE], up, 0), back, 1)
            moved16 = moved.astype(jnp.bfloat16)

            @pl.when(offset == sign)
            def _():
                to_chip[pl.ds(pl.multiple_of(RECORD + counts[0] * TILE, EDGE), TILE), :] = moved16

            @pl.when(offset != sign)
            def _():
                to_next[pl.ds(pl.multiple_of(NEAR_ROWS + counts[1] * TILE, EDGE), TILE), :] = moved16

        counts[0] = counts[0] + jnp.where(offset == sign, 1, 0)
        counts[1] = counts[1] + jnp.where(offset == -sign, 1, 0)

    def slot_step(k, carry):
        tile = slot_of[k]

        @pl.when(tile >= 0)
        def _():
            down = margin[1, tile]
            right = margin[2, tile]
            local = lax.rem(margin[0, tile], owned)
            pltpu.make_async_copy(patches.at[local], patch_buf.at[k], patch_sem.at[k]).wait()
            moved = pltpu.roll(pltpu.roll(patch_buf[k], down, 0), right, 1)
            moved16 = moved.astype(jnp.bfloat16)
            aligned[k] = moved16
            relative = lax.div(k, CAP) - 1
            j = lax.rem(k, CAP)
            left = jnp.transpose(moved[:, :HALF])[:EDGE]
            right_edge = jnp.transpose(moved[:, TILE - HALF :])[HALF - RADIUS :]
            empty = jnp.zeros((EDGE - RADIUS, TILE), jnp.float32)
            bottom = jnp.concatenate([moved[TILE - RADIUS :], empty], axis=0)
            right_edge = jnp.concatenate([right_edge, empty], axis=0)
            edges = [moved16[:EDGE]] + [edge.astype(jnp.bfloat16) for edge in (bottom, left, right_edge)]
            for kind in range(KINDS):
                position = piece_position(relative, jnp.int32(kind), sign)
                row = pl.multiple_of(COEF_ROWS + (position * CAP + j) * EDGE, EDGE)
                to_chip[pl.ds(row, EDGE), :] = edges[kind]

                @pl.when(position == 0)
                def _(kind=kind):
                    to_far[pl.ds(pl.multiple_of(j * EDGE, EDGE), EDGE), :] = edges[kind]

        return carry

    lax.fori_loop(0, SLOTS, slot_step, 0)
    to_next[COEF_ROWS:NEAR_ROWS, :] = packed(to_chip, 0, NEAR * CAP)
    to_two[...] = packed(to_chip, NEAR * CAP, PIECES - NEAR * CAP)


def profile(u, sigma, order):
    taps = np.arange(-RADIUS, RADIUS + 1).astype(np.float32)
    total = float(np.sum(np.exp(-taps * taps / np.float32(2.0 * sigma * sigma)), dtype=np.float32))
    shape = jnp.where(jnp.abs(u) <= RADIUS, jnp.exp(-u * u / (2.0 * sigma * sigma)) / total, 0.0)
    for _ in range(order):
        shape = shape * (u / sigma)
    return shape


def fill_tables(across, mixing):
    w = lax.broadcasted_iota(jnp.int32, (TILE, HALF), 0) - lax.broadcasted_iota(jnp.int32, (TILE, HALF), 1)
    w = jnp.where(w > HALF, w - TILE, w).astype(jnp.float32)
    for g in range(SIGMAS):
        for h in range(ORDERS):
            n = g * ORDERS + h
            across[:, n * HALF : (n + 1) * HALF] = profile(w, 0.75 * 2.0**g, h).astype(jnp.bfloat16)
    lanes = SIGMAS * ORDERS * REACH
    for at in range(0, lanes, HALF):
        wide = min(HALF, lanes - at)
        lane = lax.broadcasted_iota(jnp.int32, (HALF, wide), 1) + at
        row = lax.broadcasted_iota(jnp.int32, (HALF, wide), 0)
        one = at // REACH
        two = (at + wide - 1) // REACH
        start = jnp.where(lane < two * REACH, one * REACH, two * REACH)
        u = (lane - start - row - EDGE).astype(jnp.float32)
        low, high = one // ORDERS, two // ORDERS
        sigma = 0.75 * 2.0**low
        if high != low:
            sigma = jnp.where(lane < two * REACH, sigma, 0.75 * 2.0**high)
        totals = []
        for g in (low, high):
            taps = np.arange(-RADIUS, RADIUS + 1).astype(np.float32)
            totals.append(float(np.sum(np.exp(-taps * taps / np.float32(2.0 * (0.75 * 2.0**g) ** 2)), dtype=np.float32)))
        total = totals[0] if high == low else jnp.where(lane < two * REACH, totals[0], totals[1])
        shape = jnp.where(jnp.abs(u) <= RADIUS, jnp.exp(-u * u / (2.0 * sigma * sigma)) / total, 0.0)
        for v in range(ORDERS):
            mixing[v, :, at : at + wide] = shape
            shape = shape * (u / sigma)


def plan_kernel(sizes, margin, ccd_first, from_chip, science, plan, across, mixing, first, rows):
    strips, per_strip, owned = sizes
    owner = lax.axis_index("visit")
    sign = sign_of(owner)
    slots = owned_slots(margin, owner, strips, per_strip, owned)
    ids = [jnp.where(t >= 0, margin[0, jnp.maximum(t, 0)], -1) for t in slots]
    counts = [sum(jnp.where(other == mine, 1, 0) for other in ids) for mine in ids]
    entry = jnp.int32(0)
    places = []
    for k in range(SLOTS):
        places.append(entry)
        entry = entry + jnp.where(slots[k] >= 0, 1, 0)
        plan[k] = slots[k]
        plan[SLOTS + k] = counts[k]
        plan[2 * SLOTS + k] = places[k]
    plan[3 * SLOTS] = entry

    for i in range(2 * STRIPS - 1):
        strip = jnp.clip(owner - STRIPS + 1 + i, 0, strips - 1)
        owners = [owner_of(margin[0, strip * per_strip + n], owned) for n in range(per_strip)]
        for n, its_owner in enumerate(owners):
            rank = sum((jnp.where(other == its_owner, 1, 0) for other in owners[:n]), jnp.int32(0))
            start = ((its_owner - owner) * sign + 3) * RECORD + COEF_ROWS + rank * EDGE
            its_sign = sign_of(its_owner)
            for kind in range(KINDS):
                place = piece_position(strip - its_owner, jnp.int32(kind), its_sign)
                rows[(i * per_strip + n) * KINDS + kind] = start + place * PIECE_ROWS

    def piece_row(strip, position, kind, allowed):
        inside = (position >= 0) & (position < per_strip) & allowed
        at = ((strip - owner + STRIPS - 1) * per_strip + position) * KINDS + kind
        return jnp.where(inside, rows[jnp.where(inside, at, 0)], MEMBERS * RECORD)

    def fill(k, carry):
        tile = plan[k]

        @pl.when(tile >= 0)
        def _():
            q = lax.div(k, CAP)
            j = lax.rem(k, CAP)
            strip = owner - 1 + q
            position = tile - strip * per_strip
            local = lax.rem(margin[0, tile], owned)
            up = lax.rem(TILE - margin[1, tile], TILE)
            back = lax.rem(TILE - margin[2, tile], TILE)
            yes = owner >= 0
            keep_top = (strip > 0) & (ccd_first[strip] == 0)
            keep_bottom = (strip < strips - 1) & (ccd_first[jnp.minimum(strip + 1, strips - 1)] == 0)
            at = ENTRY * (plan[2 * SLOTS + k] + HEAD)
            member = (q - 1) * sign
            pieces = (
                (strip, position + 1, LEFT, yes),
                (strip, position - 1, RIGHT, yes),
                (strip - 1, position, BOTTOM, keep_top),
                (strip - 1, position - 1, BOTTOM, keep_top),
                (strip - 1, position + 1, BOTTOM, keep_top),
                (strip + 1, position, TOP, keep_bottom),
                (strip + 1, position - 1, TOP, keep_bottom),
                (strip + 1, position + 1, TOP, keep_bottom),
            )
            for n, args in enumerate(pieces):
                plan[at + n] = piece_row(*args)
            plan[at + 8] = k
            plan[at + 9] = up
            plan[at + 10] = back
            plan[at + 11] = local
            plan[at + 12] = plan[SLOTS + k]
            plan[at + 13] = member + 3
            plan[at + 14] = position
            share = share_of(plan[SLOTS + k])

            @pl.when(member == 0)
            def _():
                start = pl.multiple_of(position * TILE, TILE)
                moved = pltpu.roll(pltpu.roll(science[:, pl.ds(start, TILE)], up, 0), back, 1)
                first[local] = first[local] + moved * share

            @pl.when(member == 1)
            def _():
                start = pl.multiple_of(RECORD + j * TILE, EDGE)
                first[local] = first[local] + from_chip[pl.ds(start, TILE), :].astype(jnp.float32) * share

        return carry

    first[...] = jnp.zeros(first.shape, jnp.float32)
    lax.fori_loop(0, SLOTS, fill, 0)
    fill_tables(across, mixing)


def share_of(count):
    share = jnp.float32(1.0)
    for n in range(2, SLOTS + 1):
        share = jnp.where(count == n, jnp.float32(1.0 / n), share)
    return share


def match_kernel(per_strip, plan, aligned, own_record, from_chip, from_next, from_two, from_across, from_far,
                 across, mixing, first, out,
                 frames, window, spread, mixes, total):
    def put(member, start, rows, value):
        frames[member * RECORD + start : member * RECORD + start + rows, :] = value

    near = NEAR * PIECE_ROWS
    put(0, COEF_ROWS, PIECE_ROWS, from_far[...])
    put(1, COEF_ROWS + near, RECORD - COEF_ROWS - near, spaced(from_two[...]))
    put(2, 0, COEF_ROWS, from_next[:COEF_ROWS, :])
    put(2, COEF_ROWS, near, spaced(from_next[COEF_ROWS:NEAR_ROWS, :]))
    put(3, 0, RECORD, own_record[:RECORD, :])
    put(4, 0, RECORD, from_chip[:RECORD, :])
    put(5, COEF_ROWS, near, spaced(from_across[COEF_ROWS:NEAR_ROWS, :]))
    put(6, COEF_ROWS + near, RECORD - COEF_ROWS - near, spaced(from_across[NEAR_ROWS:, :]))
    put(MEMBERS, 0, EDGE, jnp.zeros((EDGE, TILE), jnp.bfloat16))
    columns = SIGMAS * ORDERS
    window_rows = TILE + 2 * EDGE
    out[...] = first[...]
    total[...] = jnp.zeros(total.shape, jnp.float32)
    strip_lanes = per_strip

    def base(k):
        return ENTRY * (k + HEAD)

    def lowered(edge):
        empty = jnp.zeros((EDGE - RADIUS, TILE), jnp.float32)
        return jnp.concatenate([empty, edge.astype(jnp.float32)[:RADIUS]], axis=0).astype(jnp.bfloat16)

    def build(k, half):
        at = base(k)

        def piece(n):
            return frames[pl.ds(pl.multiple_of(plan[at + n], EDGE), EDGE), :]

        sides = jnp.concatenate(
            [
                piece(0).astype(jnp.float32),
                jnp.zeros((HALF - EDGE - RADIUS, TILE), jnp.float32),
                piece(1).astype(jnp.float32)[:RADIUS],
            ],
            axis=0,
        )
        sides = jnp.transpose(sides).astype(jnp.bfloat16)

        def place(start, rows, middle_a, middle_b, left_b, right_a):
            low = lax.broadcasted_iota(jnp.int32, (rows, HALF), 1) < HALF // 2
            window[half, start : start + rows, :HALF] = middle_a
            window[half, start : start + rows, HALF:] = jnp.where(low, middle_b, left_b)
            second = window_rows + start
            window[half, second : second + rows, :HALF] = middle_b
            window[half, second : second + rows, HALF:] = jnp.where(low, right_a, middle_a)

        center = aligned[plan[at + 8]]
        place(EDGE, TILE, center[:, :HALF], center[:, HALF:], sides, sides)
        for start, n in ((0, 2), (EDGE + TILE, 5)):
            middle, left, right = piece(n), piece(n + 1), piece(n + 2)
            if start == 0:
                middle, left, right = lowered(middle), lowered(left), lowered(right)
            place(start, EDGE, middle[:, :HALF], middle[:, HALF:], left[:, HALF:], right[:, :HALF])

    def finish(k, half, share):
        at = base(k)
        local = plan[at + 11]
        back = pltpu.roll(pltpu.roll(total[half], plan[at + 9], 0), plan[at + 10], 1)
        out[local] = out[local] - back * share

    count = plan[3 * SLOTS]

    for k in range(SLOTS):
        @pl.when((plan[k] >= 0) & (plan[base(plan[2 * SLOTS + k]) + 13] == 2))
        def _(k=k):
            at = base(plan[2 * SLOTS + k])
            local = plan[at + 11]
            start = NEAR_ROWS + (k % CAP) * TILE
            arrived = from_next[start : start + TILE, :].astype(jnp.float32)
            out[local] = out[local] + arrived * share_of(plan[at + 12])

    @pl.when(count > 0)
    def _():
        build(0, 0)

    def step(k, carry):
        half = lax.rem(k, 2)
        at = base(k)
        coef_row = pl.multiple_of(plan[at + 13] * RECORD, EDGE)
        block = frames[pl.ds(coef_row, COEF_ROWS), :HALF].astype(jnp.float32)
        rows = lax.broadcasted_iota(jnp.int32, block.shape, 0)
        mine = (lax.rem(rows, strip_lanes) == plan[at + 14]) & (rows < 3 * strip_lanes)
        weights = jnp.sum(jnp.where(mine, block, 0.0), axis=0, keepdims=True)
        lanes = columns * REACH
        for n in range(0, columns, 2):
            if n == 2:
                finish(jnp.maximum(k - 1, 0), 1 - half, jnp.where(k > 0, share_of(plan[base(jnp.maximum(k - 1, 0)) + 12]), 0.0))
            if n == 4:
                build(jnp.minimum(k + 1, count - 1), 1 - half)
            wide = min(2, columns - n)
            h = jnp.dot(window[half], across[:, n * HALF : (n + wide) * HALF], preferred_element_type=jnp.float32)
            h = h.astype(jnp.bfloat16)
            for m in range(wide):
                to = (n + m) * REACH
                for c in range(2):
                    for r in range(2):
                        start = c * window_rows + r * HALF
                        spread[r, to : to + REACH, c * HALF : (c + 1) * HALF] = h[
                            start : start + REACH, m * HALF : (m + 1) * HALF
                        ]
            for at in range(n * REACH // HALF * HALF, min(lanes, (n + 2) * REACH // HALF * HALF), HALF):
                wide_at = min(HALF, lanes - at)
                lane = lax.broadcasted_iota(jnp.int32, (1, wide_at), 1) + at
                mix = jnp.zeros((HALF, wide_at), jnp.float32)
                one = at // REACH
                two = min((at + wide_at - 1) // REACH, columns - 1)
                for v in range(ORDERS):
                    weight = weights[:, one * ORDERS + v : one * ORDERS + v + 1]
                    if two != one:
                        other = weights[:, two * ORDERS + v : two * ORDERS + v + 1]
                        weight = jnp.where(lane < two * REACH, weight, other)
                    mix = mix + weight * mixing[v, :, at : at + wide_at]
                mixes[:, at : at + wide_at] = mix.astype(jnp.bfloat16)
        for r in range(2):
            total[half, r * HALF : (r + 1) * HALF, :] = jnp.dot(
                mixes[...], spread[r], preferred_element_type=jnp.float32
            )
        return carry

    lax.fori_loop(0, count, step, 0)

    @pl.when(count > 0)
    def _():
        finish(count - 1, lax.rem(count - 1, 2), share_of(plan[base(count - 1) + 12]))


def step(science, patches, margin, kernel_coef, ccd_first):
    strips = lax.axis_size("visit")
    owned = patches.shape[0]
    per_strip = science.shape[1] // TILE
    sizes = (strips, per_strip, owned)
    margin = margin.T
    smem = pl.BlockSpec(memory_space=pltpu.SMEM)
    vmem = pl.BlockSpec(memory_space=pltpu.VMEM)
    hbm = pl.BlockSpec(memory_space=pl.ANY)
    stays = pl.BlockSpec(memory_space=pltpu.HBM)
    bf16 = jnp.bfloat16
    f32 = jnp.float32
    aligned, to_chip, to_next, to_two, to_far = pl.pallas_call(
        functools.partial(pack_kernel, sizes),
        out_shape=(
            jax.ShapeDtypeStruct((SLOTS, TILE, TILE), bf16),
            jax.ShapeDtypeStruct((RECORD + CAP * TILE, TILE), bf16),
            jax.ShapeDtypeStruct((NEAR_ROWS + CAP * TILE, TILE), bf16),
            jax.ShapeDtypeStruct((TWO_ROWS, TILE), bf16),
            jax.ShapeDtypeStruct((PIECE_ROWS, TILE), bf16),
        ),
        in_specs=[stays] * 4,
        out_specs=(vmem, vmem, vmem, vmem, vmem),
        scratch_shapes=[
            pltpu.SMEM(margin.shape, jnp.int32),
            pltpu.VMEM(kernel_coef.shape[::-1], f32),
            pltpu.VMEM((SLOTS, TILE, TILE), f32),
            pltpu.VMEM((TILE, per_strip * TILE), f32),
            pltpu.SMEM((SLOTS,), jnp.int32),
            pltpu.SemaphoreType.DMA((SLOTS,)),
            pltpu.SemaphoreType.DMA,
            pltpu.SemaphoreType.DMA((2,)),
        ],
        compiler_params=pltpu.CompilerParams(vmem_limit_bytes=52 * 2**20),
        name="pack",
    )(margin, kernel_coef.T, patches, science)

    on_chip = [(i, i ^ 1) for i in range(strips)]
    next_chip = [p for i in range(1, strips - 1, 2) for p in ((i, i + 1), (i + 1, i))]
    far = [p for i in range(1, strips - 3, 2) for p in ((i, i + 3), (i + 3, i))]
    two = [p for i in range(0, strips - 2, 2) for p in ((i, i + 2), (i + 3, i + 1))]
    from_next = lax.ppermute(to_next, "visit", next_chip)
    from_two = lax.ppermute(to_two, "visit", two)
    from_far = lax.ppermute(to_far, "visit", far)
    from_chip = lax.ppermute(to_chip, "visit", on_chip)

    columns = SIGMAS * ORDERS
    planned = pl.pallas_call(
        functools.partial(plan_kernel, sizes),
        out_shape=(
            jax.ShapeDtypeStruct((ENTRY * (HEAD + SLOTS),), jnp.int32),
            jax.ShapeDtypeStruct((TILE, columns * HALF), bf16),
            jax.ShapeDtypeStruct((ORDERS, HALF, columns * REACH), f32),
            jax.ShapeDtypeStruct(patches.shape, f32),
        ),
        in_specs=[smem, smem] + [vmem] * 2,
        out_specs=(smem, vmem, vmem, vmem),
        scratch_shapes=[pltpu.SMEM(((2 * STRIPS - 1) * per_strip * KINDS,), jnp.int32)],
        compiler_params=pltpu.CompilerParams(vmem_limit_bytes=12 * 2**20),
        name="plan",
    )(margin, ccd_first, from_chip, science)
    from_next, from_two, from_far, planned = lax.optimization_barrier((from_next, from_two, from_far, planned))
    plan, *tables = planned
    relay = jnp.concatenate([from_next[:NEAR_ROWS], from_two], axis=0)
    from_across = lax.ppermute(relay, "visit", on_chip)

    return pl.pallas_call(
        functools.partial(match_kernel, per_strip),
        out_shape=jax.ShapeDtypeStruct(patches.shape, f32),
        in_specs=[smem] + [vmem] * 10,
        out_specs=vmem,
        scratch_shapes=[
            pltpu.VMEM((MEMBERS * RECORD + EDGE, TILE), bf16),
            pltpu.VMEM((2, 2 * (TILE + 2 * EDGE), TILE), bf16),
            pltpu.VMEM((2, columns * REACH, TILE), bf16),
            pltpu.VMEM((HALF, columns * REACH), bf16),
            pltpu.VMEM((2, TILE, TILE), f32),
        ],
        compiler_params=pltpu.CompilerParams(vmem_limit_bytes=24 * 2**20),
        name="match",
    )(plan, aligned, to_chip, from_chip, from_next, from_two, from_across, from_far, *tables)


def solution(mesh):
    in_specs = (
        P(("grp", "visit"), None),
        P(("grp", "visit"), None, None),
        P("grp", None),
        P(None, ("grp", "visit")),
        P("grp"),
    )
    out_specs = P(("grp", "visit"), None, None)
    return jax.shard_map(step, mesh=mesh, in_specs=in_specs, out_specs=out_specs, check_vma=False)
```

```python
import functools

import jax
import jax.numpy as jnp
import numpy as np
from jax import lax
from jax.experimental import pallas as pl
from jax.experimental.pallas import tpu as pltpu
from jax.sharding import PartitionSpec as P

TILE = 256
HALF = 128
RADIUS = 10
SIGMAS = 3
ORDERS = 3
EDGE = 16
CAP = 2
STRIPS = 3
SLOTS = STRIPS * CAP
KINDS = 4
TOP, BOTTOM, LEFT, RIGHT = range(KINDS)
PIECES = SLOTS * KINDS
COEF_ROWS = 16
NEAR = 8
PIECE_ROWS = CAP * EDGE
NEAR_ROWS = COEF_ROWS + NEAR * CAP * RADIUS
TWO_ROWS = (STRIPS * KINDS - NEAR) * CAP * RADIUS
RECORD = COEF_ROWS + PIECES * EDGE
MEMBERS = 7
ENTRY = 16
HEAD = 2
REACH = HALF + 2 * EDGE


def owned_slots(margin, owner, strips, per_strip, owned):
    slots = []
    for q in range(STRIPS):
        strip = owner - 1 + q
        inside = (strip >= 0) & (strip < strips)
        base = jnp.clip(strip, 0, strips - 1) * per_strip
        count = jnp.int32(0)
        found = [jnp.int32(-1) for _ in range(CAP)]
        for s in range(per_strip):
            mine = inside & (owner_of(margin[0, base + s], owned) == owner)
            for j in range(CAP):
                found[j] = jnp.where(mine & (count == j), base + s, found[j])
            count = count + jnp.where(mine, 1, 0)
        slots.extend(found)
    return slots


def sign_of(owner):
    return 1 - 2 * lax.rem(owner, 2)


def piece_position(relative, kind, sign):
    along = relative * sign
    facing = jnp.where(sign > 0, kind, jnp.where(kind == TOP, BOTTOM, jnp.where(kind == BOTTOM, TOP, kind)))
    middle = jnp.where(facing == TOP, 4, jnp.where(facing == BOTTOM, 11, facing + 3))
    return jnp.where(along < 0, facing, jnp.where(along > 0, 7 + facing, middle))


def owner_of(patch, owned):
    if owned & (owned - 1) == 0:
        return lax.shift_right_logical(patch, jnp.int32(owned.bit_length() - 1))
    return lax.div(patch, owned)


def packed(record, first, count):
    rows = record[COEF_ROWS + first * EDGE : COEF_ROWS + (first + count) * EDGE, :].astype(jnp.float32)
    return jnp.concatenate([rows[n * EDGE : n * EDGE + RADIUS] for n in range(count)], axis=0).astype(jnp.bfloat16)


def spaced(rows):
    rows = rows.astype(jnp.float32)
    empty = jnp.zeros((EDGE - RADIUS, TILE), jnp.float32)
    pieces = []
    for n in range(rows.shape[0] // RADIUS):
        pieces += [rows[n * RADIUS : (n + 1) * RADIUS], empty]
    return jnp.concatenate(pieces, axis=0).astype(jnp.bfloat16)


def pack_kernel(sizes, margin_hbm, coef_hbm, patches, science, aligned, to_chip, to_next, to_two, to_far,
                margin, coef, patch_buf, science_buf, slot_of, patch_sem, science_sem, small_sem):
    strips, per_strip, owned = sizes
    tables = [
        pltpu.make_async_copy(a, b, small_sem.at[n]) for n, (a, b) in enumerate(((margin_hbm, margin), (coef_hbm, coef)))
    ]
    for copy in tables:
        copy.start()
    whole = pltpu.make_async_copy(science, science_buf, science_sem)
    whole.start()
    to_chip[COEF_ROWS:RECORD, :] = jnp.zeros((RECORD - COEF_ROWS, TILE), jnp.bfloat16)
    to_far[...] = jnp.zeros(to_far.shape, jnp.bfloat16)
    for copy in tables:
        copy.wait()
    owner = lax.axis_index("visit")
    sign = sign_of(owner)
    slots = owned_slots(margin, owner, strips, per_strip, owned)
    for k in range(SLOTS):
        slot_of[k] = slots[k]

        @pl.when(slots[k] >= 0)
        def _(k=k):
            local = lax.rem(margin[0, jnp.maximum(slots[k], 0)], owned)
            pltpu.make_async_copy(patches.at[local], patch_buf.at[k], patch_sem.at[k]).start()

    values = coef[...]
    bases = values.shape[1]
    high = values.astype(jnp.bfloat16).astype(jnp.float32)
    middle = (values - high).astype(jnp.bfloat16).astype(jnp.float32)
    low = values - high - middle
    parts = jnp.concatenate([high, middle, low, jnp.zeros_like(low)], axis=0).astype(jnp.bfloat16)
    to_chip[:COEF_ROWS, :bases] = parts
    to_next[:COEF_ROWS, :bases] = parts

    whole.wait()
    counts = [jnp.int32(0), jnp.int32(0)]
    for s in range(per_strip):
        tile = owner * per_strip + s
        offset = lax.div(margin[0, tile], owned) - owner

        @pl.when(offset != 0)
        def _(s=s, tile=tile, offset=offset, counts=tuple(counts)):
            up = lax.rem(TILE - margin[1, tile], TILE)
            back = lax.rem(TILE - margin[2, tile], TILE)
            moved = pltpu.roll(pltpu.roll(science_buf[:, s * TILE : (s + 1) * TILE], up, 0), back, 1)
            moved16 = moved.astype(jnp.bfloat16)

            @pl.when(offset == sign)
            def _():
                to_chip[pl.ds(pl.multiple_of(RECORD + counts[0] * TILE, EDGE), TILE), :] = moved16

            @pl.when(offset != sign)
            def _():
                to_next[pl.ds(pl.multiple_of(NEAR_ROWS + counts[1] * TILE, EDGE), TILE), :] = moved16

        counts[0] = counts[0] + jnp.where(offset == sign, 1, 0)
        counts[1] = counts[1] + jnp.where(offset == -sign, 1, 0)

    def slot_step(k, carry):
        tile = slot_of[k]

        @pl.when(tile >= 0)
        def _():
            down = margin[1, tile]
            right = margin[2, tile]
            local = lax.rem(margin[0, tile], owned)
            pltpu.make_async_copy(patches.at[local], patch_buf.at[k], patch_sem.at[k]).wait()
            moved = pltpu.roll(pltpu.roll(patch_buf[k], down, 0), right, 1)
            moved16 = moved.astype(jnp.bfloat16)
            aligned[k] = moved16
            relative = lax.div(k, CAP) - 1
            j = lax.rem(k, CAP)
            left = jnp.transpose(moved[:, :HALF])[:EDGE]
            right_edge = jnp.transpose(moved[:, TILE - HALF :])[HALF - RADIUS :]
            empty = jnp.zeros((EDGE - RADIUS, TILE), jnp.float32)
            bottom = jnp.concatenate([moved[TILE - RADIUS :], empty], axis=0)
            right_edge = jnp.concatenate([right_edge, empty], axis=0)
            edges = [moved16[:EDGE]] + [edge.astype(jnp.bfloat16) for edge in (bottom, left, right_edge)]
            for kind in range(KINDS):
                position = piece_position(relative, jnp.int32(kind), sign)
                row = pl.multiple_of(COEF_ROWS + (position * CAP + j) * EDGE, EDGE)
                to_chip[pl.ds(row, EDGE), :] = edges[kind]

                @pl.when(position == 0)
                def _(kind=kind):
                    to_far[pl.ds(pl.multiple_of(j * EDGE, EDGE), EDGE), :] = edges[kind]

        return carry

    lax.fori_loop(0, SLOTS, slot_step, 0)
    to_next[COEF_ROWS:NEAR_ROWS, :] = packed(to_chip, 0, NEAR * CAP)
    to_two[...] = packed(to_chip, NEAR * CAP, PIECES - NEAR * CAP)


def profile(u, sigma, order):
    taps = np.arange(-RADIUS, RADIUS + 1).astype(np.float32)
    total = float(np.sum(np.exp(-taps * taps / np.float32(2.0 * sigma * sigma)), dtype=np.float32))
    shape = jnp.where(jnp.abs(u) <= RADIUS, jnp.exp(-u * u / (2.0 * sigma * sigma)) / total, 0.0)
    for _ in range(order):
        shape = shape * (u / sigma)
    return shape


def fill_tables(across, mixing):
    w = lax.broadcasted_iota(jnp.int32, (TILE, HALF), 0) - lax.broadcasted_iota(jnp.int32, (TILE, HALF), 1)
    w = jnp.where(w > HALF, w - TILE, w).astype(jnp.float32)
    for g in range(SIGMAS):
        for h in range(ORDERS):
            n = g * ORDERS + h
            across[:, n * HALF : (n + 1) * HALF] = profile(w, 0.75 * 2.0**g, h).astype(jnp.bfloat16)
    lanes = SIGMAS * ORDERS * REACH
    for at in range(0, lanes, HALF):
        wide = min(HALF, lanes - at)
        lane = lax.broadcasted_iota(jnp.int32, (HALF, wide), 1) + at
        row = lax.broadcasted_iota(jnp.int32, (HALF, wide), 0)
        one = at // REACH
        two = (at + wide - 1) // REACH
        start = jnp.where(lane < two * REACH, one * REACH, two * REACH)
        u = (lane - start - row - EDGE).astype(jnp.float32)
        low, high = one // ORDERS, two // ORDERS
        sigma = 0.75 * 2.0**low
        if high != low:
            sigma = jnp.where(lane < two * REACH, sigma, 0.75 * 2.0**high)
        totals = []
        for g in (low, high):
            taps = np.arange(-RADIUS, RADIUS + 1).astype(np.float32)
            totals.append(float(np.sum(np.exp(-taps * taps / np.float32(2.0 * (0.75 * 2.0**g) ** 2)), dtype=np.float32)))
        total = totals[0] if high == low else jnp.where(lane < two * REACH, totals[0], totals[1])
        shape = jnp.where(jnp.abs(u) <= RADIUS, jnp.exp(-u * u / (2.0 * sigma * sigma)) / total, 0.0)
        for v in range(ORDERS):
            mixing[v, :, at : at + wide] = shape
            shape = shape * (u / sigma)


def plan_kernel(sizes, margin, ccd_first, from_chip, science, plan, across, mixing, first, rows):
    strips, per_strip, owned = sizes
    owner = lax.axis_index("visit")
    sign = sign_of(owner)
    slots = owned_slots(margin, owner, strips, per_strip, owned)
    ids = [jnp.where(t >= 0, margin[0, jnp.maximum(t, 0)], -1) for t in slots]
    counts = [sum(jnp.where(other == mine, 1, 0) for other in ids) for mine in ids]
    entry = jnp.int32(0)
    places = []
    for k in range(SLOTS):
        places.append(entry)
        entry = entry + jnp.where(slots[k] >= 0, 1, 0)
        plan[k] = slots[k]
        plan[SLOTS + k] = counts[k]
        plan[2 * SLOTS + k] = places[k]
        later = sum((jnp.where(other == ids[k], 1, 0) for other in ids[k + 1 :]), jnp.int32(0))
        plan[3 * SLOTS + 1 + k] = later
    plan[3 * SLOTS] = entry

    for i in range(2 * STRIPS - 1):
        strip = jnp.clip(owner - STRIPS + 1 + i, 0, strips - 1)
        owners = [owner_of(margin[0, strip * per_strip + n], owned) for n in range(per_strip)]
        for n, its_owner in enumerate(owners):
            rank = sum((jnp.where(other == its_owner, 1, 0) for other in owners[:n]), jnp.int32(0))
            start = ((its_owner - owner) * sign + 3) * RECORD + COEF_ROWS + rank * EDGE
            its_sign = sign_of(its_owner)
            for kind in range(KINDS):
                place = piece_position(strip - its_owner, jnp.int32(kind), its_sign)
                rows[(i * per_strip + n) * KINDS + kind] = start + place * PIECE_ROWS

    def piece_row(strip, position, kind, allowed):
        inside = (position >= 0) & (position < per_strip) & allowed
        at = ((strip - owner + STRIPS - 1) * per_strip + position) * KINDS + kind
        return jnp.where(inside, rows[jnp.where(inside, at, 0)], MEMBERS * RECORD)

    def fill(k, carry):
        tile = plan[k]

        @pl.when(tile >= 0)
        def _():
            q = lax.div(k, CAP)
            j = lax.rem(k, CAP)
            strip = owner - 1 + q
            position = tile - strip * per_strip
            local = lax.rem(margin[0, tile], owned)
            up = lax.rem(TILE - margin[1, tile], TILE)
            back = lax.rem(TILE - margin[2, tile], TILE)
            yes = owner >= 0
            keep_top = (strip > 0) & (ccd_first[strip] == 0)
            keep_bottom = (strip < strips - 1) & (ccd_first[jnp.minimum(strip + 1, strips - 1)] == 0)
            at = ENTRY * (plan[2 * SLOTS + k] + HEAD)
            member = (q - 1) * sign
            pieces = (
                (strip, position + 1, LEFT, yes),
                (strip, position - 1, RIGHT, yes),
                (strip - 1, position, BOTTOM, keep_top),
                (strip - 1, position - 1, BOTTOM, keep_top),
                (strip - 1, position + 1, BOTTOM, keep_top),
                (strip + 1, position, TOP, keep_bottom),
                (strip + 1, position - 1, TOP, keep_bottom),
                (strip + 1, position + 1, TOP, keep_bottom),
            )
            for n, args in enumerate(pieces):
                plan[at + n] = piece_row(*args)
            plan[at + 8] = k
            plan[at + 9] = up
            plan[at + 10] = back
            plan[at + 11] = local
            plan[at + 12] = plan[SLOTS + k]
            plan[at + 13] = member + 3
            plan[at + 14] = position
            plan[at + 15] = plan[3 * SLOTS + 1 + k]
            share = share_of(plan[SLOTS + k])

            @pl.when(member == 0)
            def _():
                start = pl.multiple_of(position * TILE, TILE)
                moved = pltpu.roll(pltpu.roll(science[:, pl.ds(start, TILE)], up, 0), back, 1)
                first[local] = first[local] + moved * share

            @pl.when(member == 1)
            def _():
                start = pl.multiple_of(RECORD + j * TILE, EDGE)
                first[local] = first[local] + from_chip[pl.ds(start, TILE), :].astype(jnp.float32) * share

        return carry

    first[...] = jnp.zeros(first.shape, jnp.float32)
    lax.fori_loop(0, SLOTS, fill, 0)
    fill_tables(across, mixing)


def share_of(count):
    share = jnp.float32(1.0)
    for n in range(2, SLOTS + 1):
        share = jnp.where(count == n, jnp.float32(1.0 / n), share)
    return share


def match_kernel(per_strip, plan, aligned, own_record, from_chip, from_next, from_two, from_across, from_far,
                 across, mixing, first, result,
                 frames, window, spread, mixes, total, out, sems):
    def put(member, start, rows, value):
        frames[member * RECORD + start : member * RECORD + start + rows, :] = value

    near = NEAR * PIECE_ROWS
    put(0, COEF_ROWS, PIECE_ROWS, from_far[...])
    put(1, COEF_ROWS + near, RECORD - COEF_ROWS - near, spaced(from_two[...]))
    put(2, 0, COEF_ROWS, from_next[:COEF_ROWS, :])
    put(2, COEF_ROWS, near, spaced(from_next[COEF_ROWS:NEAR_ROWS, :]))
    put(3, 0, RECORD, own_record[:RECORD, :])
    put(4, 0, RECORD, from_chip[:RECORD, :])
    put(5, COEF_ROWS, near, spaced(from_across[COEF_ROWS:NEAR_ROWS, :]))
    put(6, COEF_ROWS + near, RECORD - COEF_ROWS - near, spaced(from_across[NEAR_ROWS:, :]))
    put(MEMBERS, 0, EDGE, jnp.zeros((EDGE, TILE), jnp.bfloat16))
    columns = SIGMAS * ORDERS
    window_rows = TILE + 2 * EDGE
    out[...] = first[...]
    total[...] = jnp.zeros(total.shape, jnp.float32)
    strip_lanes = per_strip

    def base(k):
        return ENTRY * (k + HEAD)

    def lowered(edge):
        empty = jnp.zeros((EDGE - RADIUS, TILE), jnp.float32)
        return jnp.concatenate([empty, edge.astype(jnp.float32)[:RADIUS]], axis=0).astype(jnp.bfloat16)

    def build(k, half):
        at = base(k)

        def piece(n):
            return frames[pl.ds(pl.multiple_of(plan[at + n], EDGE), EDGE), :]

        sides = jnp.concatenate(
            [
                piece(0).astype(jnp.float32),
                jnp.zeros((HALF - EDGE - RADIUS, TILE), jnp.float32),
                piece(1).astype(jnp.float32)[:RADIUS],
            ],
            axis=0,
        )
        sides = jnp.transpose(sides).astype(jnp.bfloat16)

        def place(start, rows, middle_a, middle_b, left_b, right_a):
            low = lax.broadcasted_iota(jnp.int32, (rows, HALF), 1) < HALF // 2
            window[half, start : start + rows, :HALF] = middle_a
            window[half, start : start + rows, HALF:] = jnp.where(low, middle_b, left_b)
            second = window_rows + start
            window[half, second : second + rows, :HALF] = middle_b
            window[half, second : second + rows, HALF:] = jnp.where(low, right_a, middle_a)

        center = aligned[plan[at + 8]]
        place(EDGE, TILE, center[:, :HALF], center[:, HALF:], sides, sides)
        for start, n in ((0, 2), (EDGE + TILE, 5)):
            middle, left, right = piece(n), piece(n + 1), piece(n + 2)
            if start == 0:
                middle, left, right = lowered(middle), lowered(left), lowered(right)
            place(start, EDGE, middle[:, :HALF], middle[:, HALF:], left[:, HALF:], right[:, :HALF])

    def finish(k, half, share):
        at = base(k)
        local = plan[at + 11]
        back = pltpu.roll(pltpu.roll(total[half], plan[at + 9], 0), plan[at + 10], 1)
        out[local] = out[local] - back * share

    count = plan[3 * SLOTS]
    owned = out.shape[0]

    def leave(local):
        return pltpu.make_async_copy(out.at[local], result.at[local], sems.at[local])

    for k in range(SLOTS):
        @pl.when((plan[k] >= 0) & (plan[base(plan[2 * SLOTS + k]) + 13] == 2))
        def _(k=k):
            at = base(plan[2 * SLOTS + k])
            local = plan[at + 11]
            start = NEAR_ROWS + (k % CAP) * TILE
            arrived = from_next[start : start + TILE, :].astype(jnp.float32)
            out[local] = out[local] + arrived * share_of(plan[at + 12])

    for local in range(owned):
        named = sum(
            jnp.where((plan[k] >= 0) & (plan[base(plan[2 * SLOTS + k]) + 11] == local), 1, 0) for k in range(SLOTS)
        )

        @pl.when(named == 0)
        def _(local=local):
            leave(local).start()

    @pl.when(count > 0)
    def _():
        build(0, 0)

    def step(k, carry):
        half = lax.rem(k, 2)
        at = base(k)
        coef_row = pl.multiple_of(plan[at + 13] * RECORD, EDGE)
        block = frames[pl.ds(coef_row, COEF_ROWS), :HALF].astype(jnp.float32)
        rows = lax.broadcasted_iota(jnp.int32, block.shape, 0)
        mine = (lax.rem(rows, strip_lanes) == plan[at + 14]) & (rows < 3 * strip_lanes)
        weights = jnp.sum(jnp.where(mine, block, 0.0), axis=0, keepdims=True)
        lanes = columns * REACH
        for n in range(0, columns, 2):
            if n == 2:
                finish(jnp.maximum(k - 1, 0), 1 - half, jnp.where(k > 0, share_of(plan[base(jnp.maximum(k - 1, 0)) + 12]), 0.0))
            if n == 4:
                build(jnp.minimum(k + 1, count - 1), 1 - half)
            wide = min(2, columns - n)
            h = jnp.dot(window[half], across[:, n * HALF : (n + wide) * HALF], preferred_element_type=jnp.float32)
            h = h.astype(jnp.bfloat16)
            for m in range(wide):
                to = (n + m) * REACH
                for c in range(2):
                    for r in range(2):
                        start = c * window_rows + r * HALF
                        spread[r, to : to + REACH, c * HALF : (c + 1) * HALF] = h[
                            start : start + REACH, m * HALF : (m + 1) * HALF
                        ]
            for at in range(n * REACH // HALF * HALF, min(lanes, (n + 2) * REACH // HALF * HALF), HALF):
                wide_at = min(HALF, lanes - at)
                lane = lax.broadcasted_iota(jnp.int32, (1, wide_at), 1) + at
                mix = jnp.zeros((HALF, wide_at), jnp.float32)
                one = at // REACH
                two = min((at + wide_at - 1) // REACH, columns - 1)
                for v in range(ORDERS):
                    weight = weights[:, one * ORDERS + v : one * ORDERS + v + 1]
                    if two != one:
                        other = weights[:, two * ORDERS + v : two * ORDERS + v + 1]
                        weight = jnp.where(lane < two * REACH, weight, other)
                    mix = mix + weight * mixing[v, :, at : at + wide_at]
                mixes[:, at : at + wide_at] = mix.astype(jnp.bfloat16)
        for r in range(2):
            total[half, r * HALF : (r + 1) * HALF, :] = jnp.dot(
                mixes[...], spread[r], preferred_element_type=jnp.float32
            )
        before = base(jnp.maximum(k - 1, 0))

        @pl.when((k > 0) & (plan[before + 15] == 0))
        def _():
            leave(plan[before + 11]).start()

        return carry

    lax.fori_loop(0, count, step, 0)

    @pl.when(count > 0)
    def _():
        finish(count - 1, lax.rem(count - 1, 2), share_of(plan[base(count - 1) + 12]))
        leave(plan[base(count - 1) + 11]).start()

    for local in range(owned):
        leave(local).wait()


def step(science, patches, margin, kernel_coef, ccd_first):
    strips = lax.axis_size("visit")
    owned = patches.shape[0]
    per_strip = science.shape[1] // TILE
    sizes = (strips, per_strip, owned)
    margin = margin.T
    smem = pl.BlockSpec(memory_space=pltpu.SMEM)
    vmem = pl.BlockSpec(memory_space=pltpu.VMEM)
    hbm = pl.BlockSpec(memory_space=pl.ANY)
    stays = pl.BlockSpec(memory_space=pltpu.HBM)
    bf16 = jnp.bfloat16
    f32 = jnp.float32
    aligned, to_chip, to_next, to_two, to_far = pl.pallas_call(
        functools.partial(pack_kernel, sizes),
        out_shape=(
            jax.ShapeDtypeStruct((SLOTS, TILE, TILE), bf16),
            jax.ShapeDtypeStruct((RECORD + CAP * TILE, TILE), bf16),
            jax.ShapeDtypeStruct((NEAR_ROWS + CAP * TILE, TILE), bf16),
            jax.ShapeDtypeStruct((TWO_ROWS, TILE), bf16),
            jax.ShapeDtypeStruct((PIECE_ROWS, TILE), bf16),
        ),
        in_specs=[stays] * 4,
        out_specs=(vmem, vmem, vmem, vmem, vmem),
        scratch_shapes=[
            pltpu.SMEM(margin.shape, jnp.int32),
            pltpu.VMEM(kernel_coef.shape[::-1], f32),
            pltpu.VMEM((SLOTS, TILE, TILE), f32),
            pltpu.VMEM((TILE, per_strip * TILE), f32),
            pltpu.SMEM((SLOTS,), jnp.int32),
            pltpu.SemaphoreType.DMA((SLOTS,)),
            pltpu.SemaphoreType.DMA,
            pltpu.SemaphoreType.DMA((2,)),
        ],
        compiler_params=pltpu.CompilerParams(vmem_limit_bytes=52 * 2**20),
        name="pack",
    )(margin, kernel_coef.T, patches, science)

    on_chip = [(i, i ^ 1) for i in range(strips)]
    next_chip = [p for i in range(1, strips - 1, 2) for p in ((i, i + 1), (i + 1, i))]
    far = [p for i in range(1, strips - 3, 2) for p in ((i, i + 3), (i + 3, i))]
    two = [p for i in range(0, strips - 2, 2) for p in ((i, i + 2), (i + 3, i + 1))]
    from_next = lax.ppermute(to_next, "visit", next_chip)
    from_two = lax.ppermute(to_two, "visit", two)
    from_far = lax.ppermute(to_far, "visit", far)
    from_chip = lax.ppermute(to_chip, "visit", on_chip)

    columns = SIGMAS * ORDERS
    planned = pl.pallas_call(
        functools.partial(plan_kernel, sizes),
        out_shape=(
            jax.ShapeDtypeStruct((ENTRY * (HEAD + SLOTS),), jnp.int32),
            jax.ShapeDtypeStruct((TILE, columns * HALF), bf16),
            jax.ShapeDtypeStruct((ORDERS, HALF, columns * REACH), f32),
            jax.ShapeDtypeStruct(patches.shape, f32),
        ),
        in_specs=[smem, smem] + [vmem] * 2,
        out_specs=(smem, vmem, vmem, vmem),
        scratch_shapes=[pltpu.SMEM(((2 * STRIPS - 1) * per_strip * KINDS,), jnp.int32)],
        compiler_params=pltpu.CompilerParams(vmem_limit_bytes=12 * 2**20),
        name="plan",
    )(margin, ccd_first, from_chip, science)
    from_next, from_two, from_far, planned = lax.optimization_barrier((from_next, from_two, from_far, planned))
    plan, *tables = planned
    relay = jnp.concatenate([from_next[:NEAR_ROWS], from_two], axis=0)
    from_across = lax.ppermute(relay, "visit", on_chip)

    return pl.pallas_call(
        functools.partial(match_kernel, per_strip),
        out_shape=jax.ShapeDtypeStruct(patches.shape, f32),
        in_specs=[smem] + [vmem] * 10,
        out_specs=stays,
        scratch_shapes=[
            pltpu.VMEM((MEMBERS * RECORD + EDGE, TILE), bf16),
            pltpu.VMEM((2, 2 * (TILE + 2 * EDGE), TILE), bf16),
            pltpu.VMEM((2, columns * REACH, TILE), bf16),
            pltpu.VMEM((HALF, columns * REACH), bf16),
            pltpu.VMEM((2, TILE, TILE), f32),
            pltpu.VMEM(patches.shape, f32),
            pltpu.SemaphoreType.DMA((patches.shape[0],)),
        ],
        compiler_params=pltpu.CompilerParams(vmem_limit_bytes=24 * 2**20),
        name="match",
    )(plan, aligned, to_chip, from_chip, from_next, from_two, from_across, from_far, *tables)


def solution(mesh):
    in_specs = (
        P(("grp", "visit"), None),
        P(("grp", "visit"), None, None),
        P("grp", None),
        P(None, ("grp", "visit")),
        P("grp"),
    )
    out_specs = P(("grp", "visit"), None, None)
    return jax.shard_map(step, mesh=mesh, in_specs=in_specs, out_specs=out_specs, check_vma=False)
```

```python
import functools

import jax
import jax.numpy as jnp
import numpy as np
from jax import lax
from jax.experimental import pallas as pl
from jax.experimental.pallas import tpu as pltpu
from jax.sharding import PartitionSpec as P

TILE = 256
HALF = 128
RADIUS = 10
SIGMAS = 3
ORDERS = 3
EDGE = 16
CAP = 2
STRIPS = 3
SLOTS = STRIPS * CAP
KINDS = 4
TOP, BOTTOM, LEFT, RIGHT = range(KINDS)
PIECES = SLOTS * KINDS
COEF_ROWS = 16
NEAR = 8
PIECE_ROWS = CAP * EDGE
NEAR_ROWS = COEF_ROWS + NEAR * CAP * RADIUS
TWO_ROWS = (STRIPS * KINDS - NEAR) * CAP * RADIUS
RECORD = COEF_ROWS + PIECES * EDGE
MEMBERS = 7
ENTRY = 16
HEAD = 2
REACH = HALF + 2 * EDGE


def owned_slots(margin, owner, strips, per_strip, owned):
    slots = []
    for q in range(STRIPS):
        strip = owner - 1 + q
        inside = (strip >= 0) & (strip < strips)
        base = jnp.clip(strip, 0, strips - 1) * per_strip
        count = jnp.int32(0)
        found = [jnp.int32(-1) for _ in range(CAP)]
        for s in range(per_strip):
            mine = inside & (owner_of(margin[0, base + s], owned) == owner)
            for j in range(CAP):
                found[j] = jnp.where(mine & (count == j), base + s, found[j])
            count = count + jnp.where(mine, 1, 0)
        slots.extend(found)
    return slots


def sign_of(owner):
    return 1 - 2 * lax.rem(owner, 2)


def piece_position(relative, kind, sign):
    along = relative * sign
    facing = jnp.where(sign > 0, kind, jnp.where(kind == TOP, BOTTOM, jnp.where(kind == BOTTOM, TOP, kind)))
    middle = jnp.where(facing == TOP, 4, jnp.where(facing == BOTTOM, 11, facing + 3))
    return jnp.where(along < 0, facing, jnp.where(along > 0, 7 + facing, middle))


def owner_of(patch, owned):
    if owned & (owned - 1) == 0:
        return lax.shift_right_logical(patch, jnp.int32(owned.bit_length() - 1))
    return lax.div(patch, owned)


def packed(record, first, count):
    rows = record[COEF_ROWS + first * EDGE : COEF_ROWS + (first + count) * EDGE, :].astype(jnp.float32)
    return jnp.concatenate([rows[n * EDGE : n * EDGE + RADIUS] for n in range(count)], axis=0).astype(jnp.bfloat16)


def spaced(rows):
    rows = rows.astype(jnp.float32)
    empty = jnp.zeros((EDGE - RADIUS, TILE), jnp.float32)
    pieces = []
    for n in range(rows.shape[0] // RADIUS):
        pieces += [rows[n * RADIUS : (n + 1) * RADIUS], empty]
    return jnp.concatenate(pieces, axis=0).astype(jnp.bfloat16)


def pack_kernel(sizes, margin_hbm, coef_hbm, patches, science, aligned, to_chip, to_next, to_two, to_far,
                margin, coef, patch_buf, science_buf, slot_of, patch_sem, science_sem, small_sem):
    strips, per_strip, owned = sizes
    tables = [
        pltpu.make_async_copy(a, b, small_sem.at[n]) for n, (a, b) in enumerate(((margin_hbm, margin), (coef_hbm, coef)))
    ]
    for copy in tables:
        copy.start()
    whole = pltpu.make_async_copy(science, science_buf, science_sem)
    whole.start()
    to_chip[COEF_ROWS:RECORD, :] = jnp.zeros((RECORD - COEF_ROWS, TILE), jnp.bfloat16)
    to_far[...] = jnp.zeros(to_far.shape, jnp.bfloat16)
    for copy in tables:
        copy.wait()
    owner = lax.axis_index("visit")
    sign = sign_of(owner)
    slots = owned_slots(margin, owner, strips, per_strip, owned)
    for k in range(SLOTS):
        slot_of[k] = slots[k]

        @pl.when(slots[k] >= 0)
        def _(k=k):
            local = lax.rem(margin[0, jnp.maximum(slots[k], 0)], owned)
            pltpu.make_async_copy(patches.at[local], patch_buf.at[k], patch_sem.at[k]).start()

    values = coef[...]
    bases = values.shape[1]
    high = values.astype(jnp.bfloat16).astype(jnp.float32)
    middle = (values - high).astype(jnp.bfloat16).astype(jnp.float32)
    low = values - high - middle
    parts = jnp.concatenate([high, middle, low, jnp.zeros_like(low)], axis=0).astype(jnp.bfloat16)
    to_chip[:COEF_ROWS, :bases] = parts
    to_next[:COEF_ROWS, :bases] = parts

    whole.wait()
    counts = [jnp.int32(0), jnp.int32(0)]
    for s in range(per_strip):
        tile = owner * per_strip + s
        offset = lax.div(margin[0, tile], owned) - owner

        @pl.when(offset != 0)
        def _(s=s, tile=tile, offset=offset, counts=tuple(counts)):
            up = lax.rem(TILE - margin[1, tile], TILE)
            back = lax.rem(TILE - margin[2, tile], TILE)
            moved = pltpu.roll(pltpu.roll(science_buf[:, s * TILE : (s + 1) * TILE], up, 0), back, 1)
            moved16 = moved.astype(jnp.bfloat16)

            @pl.when(offset == sign)
            def _():
                to_chip[pl.ds(pl.multiple_of(RECORD + counts[0] * TILE, EDGE), TILE), :] = moved16

            @pl.when(offset != sign)
            def _():
                to_next[pl.ds(pl.multiple_of(NEAR_ROWS + counts[1] * TILE, EDGE), TILE), :] = moved16

        counts[0] = counts[0] + jnp.where(offset == sign, 1, 0)
        counts[1] = counts[1] + jnp.where(offset == -sign, 1, 0)

    def slot_step(k, carry):
        tile = slot_of[k]

        @pl.when(tile >= 0)
        def _():
            down = margin[1, tile]
            right = margin[2, tile]
            local = lax.rem(margin[0, tile], owned)
            pltpu.make_async_copy(patches.at[local], patch_buf.at[k], patch_sem.at[k]).wait()
            moved = pltpu.roll(pltpu.roll(patch_buf[k], down, 0), right, 1)
            moved16 = moved.astype(jnp.bfloat16)
            aligned[k] = moved16
            relative = lax.div(k, CAP) - 1
            j = lax.rem(k, CAP)
            left = jnp.transpose(moved[:, :HALF])[:EDGE]
            right_edge = jnp.transpose(moved[:, TILE - HALF :])[HALF - RADIUS :]
            empty = jnp.zeros((EDGE - RADIUS, TILE), jnp.float32)
            bottom = jnp.concatenate([moved[TILE - RADIUS :], empty], axis=0)
            right_edge = jnp.concatenate([right_edge, empty], axis=0)
            edges = [moved16[:EDGE]] + [edge.astype(jnp.bfloat16) for edge in (bottom, left, right_edge)]
            for kind in range(KINDS):
                position = piece_position(relative, jnp.int32(kind), sign)
                row = pl.multiple_of(COEF_ROWS + (position * CAP + j) * EDGE, EDGE)
                to_chip[pl.ds(row, EDGE), :] = edges[kind]

                @pl.when(position == 0)
                def _(kind=kind):
                    to_far[pl.ds(pl.multiple_of(j * EDGE, EDGE), EDGE), :] = edges[kind]

        return carry

    lax.fori_loop(0, SLOTS, slot_step, 0)
    to_next[COEF_ROWS:NEAR_ROWS, :] = packed(to_chip, 0, NEAR * CAP)
    to_two[...] = packed(to_chip, NEAR * CAP, PIECES - NEAR * CAP)


def profile(u, sigma, order):
    taps = np.arange(-RADIUS, RADIUS + 1).astype(np.float32)
    total = float(np.sum(np.exp(-taps * taps / np.float32(2.0 * sigma * sigma)), dtype=np.float32))
    shape = jnp.where(jnp.abs(u) <= RADIUS, jnp.exp(-u * u / (2.0 * sigma * sigma)) / total, 0.0)
    for _ in range(order):
        shape = shape * (u / sigma)
    return shape


def fill_tables(across, mixing):
    w = lax.broadcasted_iota(jnp.int32, (TILE, HALF), 0) - lax.broadcasted_iota(jnp.int32, (TILE, HALF), 1)
    w = jnp.where(w > HALF, w - TILE, w).astype(jnp.float32)
    for g in range(SIGMAS):
        for h in range(ORDERS):
            n = g * ORDERS + h
            across[:, n * HALF : (n + 1) * HALF] = profile(w, 0.75 * 2.0**g, h).astype(jnp.bfloat16)
    lanes = SIGMAS * ORDERS * REACH
    for at in range(0, lanes, HALF):
        wide = min(HALF, lanes - at)
        lane = lax.broadcasted_iota(jnp.int32, (HALF, wide), 1) + at
        row = lax.broadcasted_iota(jnp.int32, (HALF, wide), 0)
        one = at // REACH
        two = (at + wide - 1) // REACH
        start = jnp.where(lane < two * REACH, one * REACH, two * REACH)
        u = (lane - start - row - EDGE).astype(jnp.float32)
        low, high = one // ORDERS, two // ORDERS
        sigma = 0.75 * 2.0**low
        if high != low:
            sigma = jnp.where(lane < two * REACH, sigma, 0.75 * 2.0**high)
        totals = []
        for g in (low, high):
            taps = np.arange(-RADIUS, RADIUS + 1).astype(np.float32)
            totals.append(float(np.sum(np.exp(-taps * taps / np.float32(2.0 * (0.75 * 2.0**g) ** 2)), dtype=np.float32)))
        total = totals[0] if high == low else jnp.where(lane < two * REACH, totals[0], totals[1])
        shape = jnp.where(jnp.abs(u) <= RADIUS, jnp.exp(-u * u / (2.0 * sigma * sigma)) / total, 0.0)
        for v in range(ORDERS):
            mixing[v, :, at : at + wide] = shape
            shape = shape * (u / sigma)


def plan_kernel(sizes, margin, ccd_first, from_chip, science, plan, first, rows):
    strips, per_strip, owned = sizes
    owner = lax.axis_index("visit")
    sign = sign_of(owner)
    slots = owned_slots(margin, owner, strips, per_strip, owned)
    ids = [jnp.where(t >= 0, margin[0, jnp.maximum(t, 0)], -1) for t in slots]
    counts = [sum(jnp.where(other == mine, 1, 0) for other in ids) for mine in ids]
    entry = jnp.int32(0)
    places = []
    for k in range(SLOTS):
        places.append(entry)
        entry = entry + jnp.where(slots[k] >= 0, 1, 0)
        plan[k] = slots[k]
        plan[SLOTS + k] = counts[k]
        plan[2 * SLOTS + k] = places[k]
        later = sum((jnp.where(other == ids[k], 1, 0) for other in ids[k + 1 :]), jnp.int32(0))
        plan[3 * SLOTS + 1 + k] = later
    plan[3 * SLOTS] = entry

    for i in range(2 * STRIPS - 1):
        strip = jnp.clip(owner - STRIPS + 1 + i, 0, strips - 1)
        owners = [owner_of(margin[0, strip * per_strip + n], owned) for n in range(per_strip)]
        for n, its_owner in enumerate(owners):
            rank = sum((jnp.where(other == its_owner, 1, 0) for other in owners[:n]), jnp.int32(0))
            start = ((its_owner - owner) * sign + 3) * RECORD + COEF_ROWS + rank * EDGE
            its_sign = sign_of(its_owner)
            for kind in range(KINDS):
                place = piece_position(strip - its_owner, jnp.int32(kind), its_sign)
                rows[(i * per_strip + n) * KINDS + kind] = start + place * PIECE_ROWS

    def piece_row(strip, position, kind, allowed):
        inside = (position >= 0) & (position < per_strip) & allowed
        at = ((strip - owner + STRIPS - 1) * per_strip + position) * KINDS + kind
        return jnp.where(inside, rows[jnp.where(inside, at, 0)], MEMBERS * RECORD)

    def fill(k, carry):
        tile = plan[k]

        @pl.when(tile >= 0)
        def _():
            q = lax.div(k, CAP)
            j = lax.rem(k, CAP)
            strip = owner - 1 + q
            position = tile - strip * per_strip
            local = lax.rem(margin[0, tile], owned)
            up = lax.rem(TILE - margin[1, tile], TILE)
            back = lax.rem(TILE - margin[2, tile], TILE)
            yes = owner >= 0
            keep_top = (strip > 0) & (ccd_first[strip] == 0)
            keep_bottom = (strip < strips - 1) & (ccd_first[jnp.minimum(strip + 1, strips - 1)] == 0)
            at = ENTRY * (plan[2 * SLOTS + k] + HEAD)
            member = (q - 1) * sign
            pieces = (
                (strip, position + 1, LEFT, yes),
                (strip, position - 1, RIGHT, yes),
                (strip - 1, position, BOTTOM, keep_top),
                (strip - 1, position - 1, BOTTOM, keep_top),
                (strip - 1, position + 1, BOTTOM, keep_top),
                (strip + 1, position, TOP, keep_bottom),
                (strip + 1, position - 1, TOP, keep_bottom),
                (strip + 1, position + 1, TOP, keep_bottom),
            )
            for n, args in enumerate(pieces):
                plan[at + n] = piece_row(*args)
            plan[at + 8] = k
            plan[at + 9] = up
            plan[at + 10] = back
            plan[at + 11] = local
            plan[at + 12] = plan[SLOTS + k]
            plan[at + 13] = member + 3
            plan[at + 14] = position
            plan[at + 15] = plan[3 * SLOTS + 1 + k]
            share = share_of(plan[SLOTS + k])

            @pl.when(member == 0)
            def _():
                start = pl.multiple_of(position * TILE, TILE)
                moved = pltpu.roll(pltpu.roll(science[:, pl.ds(start, TILE)], up, 0), back, 1)
                first[local] = first[local] + moved * share

            @pl.when(member == 1)
            def _():
                start = pl.multiple_of(RECORD + j * TILE, EDGE)
                first[local] = first[local] + from_chip[pl.ds(start, TILE), :].astype(jnp.float32) * share

        return carry

    first[...] = jnp.zeros(first.shape, jnp.float32)
    lax.fori_loop(0, SLOTS, fill, 0)


def share_of(count):
    share = jnp.float32(1.0)
    for n in range(2, SLOTS + 1):
        share = jnp.where(count == n, jnp.float32(1.0 / n), share)
    return share


def match_kernel(per_strip, plan, aligned, own_record, from_chip, from_next, from_two, from_across, from_far,
                 across, mixing, first, result,
                 frames, window, spread, mixes, total, out, sems):
    def put(member, start, rows, value):
        frames[member * RECORD + start : member * RECORD + start + rows, :] = value

    near = NEAR * PIECE_ROWS
    put(0, COEF_ROWS, PIECE_ROWS, from_far[...])
    put(1, COEF_ROWS + near, RECORD - COEF_ROWS - near, spaced(from_two[...]))
    put(2, 0, COEF_ROWS, from_next[:COEF_ROWS, :])
    put(2, COEF_ROWS, near, spaced(from_next[COEF_ROWS:NEAR_ROWS, :]))
    put(3, 0, RECORD, own_record[:RECORD, :])
    put(4, 0, RECORD, from_chip[:RECORD, :])
    put(5, COEF_ROWS, near, spaced(from_across[COEF_ROWS:NEAR_ROWS, :]))
    put(6, COEF_ROWS + near, RECORD - COEF_ROWS - near, spaced(from_across[NEAR_ROWS:, :]))
    put(MEMBERS, 0, EDGE, jnp.zeros((EDGE, TILE), jnp.bfloat16))
    columns = SIGMAS * ORDERS
    window_rows = TILE + 2 * EDGE
    out[...] = first[...]
    total[...] = jnp.zeros(total.shape, jnp.float32)
    strip_lanes = per_strip

    def base(k):
        return ENTRY * (k + HEAD)

    def lowered(edge):
        empty = jnp.zeros((EDGE - RADIUS, TILE), jnp.float32)
        return jnp.concatenate([empty, edge.astype(jnp.float32)[:RADIUS]], axis=0).astype(jnp.bfloat16)

    def build(k, half):
        at = base(k)

        def piece(n):
            return frames[pl.ds(pl.multiple_of(plan[at + n], EDGE), EDGE), :]

        sides = jnp.concatenate(
            [
                piece(0).astype(jnp.float32),
                jnp.zeros((HALF - EDGE - RADIUS, TILE), jnp.float32),
                piece(1).astype(jnp.float32)[:RADIUS],
            ],
            axis=0,
        )
        sides = jnp.transpose(sides).astype(jnp.bfloat16)

        def place(start, rows, middle_a, middle_b, left_b, right_a):
            low = lax.broadcasted_iota(jnp.int32, (rows, HALF), 1) < HALF // 2
            window[half, start : start + rows, :HALF] = middle_a
            window[half, start : start + rows, HALF:] = jnp.where(low, middle_b, left_b)
            second = window_rows + start
            window[half, second : second + rows, :HALF] = middle_b
            window[half, second : second + rows, HALF:] = jnp.where(low, right_a, middle_a)

        center = aligned[plan[at + 8]]
        place(EDGE, TILE, center[:, :HALF], center[:, HALF:], sides, sides)
        for start, n in ((0, 2), (EDGE + TILE, 5)):
            middle, left, right = piece(n), piece(n + 1), piece(n + 2)
            if start == 0:
                middle, left, right = lowered(middle), lowered(left), lowered(right)
            place(start, EDGE, middle[:, :HALF], middle[:, HALF:], left[:, HALF:], right[:, :HALF])

    def finish(k, half, share):
        at = base(k)
        local = plan[at + 11]
        back = pltpu.roll(pltpu.roll(total[half], plan[at + 9], 0), plan[at + 10], 1)
        out[local] = out[local] - back * share

    count = plan[3 * SLOTS]
    owned = out.shape[0]

    def leave(local):
        return pltpu.make_async_copy(out.at[local], result.at[local], sems.at[local])

    for k in range(SLOTS):
        @pl.when((plan[k] >= 0) & (plan[base(plan[2 * SLOTS + k]) + 13] == 2))
        def _(k=k):
            at = base(plan[2 * SLOTS + k])
            local = plan[at + 11]
            start = NEAR_ROWS + (k % CAP) * TILE
            arrived = from_next[start : start + TILE, :].astype(jnp.float32)
            out[local] = out[local] + arrived * share_of(plan[at + 12])

    for local in range(owned):
        named = sum(
            jnp.where((plan[k] >= 0) & (plan[base(plan[2 * SLOTS + k]) + 11] == local), 1, 0) for k in range(SLOTS)
        )

        @pl.when(named == 0)
        def _(local=local):
            leave(local).start()

    @pl.when(count > 0)
    def _():
        build(0, 0)

    def step(k, carry):
        half = lax.rem(k, 2)
        at = base(k)
        coef_row = pl.multiple_of(plan[at + 13] * RECORD, EDGE)
        block = frames[pl.ds(coef_row, COEF_ROWS), :HALF].astype(jnp.float32)
        rows = lax.broadcasted_iota(jnp.int32, block.shape, 0)
        mine = (lax.rem(rows, strip_lanes) == plan[at + 14]) & (rows < 3 * strip_lanes)
        weights = jnp.sum(jnp.where(mine, block, 0.0), axis=0, keepdims=True)
        lanes = columns * REACH
        for n in range(0, columns, 2):
            if n == 2:
                finish(jnp.maximum(k - 1, 0), 1 - half, jnp.where(k > 0, share_of(plan[base(jnp.maximum(k - 1, 0)) + 12]), 0.0))
            if n == 4:
                build(jnp.minimum(k + 1, count - 1), 1 - half)
            wide = min(2, columns - n)
            h = jnp.dot(window[half], across[:, n * HALF : (n + wide) * HALF], preferred_element_type=jnp.float32)
            h = h.astype(jnp.bfloat16)
            for m in range(wide):
                to = (n + m) * REACH
                for c in range(2):
                    for r in range(2):
                        start = c * window_rows + r * HALF
                        spread[r, to : to + REACH, c * HALF : (c + 1) * HALF] = h[
                            start : start + REACH, m * HALF : (m + 1) * HALF
                        ]
            for at in range(n * REACH // HALF * HALF, min(lanes, (n + 2) * REACH // HALF * HALF), HALF):
                wide_at = min(HALF, lanes - at)
                lane = lax.broadcasted_iota(jnp.int32, (1, wide_at), 1) + at
                mix = jnp.zeros((HALF, wide_at), jnp.float32)
                one = at // REACH
                two = min((at + wide_at - 1) // REACH, columns - 1)
                for v in range(ORDERS):
                    weight = weights[:, one * ORDERS + v : one * ORDERS + v + 1]
                    if two != one:
                        other = weights[:, two * ORDERS + v : two * ORDERS + v + 1]
                        weight = jnp.where(lane < two * REACH, weight, other)
                    mix = mix + weight * mixing[v, :, at : at + wide_at]
                mixes[:, at : at + wide_at] = mix.astype(jnp.bfloat16)
        for r in range(2):
            total[half, r * HALF : (r + 1) * HALF, :] = jnp.dot(
                mixes[...], spread[r], preferred_element_type=jnp.float32
            )
        before = base(jnp.maximum(k - 1, 0))

        @pl.when((k > 0) & (plan[before + 15] == 0))
        def _():
            leave(plan[before + 11]).start()

        return carry

    lax.fori_loop(0, count, step, 0)

    @pl.when(count > 0)
    def _():
        finish(count - 1, lax.rem(count - 1, 2), share_of(plan[base(count - 1) + 12]))
        leave(plan[base(count - 1) + 11]).start()

    for local in range(owned):
        leave(local).wait()


def step(science, patches, margin, kernel_coef, ccd_first):
    strips = lax.axis_size("visit")
    owned = patches.shape[0]
    per_strip = science.shape[1] // TILE
    sizes = (strips, per_strip, owned)
    margin = margin.T
    smem = pl.BlockSpec(memory_space=pltpu.SMEM)
    vmem = pl.BlockSpec(memory_space=pltpu.VMEM)
    hbm = pl.BlockSpec(memory_space=pl.ANY)
    stays = pl.BlockSpec(memory_space=pltpu.HBM)
    bf16 = jnp.bfloat16
    f32 = jnp.float32
    columns = SIGMAS * ORDERS
    tables = pl.pallas_call(
        fill_tables,
        out_shape=(
            jax.ShapeDtypeStruct((TILE, columns * HALF), bf16),
            jax.ShapeDtypeStruct((ORDERS, HALF, columns * REACH), f32),
        ),
        in_specs=[],
        out_specs=(vmem, vmem),
        compiler_params=pltpu.CompilerParams(vmem_limit_bytes=8 * 2**20),
        cost_estimate=pl.CostEstimate(flops=2 * 10**9, bytes_accessed=3 * 2**20, transcendentals=10**6),
        name="tables",
    )()
    aligned, to_chip, to_next, to_two, to_far = pl.pallas_call(
        functools.partial(pack_kernel, sizes),
        out_shape=(
            jax.ShapeDtypeStruct((SLOTS, TILE, TILE), bf16),
            jax.ShapeDtypeStruct((RECORD + CAP * TILE, TILE), bf16),
            jax.ShapeDtypeStruct((NEAR_ROWS + CAP * TILE, TILE), bf16),
            jax.ShapeDtypeStruct((TWO_ROWS, TILE), bf16),
            jax.ShapeDtypeStruct((PIECE_ROWS, TILE), bf16),
        ),
        in_specs=[stays] * 4,
        out_specs=(vmem, vmem, vmem, vmem, vmem),
        scratch_shapes=[
            pltpu.SMEM(margin.shape, jnp.int32),
            pltpu.VMEM(kernel_coef.shape[::-1], f32),
            pltpu.VMEM((SLOTS, TILE, TILE), f32),
            pltpu.VMEM((TILE, per_strip * TILE), f32),
            pltpu.SMEM((SLOTS,), jnp.int32),
            pltpu.SemaphoreType.DMA((SLOTS,)),
            pltpu.SemaphoreType.DMA,
            pltpu.SemaphoreType.DMA((2,)),
        ],
        compiler_params=pltpu.CompilerParams(vmem_limit_bytes=52 * 2**20),
        name="pack",
    )(margin, kernel_coef.T, patches, science)

    on_chip = [(i, i ^ 1) for i in range(strips)]
    next_chip = [p for i in range(1, strips - 1, 2) for p in ((i, i + 1), (i + 1, i))]
    far = [p for i in range(1, strips - 3, 2) for p in ((i, i + 3), (i + 3, i))]
    two = [p for i in range(0, strips - 2, 2) for p in ((i, i + 2), (i + 3, i + 1))]
    from_next = lax.ppermute(to_next, "visit", next_chip)
    from_two = lax.ppermute(to_two, "visit", two)
    from_far = lax.ppermute(to_far, "visit", far)
    from_chip = lax.ppermute(to_chip, "visit", on_chip)

    planned = pl.pallas_call(
        functools.partial(plan_kernel, sizes),
        out_shape=(
            jax.ShapeDtypeStruct((ENTRY * (HEAD + SLOTS),), jnp.int32),
            jax.ShapeDtypeStruct(patches.shape, f32),
        ),
        in_specs=[smem, smem] + [vmem] * 2,
        out_specs=(smem, vmem),
        scratch_shapes=[pltpu.SMEM(((2 * STRIPS - 1) * per_strip * KINDS,), jnp.int32)],
        compiler_params=pltpu.CompilerParams(vmem_limit_bytes=12 * 2**20),
        name="plan",
    )(margin, ccd_first, from_chip, science)
    from_next, from_two, from_far, planned = lax.optimization_barrier((from_next, from_two, from_far, planned))
    plan, first = planned
    relay = jnp.concatenate([from_next[:NEAR_ROWS], from_two], axis=0)
    from_across = lax.ppermute(relay, "visit", on_chip)

    return pl.pallas_call(
        functools.partial(match_kernel, per_strip),
        out_shape=jax.ShapeDtypeStruct(patches.shape, f32),
        in_specs=[smem] + [vmem] * 10,
        out_specs=stays,
        scratch_shapes=[
            pltpu.VMEM((MEMBERS * RECORD + EDGE, TILE), bf16),
            pltpu.VMEM((2, 2 * (TILE + 2 * EDGE), TILE), bf16),
            pltpu.VMEM((2, columns * REACH, TILE), bf16),
            pltpu.VMEM((HALF, columns * REACH), bf16),
            pltpu.VMEM((2, TILE, TILE), f32),
            pltpu.VMEM(patches.shape, f32),
            pltpu.SemaphoreType.DMA((patches.shape[0],)),
        ],
        compiler_params=pltpu.CompilerParams(vmem_limit_bytes=24 * 2**20),
        name="match",
    )(plan, aligned, to_chip, from_chip, from_next, from_two, from_across, from_far, *tables, first)


def solution(mesh):
    in_specs = (
        P(("grp", "visit"), None),
        P(("grp", "visit"), None, None),
        P("grp", None),
        P(None, ("grp", "visit")),
        P("grp"),
    )
    out_specs = P(("grp", "visit"), None, None)
    return jax.shard_map(step, mesh=mesh, in_specs=in_specs, out_specs=out_specs, check_vma=False)
```

```python
import functools

import jax
import jax.numpy as jnp
import numpy as np
from jax import lax
from jax.experimental import pallas as pl
from jax.experimental.pallas import tpu as pltpu
from jax.sharding import PartitionSpec as P

TILE = 256
HALF = 128
RADIUS = 10
SIGMAS = 3
ORDERS = 3
EDGE = 16
CAP = 2
STRIPS = 3
SLOTS = STRIPS * CAP
KINDS = 4
TOP, BOTTOM, LEFT, RIGHT = range(KINDS)
PIECES = SLOTS * KINDS
COEF_ROWS = 16
NEAR = 8
PIECE_ROWS = CAP * EDGE
NEAR_ROWS = COEF_ROWS + NEAR * CAP * RADIUS
TWO_ROWS = (STRIPS * KINDS - NEAR) * CAP * RADIUS
RECORD = COEF_ROWS + PIECES * EDGE
EARLY = 5
LATE = 2
ZEROS = EARLY * RECORD
LATE_ROW = ZEROS + EDGE
ENTRY = 16
HEAD = 2
REACH = HALF + 2 * EDGE


def owned_slots(margin, owner, strips, per_strip, owned):
    slots = []
    for q in range(STRIPS):
        strip = owner - 1 + q
        inside = (strip >= 0) & (strip < strips)
        base = jnp.clip(strip, 0, strips - 1) * per_strip
        count = jnp.int32(0)
        found = [jnp.int32(-1) for _ in range(CAP)]
        for s in range(per_strip):
            mine = inside & (owner_of(margin[0, base + s], owned) == owner)
            for j in range(CAP):
                found[j] = jnp.where(mine & (count == j), base + s, found[j])
            count = count + jnp.where(mine, 1, 0)
        slots.extend(found)
    return slots


def sign_of(owner):
    return 1 - 2 * lax.rem(owner, 2)


def piece_position(relative, kind, sign):
    along = relative * sign
    facing = jnp.where(sign > 0, kind, jnp.where(kind == TOP, BOTTOM, jnp.where(kind == BOTTOM, TOP, kind)))
    middle = jnp.where(facing == TOP, 4, jnp.where(facing == BOTTOM, 11, facing + 3))
    return jnp.where(along < 0, facing, jnp.where(along > 0, 7 + facing, middle))


def owner_of(patch, owned):
    if owned & (owned - 1) == 0:
        return lax.shift_right_logical(patch, jnp.int32(owned.bit_length() - 1))
    return lax.div(patch, owned)


def packed(record, first, count):
    rows = record[COEF_ROWS + first * EDGE : COEF_ROWS + (first + count) * EDGE, :].astype(jnp.float32)
    return jnp.concatenate([rows[n * EDGE : n * EDGE + RADIUS] for n in range(count)], axis=0).astype(jnp.bfloat16)


def spaced(rows):
    rows = rows.astype(jnp.float32)
    empty = jnp.zeros((EDGE - RADIUS, TILE), jnp.float32)
    pieces = []
    for n in range(rows.shape[0] // RADIUS):
        pieces += [rows[n * RADIUS : (n + 1) * RADIUS], empty]
    return jnp.concatenate(pieces, axis=0).astype(jnp.bfloat16)


def column_half(patches, local, patch_buf, k, n, sem):
    source = patches.at[local, :, pl.ds(n * HALF, HALF)]
    return pltpu.make_async_copy(source, patch_buf.at[k, n, pl.ds(0, TILE)], sem.at[k, n])


def pack_kernel(sizes, margin_hbm, coef_hbm, patches, science, aligned, to_chip, to_next, to_two, to_far,
                margin, coef, patch_buf, science_buf, slot_of, patch_sem, science_sem, small_sem):
    strips, per_strip, owned = sizes
    tables = [
        pltpu.make_async_copy(a, b, small_sem.at[n]) for n, (a, b) in enumerate(((margin_hbm, margin), (coef_hbm, coef)))
    ]
    for copy in tables:
        copy.start()
    blocks = [
        pltpu.make_async_copy(
            science.at[:, pl.ds(n * HALF, HALF)], science_buf.at[n, pl.ds(0, TILE)], science_sem.at[n]
        )
        for n in range(2 * per_strip)
    ]
    for copy in blocks:
        copy.start()
    for copy in tables:
        copy.wait()
    owner = lax.axis_index("visit")
    sign = sign_of(owner)
    slots = owned_slots(margin, owner, strips, per_strip, owned)
    for k in range(SLOTS):
        slot_of[k] = slots[k]

        @pl.when(slots[k] >= 0)
        def _(k=k):
            local = lax.rem(margin[0, jnp.maximum(slots[k], 0)], owned)
            for n in range(2):
                column_half(patches, local, patch_buf, k, n, patch_sem).start()

    values = coef[...]
    bases = values.shape[1]
    high = values.astype(jnp.bfloat16).astype(jnp.float32)
    middle = (values - high).astype(jnp.bfloat16).astype(jnp.float32)
    low = values - high - middle
    parts = jnp.concatenate([high, middle, low, jnp.zeros_like(low)], axis=0).astype(jnp.bfloat16)
    to_chip[:COEF_ROWS, :bases] = parts
    to_next[:COEF_ROWS, :bases] = parts

    for copy in blocks:
        copy.wait()
    counts = [jnp.int32(0), jnp.int32(0)]
    for s in range(per_strip):
        tile = owner * per_strip + s
        offset = lax.div(margin[0, tile], owned) - owner

        @pl.when(offset != 0)
        def _(s=s, tile=tile, offset=offset, counts=tuple(counts)):
            back = lax.rem(TILE - margin[2, tile], TILE)
            rows = pl.ds(margin[1, tile], TILE)
            for n in (2 * s, 2 * s + 1):
                science_buf[n, TILE:, :] = science_buf[n, :TILE, :]
            moved = jnp.concatenate([science_buf[2 * s, rows, :], science_buf[2 * s + 1, rows, :]], axis=1)
            moved = pltpu.roll(moved, back, 1)
            moved16 = moved.astype(jnp.bfloat16)

            @pl.when(offset == sign)
            def _():
                to_chip[pl.ds(pl.multiple_of(RECORD + counts[0] * TILE, EDGE), TILE), :] = moved16

            @pl.when(offset != sign)
            def _():
                to_next[pl.ds(pl.multiple_of(NEAR_ROWS + counts[1] * TILE, EDGE), TILE), :] = moved16

        counts[0] = counts[0] + jnp.where(offset == sign, 1, 0)
        counts[1] = counts[1] + jnp.where(offset == -sign, 1, 0)

    def strip_step(q, carry):
        for j in range(CAP):
            k = q * CAP + j
            tile = slot_of[k]

            @pl.when(tile >= 0)
            def _(k=k, tile=tile):
                local = lax.rem(margin[0, tile], owned)
                for n in range(2):
                    column_half(patches, local, patch_buf, k, n, patch_sem).wait()

        for j in range(CAP):
            k = q * CAP + j
            tile = jnp.maximum(slot_of[k], 0)
            for n in range(2):
                patch_buf[k, n, TILE:, :] = patch_buf[k, n, :TILE, :]
            rows = pl.ds(TILE - margin[1, tile], TILE)
            moved = jnp.concatenate([patch_buf[k, 0, rows, :], patch_buf[k, 1, rows, :]], axis=1)
            moved = pltpu.roll(moved, margin[2, tile], 1)
            moved16 = moved.astype(jnp.bfloat16)
            aligned[k] = moved16
            left = jnp.transpose(moved[:, :HALF])[:EDGE]
            right_edge = jnp.transpose(moved[:, TILE - HALF :])[HALF - RADIUS :]
            empty = jnp.zeros((EDGE - RADIUS, TILE), jnp.float32)
            bottom = jnp.concatenate([moved[TILE - RADIUS :], empty], axis=0)
            right_edge = jnp.concatenate([right_edge, empty], axis=0)
            edges = [moved16[:EDGE]] + [edge.astype(jnp.bfloat16) for edge in (bottom, left, right_edge)]
            for kind in range(KINDS):
                position = piece_position(q - 1, jnp.int32(kind), sign)
                row = pl.multiple_of(COEF_ROWS + (position * CAP + j) * EDGE, EDGE)
                to_chip[pl.ds(row, EDGE), :] = edges[kind]
        return carry

    for k in range(SLOTS):

        @pl.when(slots[k] < 0)
        def _(k=k):
            patch_buf[k, :, :TILE, :] = jnp.zeros((2, TILE, HALF), jnp.float32)

    lax.fori_loop(0, STRIPS, strip_step, 0)
    to_far[...] = to_chip[COEF_ROWS : COEF_ROWS + PIECE_ROWS, :]
    to_next[COEF_ROWS:NEAR_ROWS, :] = packed(to_chip, 0, NEAR * CAP)
    to_two[...] = packed(to_chip, NEAR * CAP, PIECES - NEAR * CAP)


def profile(u, sigma, order):
    taps = np.arange(-RADIUS, RADIUS + 1).astype(np.float32)
    total = float(np.sum(np.exp(-taps * taps / np.float32(2.0 * sigma * sigma)), dtype=np.float32))
    shape = jnp.where(jnp.abs(u) <= RADIUS, jnp.exp(-u * u / (2.0 * sigma * sigma)) / total, 0.0)
    for _ in range(order):
        shape = shape * (u / sigma)
    return shape


def fill_tables(across, mixing):
    w = lax.broadcasted_iota(jnp.int32, (TILE, HALF), 0) - lax.broadcasted_iota(jnp.int32, (TILE, HALF), 1)
    w = jnp.where(w > HALF, w - TILE, w).astype(jnp.float32)
    for g in range(SIGMAS):
        for h in range(ORDERS):
            n = g * ORDERS + h
            across[:, n * HALF : (n + 1) * HALF] = profile(w, 0.75 * 2.0**g, h).astype(jnp.bfloat16)
    lanes = SIGMAS * ORDERS * REACH
    for at in range(0, lanes, HALF):
        wide = min(HALF, lanes - at)
        lane = lax.broadcasted_iota(jnp.int32, (HALF, wide), 1) + at
        row = lax.broadcasted_iota(jnp.int32, (HALF, wide), 0)
        one = at // REACH
        two = (at + wide - 1) // REACH
        start = jnp.where(lane < two * REACH, one * REACH, two * REACH)
        u = (lane - start - row - EDGE).astype(jnp.float32)
        low, high = one // ORDERS, two // ORDERS
        sigma = 0.75 * 2.0**low
        if high != low:
            sigma = jnp.where(lane < two * REACH, sigma, 0.75 * 2.0**high)
        totals = []
        for g in (low, high):
            taps = np.arange(-RADIUS, RADIUS + 1).astype(np.float32)
            totals.append(float(np.sum(np.exp(-taps * taps / np.float32(2.0 * (0.75 * 2.0**g) ** 2)), dtype=np.float32)))
        total = totals[0] if high == low else jnp.where(lane < two * REACH, totals[0], totals[1])
        shape = jnp.where(jnp.abs(u) <= RADIUS, jnp.exp(-u * u / (2.0 * sigma * sigma)) / total, 0.0)
        for v in range(ORDERS):
            mixing[v, :, at : at + wide] = shape
            shape = shape * (u / sigma)


def plan_kernel(sizes, margin, ccd_first, from_chip, science, plan, first, rows):
    strips, per_strip, owned = sizes
    owner = lax.axis_index("visit")
    sign = sign_of(owner)
    slots = owned_slots(margin, owner, strips, per_strip, owned)
    ids = [jnp.where(t >= 0, margin[0, jnp.maximum(t, 0)], -1) for t in slots]
    counts = [sum(jnp.where(other == mine, 1, 0) for other in ids) for mine in ids]
    entry = jnp.int32(0)
    places = []
    for k in range(SLOTS):
        places.append(entry)
        entry = entry + jnp.where(slots[k] >= 0, 1, 0)
        plan[k] = slots[k]
        plan[SLOTS + k] = counts[k]
        plan[2 * SLOTS + k] = places[k]
        later = sum((jnp.where(other == ids[k], 1, 0) for other in ids[k + 1 :]), jnp.int32(0))
        sooner = sum((jnp.where(other == ids[k], 1, 0) for other in ids[:k]), jnp.int32(0))
        plan[3 * SLOTS + 1 + k] = later + SLOTS * sooner
    plan[3 * SLOTS] = entry

    for i in range(2 * STRIPS - 1):
        strip = jnp.clip(owner - STRIPS + 1 + i, 0, strips - 1)
        owners = [owner_of(margin[0, strip * per_strip + n], owned) for n in range(per_strip)]
        for n, its_owner in enumerate(owners):
            rank = sum((jnp.where(other == its_owner, 1, 0) for other in owners[:n]), jnp.int32(0))
            member = (its_owner - owner) * sign + 3
            start = member * RECORD + jnp.where(member < EARLY, 0, EDGE) + COEF_ROWS + rank * EDGE
            its_sign = sign_of(its_owner)
            for kind in range(KINDS):
                place = piece_position(strip - its_owner, jnp.int32(kind), its_sign)
                rows[(i * per_strip + n) * KINDS + kind] = start + place * PIECE_ROWS

    def piece_row(strip, position, kind, allowed):
        inside = (position >= 0) & (position < per_strip) & allowed
        at = ((strip - owner + STRIPS - 1) * per_strip + position) * KINDS + kind
        return jnp.where(inside, rows[jnp.where(inside, at, 0)], ZEROS)

    def fill(k, carry):
        tile = plan[k]

        @pl.when(tile >= 0)
        def _():
            q = lax.div(k, CAP)
            j = lax.rem(k, CAP)
            strip = owner - 1 + q
            position = tile - strip * per_strip
            local = lax.rem(margin[0, tile], owned)
            up = lax.rem(TILE - margin[1, tile], TILE)
            back = lax.rem(TILE - margin[2, tile], TILE)
            yes = owner >= 0
            keep_top = (strip > 0) & (ccd_first[strip] == 0)
            keep_bottom = (strip < strips - 1) & (ccd_first[jnp.minimum(strip + 1, strips - 1)] == 0)
            at = ENTRY * (plan[2 * SLOTS + k] + HEAD)
            member = (q - 1) * sign
            pieces = (
                (strip, position + 1, LEFT, yes),
                (strip, position - 1, RIGHT, yes),
                (strip - 1, position, BOTTOM, keep_top),
                (strip - 1, position - 1, BOTTOM, keep_top),
                (strip - 1, position + 1, BOTTOM, keep_top),
                (strip + 1, position, TOP, keep_bottom),
                (strip + 1, position - 1, TOP, keep_bottom),
                (strip + 1, position + 1, TOP, keep_bottom),
            )
            for n, args in enumerate(pieces):
                plan[at + n] = piece_row(*args)
            plan[at + 8] = k
            plan[at + 9] = up
            plan[at + 10] = back
            plan[at + 11] = local
            plan[at + 12] = plan[SLOTS + k]
            plan[at + 13] = member + 3
            plan[at + 14] = position
            plan[at + 15] = plan[3 * SLOTS + 1 + k]
            share = share_of(plan[SLOTS + k])

            @pl.when(member == 0)
            def _():
                start = pl.multiple_of(position * TILE, TILE)
                moved = pltpu.roll(pltpu.roll(science[:, pl.ds(start, TILE)], up, 0), back, 1)
                first[local] = first[local] + moved * share

            @pl.when(member == 1)
            def _():
                start = pl.multiple_of(RECORD + j * TILE, EDGE)
                first[local] = first[local] + from_chip[pl.ds(start, TILE), :].astype(jnp.float32) * share

        return carry

    first[...] = jnp.zeros(first.shape, jnp.float32)
    lax.fori_loop(0, SLOTS, fill, 0)


def share_of(count):
    share = jnp.float32(1.0)
    for n in range(2, SLOTS + 1):
        share = jnp.where(count == n, jnp.float32(1.0 / n), share)
    return share


def base(k):
    return ENTRY * (k + HEAD)


def prepare_kernel(plan, own_record, from_chip, from_next, from_two, from_far, first, frames, start):
    def put(member, row, value):
        at = member * RECORD + row
        frames[at : at + value.shape[0], :] = value

    near = COEF_ROWS + NEAR * PIECE_ROWS
    put(0, COEF_ROWS, from_far[...])
    put(1, near, spaced(from_two[...]))
    put(2, 0, from_next[:COEF_ROWS, :])
    put(2, COEF_ROWS, spaced(from_next[COEF_ROWS:NEAR_ROWS, :]))
    put(3, 0, own_record[:RECORD, :])
    put(4, 0, from_chip[:RECORD, :])
    put(EARLY, 0, jnp.zeros((EDGE, TILE), jnp.bfloat16))
    start[...] = first[...]
    for k in range(SLOTS):

        @pl.when((plan[k] >= 0) & (plan[base(plan[2 * SLOTS + k]) + 13] == 2))
        def _(k=k):
            at = base(plan[2 * SLOTS + k])
            local = plan[at + 11]
            row = NEAR_ROWS + (k % CAP) * TILE
            arrived = from_next[row : row + TILE, :].astype(jnp.float32)
            start[local] = start[local] + arrived * share_of(plan[at + 12])


def match_kernel(per_strip, plan, aligned, frames, from_across, across, mixing, start, result,
                 late, window, spread, mixes, total, out, sems):
    near = COEF_ROWS + NEAR * PIECE_ROWS
    late[COEF_ROWS:near, :] = spaced(from_across[COEF_ROWS:NEAR_ROWS, :])
    late[RECORD + near :, :] = spaced(from_across[NEAR_ROWS:, :])
    columns = SIGMAS * ORDERS
    window_rows = TILE + 2 * EDGE
    total[...] = jnp.zeros(total.shape, jnp.float32)
    strip_lanes = per_strip

    def lowered(edge):
        empty = jnp.zeros((EDGE - RADIUS, TILE), jnp.float32)
        return jnp.concatenate([empty, edge.astype(jnp.float32)[:RADIUS]], axis=0).astype(jnp.bfloat16)

    def build(k, half):
        at = base(k)

        def piece(n):
            row = plan[at + n]
            here = frames[pl.ds(pl.multiple_of(jnp.minimum(row, ZEROS), EDGE), EDGE), :]
            then = late[pl.ds(pl.multiple_of(jnp.maximum(row - LATE_ROW, 0), EDGE), EDGE), :]
            return jnp.where(row < LATE_ROW, here, then)

        sides = jnp.concatenate(
            [
                piece(0).astype(jnp.float32),
                jnp.zeros((HALF - EDGE - RADIUS, TILE), jnp.float32),
                piece(1).astype(jnp.float32)[:RADIUS],
            ],
            axis=0,
        )
        sides = jnp.transpose(sides).astype(jnp.bfloat16)

        def place(start, rows, middle_a, middle_b, left_b, right_a):
            low = lax.broadcasted_iota(jnp.int32, (rows, HALF), 1) < HALF // 2
            window[half, start : start + rows, :HALF] = middle_a
            window[half, start : start + rows, HALF:] = jnp.where(low, middle_b, left_b)
            second = window_rows + start
            window[half, second : second + rows, :HALF] = middle_b
            window[half, second : second + rows, HALF:] = jnp.where(low, right_a, middle_a)

        center = aligned[plan[at + 8]]
        place(EDGE, TILE, center[:, :HALF], center[:, HALF:], sides, sides)
        for start, n in ((0, 2), (EDGE + TILE, 5)):
            middle, left, right = piece(n), piece(n + 1), piece(n + 2)
            if start == 0:
                middle, left, right = lowered(middle), lowered(left), lowered(right)
            place(start, EDGE, middle[:, :HALF], middle[:, HALF:], left[:, HALF:], right[:, :HALF])

    def finish(k, half, share):
        at = base(k)
        local = plan[at + 11]
        rows = pl.ds(TILE - plan[at + 9], TILE)
        back = jnp.concatenate([total[half, 0, rows, :], total[half, 1, rows, :]], axis=1)
        back = pltpu.roll(back, plan[at + 10], 1)
        so_far = jnp.where(plan[at + 15] < SLOTS, start[local], out[local])
        out[local] = so_far - back * share

    count = plan[3 * SLOTS]
    owned = out.shape[0]

    def leave(local):
        return pltpu.make_async_copy(out.at[local], result.at[local], sems.at[local])

    for local in range(owned):
        named = sum(
            jnp.where((plan[k] >= 0) & (plan[base(plan[2 * SLOTS + k]) + 11] == local), 1, 0) for k in range(SLOTS)
        )

        @pl.when(named == 0)
        def _(local=local):
            pltpu.make_async_copy(start.at[local], result.at[local], sems.at[local]).start()

    @pl.when(count > 0)
    def _():
        build(0, 0)

    def step(k, carry):
        half = lax.rem(k, 2)
        at = base(k)
        coef_row = pl.multiple_of(plan[at + 13] * RECORD, EDGE)
        block = frames[pl.ds(coef_row, COEF_ROWS), :HALF].astype(jnp.float32)
        rows = lax.broadcasted_iota(jnp.int32, block.shape, 0)
        mine = (lax.rem(rows, strip_lanes) == plan[at + 14]) & (rows < 3 * strip_lanes)
        weights = jnp.sum(jnp.where(mine, block, 0.0), axis=0, keepdims=True)
        lanes = columns * REACH
        for n in range(0, columns, 2):
            if n == 2:
                finish(jnp.maximum(k - 1, 0), 1 - half, jnp.where(k > 0, share_of(plan[base(jnp.maximum(k - 1, 0)) + 12]), 0.0))
            if n == 4:
                build(jnp.minimum(k + 1, count - 1), 1 - half)
            wide = min(2, columns - n)
            h = jnp.dot(window[half], across[:, n * HALF : (n + wide) * HALF], preferred_element_type=jnp.float32)
            h = h.astype(jnp.bfloat16)
            for m in range(wide):
                to = (n + m) * REACH
                for c in range(2):
                    for r in range(2):
                        start = c * window_rows + r * HALF
                        spread[r, to : to + REACH, c * HALF : (c + 1) * HALF] = h[
                            start : start + REACH, m * HALF : (m + 1) * HALF
                        ]
            for at in range(n * REACH // HALF * HALF, min(lanes, (n + 2) * REACH // HALF * HALF), HALF):
                wide_at = min(HALF, lanes - at)
                lane = lax.broadcasted_iota(jnp.int32, (1, wide_at), 1) + at
                mix = jnp.zeros((HALF, wide_at), jnp.float32)
                one = at // REACH
                two = min((at + wide_at - 1) // REACH, columns - 1)
                for v in range(ORDERS):
                    weight = weights[:, one * ORDERS + v : one * ORDERS + v + 1]
                    if two != one:
                        other = weights[:, two * ORDERS + v : two * ORDERS + v + 1]
                        weight = jnp.where(lane < two * REACH, weight, other)
                    mix = mix + weight * mixing[v, :, at : at + wide_at]
                mixes[:, at : at + wide_at] = mix.astype(jnp.bfloat16)
        for r in range(2):
            matched = jnp.dot(mixes[...], spread[r], preferred_element_type=jnp.float32)
            for c in range(2):
                for at_row in (r * HALF, TILE + r * HALF):
                    total[half, c, at_row : at_row + HALF, :] = matched[:, c * HALF : (c + 1) * HALF]
        before = base(jnp.maximum(k - 1, 0))

        @pl.when((k > 0) & (lax.rem(plan[before + 15], SLOTS) == 0))
        def _():
            leave(plan[before + 11]).start()

        return carry

    lax.fori_loop(0, count, step, 0)

    @pl.when(count > 0)
    def _():
        finish(count - 1, lax.rem(count - 1, 2), share_of(plan[base(count - 1) + 12]))
        leave(plan[base(count - 1) + 11]).start()

    for local in range(owned):
        leave(local).wait()


def step(science, patches, margin, kernel_coef, ccd_first):
    strips = lax.axis_size("visit")
    owned = patches.shape[0]
    per_strip = science.shape[1] // TILE
    sizes = (strips, per_strip, owned)
    margin = margin.T
    smem = pl.BlockSpec(memory_space=pltpu.SMEM)
    vmem = pl.BlockSpec(memory_space=pltpu.VMEM)
    hbm = pl.BlockSpec(memory_space=pl.ANY)
    stays = pl.BlockSpec(memory_space=pltpu.HBM)
    bf16 = jnp.bfloat16
    f32 = jnp.float32
    columns = SIGMAS * ORDERS
    tables = pl.pallas_call(
        fill_tables,
        out_shape=(
            jax.ShapeDtypeStruct((TILE, columns * HALF), bf16),
            jax.ShapeDtypeStruct((ORDERS, HALF, columns * REACH), f32),
        ),
        in_specs=[],
        out_specs=(vmem, vmem),
        compiler_params=pltpu.CompilerParams(vmem_limit_bytes=8 * 2**20),
        cost_estimate=pl.CostEstimate(flops=2 * 10**9, bytes_accessed=3 * 2**20, transcendentals=10**6),
        name="tables",
    )()
    aligned, to_chip, to_next, to_two, to_far = pl.pallas_call(
        functools.partial(pack_kernel, sizes),
        out_shape=(
            jax.ShapeDtypeStruct((SLOTS, TILE, TILE), bf16),
            jax.ShapeDtypeStruct((RECORD + CAP * TILE, TILE), bf16),
            jax.ShapeDtypeStruct((NEAR_ROWS + CAP * TILE, TILE), bf16),
            jax.ShapeDtypeStruct((TWO_ROWS, TILE), bf16),
            jax.ShapeDtypeStruct((PIECE_ROWS, TILE), bf16),
        ),
        in_specs=[stays] * 4,
        out_specs=(vmem, vmem, vmem, vmem, vmem),
        scratch_shapes=[
            pltpu.SMEM(margin.shape, jnp.int32),
            pltpu.VMEM(kernel_coef.shape[::-1], f32),
            pltpu.VMEM((SLOTS, 2, 2 * TILE, HALF), f32),
            pltpu.VMEM((2 * per_strip, 2 * TILE, HALF), f32),
            pltpu.SMEM((SLOTS,), jnp.int32),
            pltpu.SemaphoreType.DMA((SLOTS, 2)),
            pltpu.SemaphoreType.DMA((2 * per_strip,)),
            pltpu.SemaphoreType.DMA((2,)),
        ],
        compiler_params=pltpu.CompilerParams(vmem_limit_bytes=52 * 2**20),
        name="pack",
    )(margin, kernel_coef.T, patches, science)

    on_chip = [(i, i ^ 1) for i in range(strips)]
    next_chip = [p for i in range(1, strips - 1, 2) for p in ((i, i + 1), (i + 1, i))]
    far = [p for i in range(1, strips - 3, 2) for p in ((i, i + 3), (i + 3, i))]
    two = [p for i in range(0, strips - 2, 2) for p in ((i, i + 2), (i + 3, i + 1))]
    from_next = lax.ppermute(to_next, "visit", next_chip)
    from_two = lax.ppermute(to_two, "visit", two)
    from_far = lax.ppermute(to_far, "visit", far)
    from_chip = lax.ppermute(to_chip, "visit", on_chip)

    planned = pl.pallas_call(
        functools.partial(plan_kernel, sizes),
        out_shape=(
            jax.ShapeDtypeStruct((ENTRY * (HEAD + SLOTS),), jnp.int32),
            jax.ShapeDtypeStruct(patches.shape, f32),
        ),
        in_specs=[smem, smem] + [vmem] * 2,
        out_specs=(smem, vmem),
        scratch_shapes=[pltpu.SMEM(((2 * STRIPS - 1) * per_strip * KINDS,), jnp.int32)],
        compiler_params=pltpu.CompilerParams(vmem_limit_bytes=12 * 2**20),
        name="plan",
    )(margin, ccd_first, from_chip, science)
    from_next, from_two, from_far, planned = lax.optimization_barrier((from_next, from_two, from_far, planned))
    plan, first = planned
    relay = jnp.concatenate([from_next[:NEAR_ROWS], from_two], axis=0)
    from_across = lax.ppermute(relay, "visit", on_chip)
    frames, start = pl.pallas_call(
        prepare_kernel,
        out_shape=(jax.ShapeDtypeStruct((LATE_ROW, TILE), bf16), jax.ShapeDtypeStruct(patches.shape, f32)),
        in_specs=[smem] + [vmem] * 6,
        out_specs=(vmem, vmem),
        compiler_params=pltpu.CompilerParams(vmem_limit_bytes=8 * 2**20),
        name="prepare",
    )(plan, to_chip, from_chip, from_next, from_two, from_far, first)

    return pl.pallas_call(
        functools.partial(match_kernel, per_strip),
        out_shape=jax.ShapeDtypeStruct(patches.shape, f32),
        in_specs=[smem] + [vmem] * 6,
        out_specs=stays,
        scratch_shapes=[
            pltpu.VMEM((LATE * RECORD, TILE), bf16),
            pltpu.VMEM((2, 2 * (TILE + 2 * EDGE), TILE), bf16),
            pltpu.VMEM((2, columns * REACH, TILE), bf16),
            pltpu.VMEM((HALF, columns * REACH), bf16),
            pltpu.VMEM((2, 2, 2 * TILE, HALF), f32),
            pltpu.VMEM(patches.shape, f32),
            pltpu.SemaphoreType.DMA((patches.shape[0],)),
        ],
        compiler_params=pltpu.CompilerParams(vmem_limit_bytes=24 * 2**20),
        name="match",
    )(plan, aligned, frames, from_across, *tables, start)


def solution(mesh):
    in_specs = (
        P(("grp", "visit"), None),
        P(("grp", "visit"), None, None),
        P("grp", None),
        P(None, ("grp", "visit")),
        P("grp"),
    )
    out_specs = P(("grp", "visit"), None, None)
    return jax.shard_map(step, mesh=mesh, in_specs=in_specs, out_specs=out_specs, check_vma=False)
```

```python
import functools

import jax
import jax.numpy as jnp
import numpy as np
from jax import lax
from jax.experimental import pallas as pl
from jax.experimental.pallas import tpu as pltpu
from jax.sharding import PartitionSpec as P

TILE = 256
HALF = 128
RADIUS = 10
SIGMAS = 3
ORDERS = 3
EDGE = 16
CAP = 2
STRIPS = 3
SLOTS = STRIPS * CAP
KINDS = 4
TOP, BOTTOM, LEFT, RIGHT = range(KINDS)
PIECES = SLOTS * KINDS
COEF_ROWS = 16
NEAR = 8
PIECE_ROWS = CAP * EDGE
NEAR_ROWS = COEF_ROWS + NEAR * CAP * RADIUS
TWO_ROWS = (STRIPS * KINDS - NEAR) * CAP * RADIUS
RECORD = COEF_ROWS + PIECES * EDGE
EARLY = 5
LATE = 2
ZEROS = EARLY * RECORD
LATE_ROW = ZEROS + EDGE
ENTRY = 16
HEAD = 2
REACH = HALF + 2 * EDGE


def owned_slots(margin, owner, strips, per_strip, owned):
    slots = []
    for q in range(STRIPS):
        strip = owner - 1 + q
        inside = (strip >= 0) & (strip < strips)
        base = jnp.clip(strip, 0, strips - 1) * per_strip
        count = jnp.int32(0)
        found = [jnp.int32(-1) for _ in range(CAP)]
        for s in range(per_strip):
            mine = inside & (owner_of(margin[0, base + s], owned) == owner)
            for j in range(CAP):
                found[j] = jnp.where(mine & (count == j), base + s, found[j])
            count = count + jnp.where(mine, 1, 0)
        slots.extend(found)
    return slots


def sign_of(owner):
    return 1 - 2 * lax.rem(owner, 2)


def piece_position(relative, kind, sign):
    along = relative * sign
    facing = jnp.where(sign > 0, kind, jnp.where(kind == TOP, BOTTOM, jnp.where(kind == BOTTOM, TOP, kind)))
    middle = jnp.where(facing == TOP, 4, jnp.where(facing == BOTTOM, 11, facing + 3))
    return jnp.where(along < 0, facing, jnp.where(along > 0, 7 + facing, middle))


def owner_of(patch, owned):
    if owned & (owned - 1) == 0:
        return lax.shift_right_logical(patch, jnp.int32(owned.bit_length() - 1))
    return lax.div(patch, owned)


def packed(record, first, count):
    rows = record[COEF_ROWS + first * EDGE : COEF_ROWS + (first + count) * EDGE, :].astype(jnp.float32)
    return jnp.concatenate([rows[n * EDGE : n * EDGE + RADIUS] for n in range(count)], axis=0).astype(jnp.bfloat16)


def spaced(rows):
    rows = rows.astype(jnp.float32)
    empty = jnp.zeros((EDGE - RADIUS, TILE), jnp.float32)
    pieces = []
    for n in range(rows.shape[0] // RADIUS):
        pieces += [rows[n * RADIUS : (n + 1) * RADIUS], empty]
    return jnp.concatenate(pieces, axis=0).astype(jnp.bfloat16)


def column_half(patches, local, patch_buf, k, n, sem):
    source = patches.at[local, :, pl.ds(n * HALF, HALF)]
    return pltpu.make_async_copy(source, patch_buf.at[k, n, pl.ds(0, TILE)], sem.at[k, n])


def pack_kernel(sizes, margin_hbm, coef_hbm, patches, science, aligned, to_chip, to_next, to_two, to_far,
                margin, coef, patch_buf, science_buf, slot_of, patch_sem, science_sem, small_sem):
    strips, per_strip, owned = sizes
    tables = [
        pltpu.make_async_copy(a, b, small_sem.at[n]) for n, (a, b) in enumerate(((margin_hbm, margin), (coef_hbm, coef)))
    ]
    for copy in tables:
        copy.start()
    blocks = [
        pltpu.make_async_copy(
            science.at[:, pl.ds(n * HALF, HALF)], science_buf.at[n, pl.ds(0, TILE)], science_sem.at[n]
        )
        for n in range(2 * per_strip)
    ]
    for copy in blocks:
        copy.start()
    for copy in tables:
        copy.wait()
    owner = lax.axis_index("visit")
    sign = sign_of(owner)
    slots = owned_slots(margin, owner, strips, per_strip, owned)
    for k in range(SLOTS):
        slot_of[k] = slots[k]

        @pl.when(slots[k] >= 0)
        def _(k=k):
            local = lax.rem(margin[0, jnp.maximum(slots[k], 0)], owned)
            for n in range(2):
                column_half(patches, local, patch_buf, k, n, patch_sem).start()

    values = coef[...]
    bases = values.shape[1]
    high = values.astype(jnp.bfloat16).astype(jnp.float32)
    middle = (values - high).astype(jnp.bfloat16).astype(jnp.float32)
    low = values - high - middle
    parts = jnp.concatenate([high, middle, low, jnp.zeros_like(low)], axis=0).astype(jnp.bfloat16)
    to_chip[:COEF_ROWS, :bases] = parts
    to_next[:COEF_ROWS, :bases] = parts

    for copy in blocks:
        copy.wait()
    counts = [jnp.int32(0), jnp.int32(0)]
    for s in range(per_strip):
        tile = owner * per_strip + s
        offset = lax.div(margin[0, tile], owned) - owner

        @pl.when(offset != 0)
        def _(s=s, tile=tile, offset=offset, counts=tuple(counts)):
            back = lax.rem(TILE - margin[2, tile], TILE)
            rows = pl.ds(margin[1, tile], TILE)
            for n in (2 * s, 2 * s + 1):
                science_buf[n, TILE:, :] = science_buf[n, :TILE, :]
            moved = jnp.concatenate([science_buf[2 * s, rows, :], science_buf[2 * s + 1, rows, :]], axis=1)
            moved = pltpu.roll(moved, back, 1)
            moved16 = moved.astype(jnp.bfloat16)

            @pl.when(offset == sign)
            def _():
                to_chip[pl.ds(pl.multiple_of(RECORD + counts[0] * TILE, EDGE), TILE), :] = moved16

            @pl.when(offset != sign)
            def _():
                to_next[pl.ds(pl.multiple_of(NEAR_ROWS + counts[1] * TILE, EDGE), TILE), :] = moved16

        counts[0] = counts[0] + jnp.where(offset == sign, 1, 0)
        counts[1] = counts[1] + jnp.where(offset == -sign, 1, 0)

    def strip_step(q, carry):
        for j in range(CAP):
            k = q * CAP + j
            tile = slot_of[k]

            @pl.when(tile >= 0)
            def _(k=k, tile=tile):
                local = lax.rem(margin[0, tile], owned)
                for n in range(2):
                    column_half(patches, local, patch_buf, k, n, patch_sem).wait()

        for j in range(CAP):
            k = q * CAP + j
            tile = jnp.maximum(slot_of[k], 0)
            for n in range(2):
                patch_buf[k, n, TILE:, :] = patch_buf[k, n, :TILE, :]
            rows = pl.ds(TILE - margin[1, tile], TILE)
            moved = jnp.concatenate([patch_buf[k, 0, rows, :], patch_buf[k, 1, rows, :]], axis=1)
            moved = pltpu.roll(moved, margin[2, tile], 1)
            moved16 = moved.astype(jnp.bfloat16)
            aligned[k] = moved16
            left = jnp.transpose(moved[:, :HALF])[:EDGE]
            right_edge = jnp.transpose(moved[:, TILE - HALF :])[HALF - RADIUS :]
            empty = jnp.zeros((EDGE - RADIUS, TILE), jnp.float32)
            bottom = jnp.concatenate([moved[TILE - RADIUS :], empty], axis=0)
            right_edge = jnp.concatenate([right_edge, empty], axis=0)
            edges = [moved16[:EDGE]] + [edge.astype(jnp.bfloat16) for edge in (bottom, left, right_edge)]
            for kind in range(KINDS):
                position = piece_position(q - 1, jnp.int32(kind), sign)
                row = pl.multiple_of(COEF_ROWS + (position * CAP + j) * EDGE, EDGE)
                to_chip[pl.ds(row, EDGE), :] = edges[kind]
        return carry

    for k in range(SLOTS):

        @pl.when(slots[k] < 0)
        def _(k=k):
            patch_buf[k, :, :TILE, :] = jnp.zeros((2, TILE, HALF), jnp.float32)

    lax.fori_loop(0, STRIPS, strip_step, 0)
    to_far[...] = to_chip[COEF_ROWS : COEF_ROWS + PIECE_ROWS, :]
    to_next[COEF_ROWS:NEAR_ROWS, :] = packed(to_chip, 0, NEAR * CAP)
    to_two[...] = packed(to_chip, NEAR * CAP, PIECES - NEAR * CAP)


def profile(u, sigma, order):
    taps = np.arange(-RADIUS, RADIUS + 1).astype(np.float32)
    total = float(np.sum(np.exp(-taps * taps / np.float32(2.0 * sigma * sigma)), dtype=np.float32))
    shape = jnp.where(jnp.abs(u) <= RADIUS, jnp.exp(-u * u / (2.0 * sigma * sigma)) / total, 0.0)
    for _ in range(order):
        shape = shape * (u / sigma)
    return shape


def fill_tables(across, mixing):
    w = lax.broadcasted_iota(jnp.int32, (TILE, HALF), 0) - lax.broadcasted_iota(jnp.int32, (TILE, HALF), 1)
    w = jnp.where(w > HALF, w - TILE, w).astype(jnp.float32)
    for g in range(SIGMAS):
        for h in range(ORDERS):
            n = g * ORDERS + h
            across[:, n * HALF : (n + 1) * HALF] = profile(w, 0.75 * 2.0**g, h).astype(jnp.bfloat16)
    lanes = SIGMAS * ORDERS * REACH
    for at in range(0, lanes, HALF):
        wide = min(HALF, lanes - at)
        lane = lax.broadcasted_iota(jnp.int32, (HALF, wide), 1) + at
        row = lax.broadcasted_iota(jnp.int32, (HALF, wide), 0)
        one = at // REACH
        two = (at + wide - 1) // REACH
        start = jnp.where(lane < two * REACH, one * REACH, two * REACH)
        u = (lane - start - row - EDGE).astype(jnp.float32)
        low, high = one // ORDERS, two // ORDERS
        sigma = 0.75 * 2.0**low
        if high != low:
            sigma = jnp.where(lane < two * REACH, sigma, 0.75 * 2.0**high)
        totals = []
        for g in (low, high):
            taps = np.arange(-RADIUS, RADIUS + 1).astype(np.float32)
            totals.append(float(np.sum(np.exp(-taps * taps / np.float32(2.0 * (0.75 * 2.0**g) ** 2)), dtype=np.float32)))
        total = totals[0] if high == low else jnp.where(lane < two * REACH, totals[0], totals[1])
        shape = jnp.where(jnp.abs(u) <= RADIUS, jnp.exp(-u * u / (2.0 * sigma * sigma)) / total, 0.0)
        for v in range(ORDERS):
            mixing[v, :, at : at + wide] = shape
            shape = shape * (u / sigma)


def plan_kernel(sizes, margin, ccd_first, from_chip, science, plan, first, rows):
    strips, per_strip, owned = sizes
    owner = lax.axis_index("visit")
    sign = sign_of(owner)
    slots = owned_slots(margin, owner, strips, per_strip, owned)
    ids = [jnp.where(t >= 0, margin[0, jnp.maximum(t, 0)], -1) for t in slots]
    counts = [sum(jnp.where(other == mine, 1, 0) for other in ids) for mine in ids]
    entry = jnp.int32(0)
    places = []
    for k in range(SLOTS):
        places.append(entry)
        entry = entry + jnp.where(slots[k] >= 0, 1, 0)
        plan[k] = slots[k]
        plan[SLOTS + k] = counts[k]
        plan[2 * SLOTS + k] = places[k]
        later = sum((jnp.where(other == ids[k], 1, 0) for other in ids[k + 1 :]), jnp.int32(0))
        sooner = sum((jnp.where(other == ids[k], 1, 0) for other in ids[:k]), jnp.int32(0))
        plan[3 * SLOTS + 1 + k] = later + SLOTS * sooner
    plan[3 * SLOTS] = entry

    for i in range(2 * STRIPS - 1):
        strip = jnp.clip(owner - STRIPS + 1 + i, 0, strips - 1)
        owners = [owner_of(margin[0, strip * per_strip + n], owned) for n in range(per_strip)]
        for n, its_owner in enumerate(owners):
            rank = sum((jnp.where(other == its_owner, 1, 0) for other in owners[:n]), jnp.int32(0))
            member = (its_owner - owner) * sign + 3
            start = member * RECORD + jnp.where(member < EARLY, 0, EDGE) + COEF_ROWS + rank * EDGE
            its_sign = sign_of(its_owner)
            for kind in range(KINDS):
                place = piece_position(strip - its_owner, jnp.int32(kind), its_sign)
                rows[(i * per_strip + n) * KINDS + kind] = start + place * PIECE_ROWS

    def piece_row(strip, position, kind, allowed):
        inside = (position >= 0) & (position < per_strip) & allowed
        at = ((strip - owner + STRIPS - 1) * per_strip + position) * KINDS + kind
        return jnp.where(inside, rows[jnp.where(inside, at, 0)], ZEROS)

    def fill(k, carry):
        tile = plan[k]

        @pl.when(tile >= 0)
        def _():
            q = lax.div(k, CAP)
            j = lax.rem(k, CAP)
            strip = owner - 1 + q
            position = tile - strip * per_strip
            local = lax.rem(margin[0, tile], owned)
            up = lax.rem(TILE - margin[1, tile], TILE)
            back = lax.rem(TILE - margin[2, tile], TILE)
            yes = owner >= 0
            keep_top = (strip > 0) & (ccd_first[strip] == 0)
            keep_bottom = (strip < strips - 1) & (ccd_first[jnp.minimum(strip + 1, strips - 1)] == 0)
            at = ENTRY * (plan[2 * SLOTS + k] + HEAD)
            member = (q - 1) * sign
            pieces = (
                (strip, position + 1, LEFT, yes),
                (strip, position - 1, RIGHT, yes),
                (strip - 1, position, BOTTOM, keep_top),
                (strip - 1, position - 1, BOTTOM, keep_top),
                (strip - 1, position + 1, BOTTOM, keep_top),
                (strip + 1, position, TOP, keep_bottom),
                (strip + 1, position - 1, TOP, keep_bottom),
                (strip + 1, position + 1, TOP, keep_bottom),
            )
            for n, args in enumerate(pieces):
                plan[at + n] = piece_row(*args)
            plan[at + 8] = k
            plan[at + 9] = up
            plan[at + 10] = back
            plan[at + 11] = local
            plan[at + 12] = plan[SLOTS + k]
            plan[at + 13] = member + 3
            plan[at + 14] = position
            plan[at + 15] = plan[3 * SLOTS + 1 + k]
            share = share_of(plan[SLOTS + k])

            @pl.when(member == 0)
            def _():
                start = pl.multiple_of(position * TILE, TILE)
                moved = pltpu.roll(pltpu.roll(science[:, pl.ds(start, TILE)], up, 0), back, 1)
                first[local] = first[local] + moved * share

            @pl.when(member == 1)
            def _():
                start = pl.multiple_of(RECORD + j * TILE, EDGE)
                first[local] = first[local] + from_chip[pl.ds(start, TILE), :].astype(jnp.float32) * share

        return carry

    first[...] = jnp.zeros(first.shape, jnp.float32)
    lax.fori_loop(0, SLOTS, fill, 0)


def share_of(count):
    share = jnp.float32(1.0)
    for n in range(2, SLOTS + 1):
        share = jnp.where(count == n, jnp.float32(1.0 / n), share)
    return share


def base(k):
    return ENTRY * (k + HEAD)


def prepare_kernel(plan, own_record, from_chip, from_next, from_two, from_far, first, frames, start):
    def put(member, row, value):
        at = member * RECORD + row
        frames[at : at + value.shape[0], :] = value

    near = COEF_ROWS + NEAR * PIECE_ROWS
    put(0, COEF_ROWS, from_far[...])
    put(1, near, spaced(from_two[...]))
    put(2, 0, from_next[:COEF_ROWS, :])
    put(2, COEF_ROWS, spaced(from_next[COEF_ROWS:NEAR_ROWS, :]))
    put(3, 0, own_record[:RECORD, :])
    put(4, 0, from_chip[:RECORD, :])
    put(EARLY, 0, jnp.zeros((EDGE, TILE), jnp.bfloat16))
    start[...] = first[...]
    for k in range(SLOTS):

        @pl.when((plan[k] >= 0) & (plan[base(plan[2 * SLOTS + k]) + 13] == 2))
        def _(k=k):
            at = base(plan[2 * SLOTS + k])
            local = plan[at + 11]
            row = NEAR_ROWS + (k % CAP) * TILE
            arrived = from_next[row : row + TILE, :].astype(jnp.float32)
            start[local] = start[local] + arrived * share_of(plan[at + 12])


def match_kernel(per_strip, plan, aligned, frames, from_across, across, mixing, start, result,
                 late, window, spread, mixes, total, out, sems):
    near = COEF_ROWS + NEAR * PIECE_ROWS
    late[COEF_ROWS:near, :] = spaced(from_across[COEF_ROWS:NEAR_ROWS, :])
    late[RECORD + near :, :] = spaced(from_across[NEAR_ROWS:, :])
    columns = SIGMAS * ORDERS
    window_rows = TILE + 2 * EDGE
    total[...] = jnp.zeros(total.shape, jnp.float32)
    strip_lanes = per_strip

    def lowered(edge):
        empty = jnp.zeros((EDGE - RADIUS, TILE), jnp.float32)
        return jnp.concatenate([empty, edge.astype(jnp.float32)[:RADIUS]], axis=0).astype(jnp.bfloat16)

    def build(k, half):
        at = base(k)

        def piece(n):
            row = plan[at + n]
            here = frames[pl.ds(pl.multiple_of(jnp.minimum(row, ZEROS), EDGE), EDGE), :]
            then = late[pl.ds(pl.multiple_of(jnp.maximum(row - LATE_ROW, 0), EDGE), EDGE), :]
            return jnp.where(row < LATE_ROW, here, then)

        sides = jnp.concatenate(
            [
                piece(0).astype(jnp.float32),
                jnp.zeros((HALF - EDGE - RADIUS, TILE), jnp.float32),
                piece(1).astype(jnp.float32)[:RADIUS],
            ],
            axis=0,
        )
        sides = jnp.transpose(sides).astype(jnp.bfloat16)

        def place(start, rows, middle_a, middle_b, left_b, right_a):
            low = lax.broadcasted_iota(jnp.int32, (rows, HALF), 1) < HALF // 2
            window[half, start : start + rows, :HALF] = middle_a
            window[half, start : start + rows, HALF:] = jnp.where(low, middle_b, left_b)
            second = window_rows + start
            window[half, second : second + rows, :HALF] = middle_b
            window[half, second : second + rows, HALF:] = jnp.where(low, right_a, middle_a)

        center = aligned[plan[at + 8]]
        place(EDGE, TILE, center[:, :HALF], center[:, HALF:], sides, sides)
        for start, n in ((0, 2), (EDGE + TILE, 5)):
            middle, left, right = piece(n), piece(n + 1), piece(n + 2)
            if start == 0:
                middle, left, right = lowered(middle), lowered(left), lowered(right)
            place(start, EDGE, middle[:, :HALF], middle[:, HALF:], left[:, HALF:], right[:, :HALF])

    def finish(k, half, share):
        at = base(k)
        local = plan[at + 11]
        back = pltpu.roll(pltpu.roll(total[half], plan[at + 9], 0), plan[at + 10], 1)
        so_far = jnp.where(plan[at + 15] < SLOTS, start[local], out[local])
        out[local] = so_far - back * share

    count = plan[3 * SLOTS]
    owned = out.shape[0]

    def leave(local):
        return pltpu.make_async_copy(out.at[local], result.at[local], sems.at[local])

    for local in range(owned):
        named = sum(
            jnp.where((plan[k] >= 0) & (plan[base(plan[2 * SLOTS + k]) + 11] == local), 1, 0) for k in range(SLOTS)
        )

        @pl.when(named == 0)
        def _(local=local):
            pltpu.make_async_copy(start.at[local], result.at[local], sems.at[local]).start()

    @pl.when(count > 0)
    def _():
        build(0, 0)

    def step(k, carry):
        half = lax.rem(k, 2)
        at = base(k)
        coef_row = pl.multiple_of(plan[at + 13] * RECORD, EDGE)
        block = frames[pl.ds(coef_row, COEF_ROWS), :HALF].astype(jnp.float32)
        rows = lax.broadcasted_iota(jnp.int32, block.shape, 0)
        mine = (lax.rem(rows, strip_lanes) == plan[at + 14]) & (rows < 3 * strip_lanes)
        weights = jnp.sum(jnp.where(mine, block, 0.0), axis=0, keepdims=True)
        lanes = columns * REACH
        for n in range(0, columns, 2):
            if n == 2:
                finish(jnp.maximum(k - 1, 0), 1 - half, jnp.where(k > 0, share_of(plan[base(jnp.maximum(k - 1, 0)) + 12]), 0.0))
            if n == 4:
                build(jnp.minimum(k + 1, count - 1), 1 - half)
            wide = min(2, columns - n)
            h = jnp.dot(window[half], across[:, n * HALF : (n + wide) * HALF], preferred_element_type=jnp.float32)
            h = h.astype(jnp.bfloat16)
            for m in range(wide):
                to = (n + m) * REACH
                for c in range(2):
                    for r in range(2):
                        start = c * window_rows + r * HALF
                        spread[r, to : to + REACH, c * HALF : (c + 1) * HALF] = h[
                            start : start + REACH, m * HALF : (m + 1) * HALF
                        ]
            for at in range(n * REACH // HALF * HALF, min(lanes, (n + 2) * REACH // HALF * HALF), HALF):
                wide_at = min(HALF, lanes - at)
                lane = lax.broadcasted_iota(jnp.int32, (1, wide_at), 1) + at
                mix = jnp.zeros((HALF, wide_at), jnp.float32)
                one = at // REACH
                two = min((at + wide_at - 1) // REACH, columns - 1)
                for v in range(ORDERS):
                    weight = weights[:, one * ORDERS + v : one * ORDERS + v + 1]
                    if two != one:
                        other = weights[:, two * ORDERS + v : two * ORDERS + v + 1]
                        weight = jnp.where(lane < two * REACH, weight, other)
                    mix = mix + weight * mixing[v, :, at : at + wide_at]
                mixes[:, at : at + wide_at] = mix.astype(jnp.bfloat16)
        for r in range(2):
            total[half, r * HALF : (r + 1) * HALF, :] = jnp.dot(
                mixes[...], spread[r], preferred_element_type=jnp.float32
            )
        before = base(jnp.maximum(k - 1, 0))

        @pl.when((k > 0) & (lax.rem(plan[before + 15], SLOTS) == 0))
        def _():
            leave(plan[before + 11]).start()

        return carry

    lax.fori_loop(0, count, step, 0)

    @pl.when(count > 0)
    def _():
        finish(count - 1, lax.rem(count - 1, 2), share_of(plan[base(count - 1) + 12]))
        leave(plan[base(count - 1) + 11]).start()

    for local in range(owned):
        leave(local).wait()


def step(science, patches, margin, kernel_coef, ccd_first):
    strips = lax.axis_size("visit")
    owned = patches.shape[0]
    per_strip = science.shape[1] // TILE
    sizes = (strips, per_strip, owned)
    margin = margin.T
    smem = pl.BlockSpec(memory_space=pltpu.SMEM)
    vmem = pl.BlockSpec(memory_space=pltpu.VMEM)
    hbm = pl.BlockSpec(memory_space=pl.ANY)
    stays = pl.BlockSpec(memory_space=pltpu.HBM)
    bf16 = jnp.bfloat16
    f32 = jnp.float32
    columns = SIGMAS * ORDERS
    tables = pl.pallas_call(
        fill_tables,
        out_shape=(
            jax.ShapeDtypeStruct((TILE, columns * HALF), bf16),
            jax.ShapeDtypeStruct((ORDERS, HALF, columns * REACH), f32),
        ),
        in_specs=[],
        out_specs=(vmem, vmem),
        compiler_params=pltpu.CompilerParams(vmem_limit_bytes=8 * 2**20),
        cost_estimate=pl.CostEstimate(flops=2 * 10**9, bytes_accessed=3 * 2**20, transcendentals=10**6),
        name="tables",
    )()
    aligned, to_chip, to_next, to_two, to_far = pl.pallas_call(
        functools.partial(pack_kernel, sizes),
        out_shape=(
            jax.ShapeDtypeStruct((SLOTS, TILE, TILE), bf16),
            jax.ShapeDtypeStruct((RECORD + CAP * TILE, TILE), bf16),
            jax.ShapeDtypeStruct((NEAR_ROWS + CAP * TILE, TILE), bf16),
            jax.ShapeDtypeStruct((TWO_ROWS, TILE), bf16),
            jax.ShapeDtypeStruct((PIECE_ROWS, TILE), bf16),
        ),
        in_specs=[stays] * 4,
        out_specs=(vmem, vmem, vmem, vmem, vmem),
        scratch_shapes=[
            pltpu.SMEM(margin.shape, jnp.int32),
            pltpu.VMEM(kernel_coef.shape[::-1], f32),
            pltpu.VMEM((SLOTS, 2, 2 * TILE, HALF), f32),
            pltpu.VMEM((2 * per_strip, 2 * TILE, HALF), f32),
            pltpu.SMEM((SLOTS,), jnp.int32),
            pltpu.SemaphoreType.DMA((SLOTS, 2)),
            pltpu.SemaphoreType.DMA((2 * per_strip,)),
            pltpu.SemaphoreType.DMA((2,)),
        ],
        compiler_params=pltpu.CompilerParams(vmem_limit_bytes=52 * 2**20),
        name="pack",
    )(margin, kernel_coef.T, patches, science)

    on_chip = [(i, i ^ 1) for i in range(strips)]
    next_chip = [p for i in range(1, strips - 1, 2) for p in ((i, i + 1), (i + 1, i))]
    far = [p for i in range(1, strips - 3, 2) for p in ((i, i + 3), (i + 3, i))]
    two = [p for i in range(0, strips - 2, 2) for p in ((i, i + 2), (i + 3, i + 1))]
    from_next = lax.ppermute(to_next, "visit", next_chip)
    from_two = lax.ppermute(to_two, "visit", two)
    from_far = lax.ppermute(to_far, "visit", far)
    from_chip = lax.ppermute(to_chip, "visit", on_chip)

    planned = pl.pallas_call(
        functools.partial(plan_kernel, sizes),
        out_shape=(
            jax.ShapeDtypeStruct((ENTRY * (HEAD + SLOTS),), jnp.int32),
            jax.ShapeDtypeStruct(patches.shape, f32),
        ),
        in_specs=[smem, smem] + [vmem] * 2,
        out_specs=(smem, vmem),
        scratch_shapes=[pltpu.SMEM(((2 * STRIPS - 1) * per_strip * KINDS,), jnp.int32)],
        compiler_params=pltpu.CompilerParams(vmem_limit_bytes=12 * 2**20),
        name="plan",
    )(margin, ccd_first, from_chip, science)
    from_next, from_two, from_far = lax.optimization_barrier((from_next, from_two, from_far))
    plan, first = planned
    relay = jnp.concatenate([from_next[:NEAR_ROWS], from_two], axis=0)
    from_across = lax.ppermute(relay, "visit", on_chip)
    frames, start = pl.pallas_call(
        prepare_kernel,
        out_shape=(jax.ShapeDtypeStruct((LATE_ROW, TILE), bf16), jax.ShapeDtypeStruct(patches.shape, f32)),
        in_specs=[smem] + [vmem] * 6,
        out_specs=(vmem, vmem),
        compiler_params=pltpu.CompilerParams(vmem_limit_bytes=8 * 2**20),
        name="prepare",
    )(plan, to_chip, from_chip, from_next, from_two, from_far, first)

    return pl.pallas_call(
        functools.partial(match_kernel, per_strip),
        out_shape=jax.ShapeDtypeStruct(patches.shape, f32),
        in_specs=[smem] + [vmem] * 6,
        out_specs=stays,
        scratch_shapes=[
            pltpu.VMEM((LATE * RECORD, TILE), bf16),
            pltpu.VMEM((2, 2 * (TILE + 2 * EDGE), TILE), bf16),
            pltpu.VMEM((2, columns * REACH, TILE), bf16),
            pltpu.VMEM((HALF, columns * REACH), bf16),
            pltpu.VMEM((2, TILE, TILE), f32),
            pltpu.VMEM(patches.shape, f32),
            pltpu.SemaphoreType.DMA((patches.shape[0],)),
        ],
        compiler_params=pltpu.CompilerParams(vmem_limit_bytes=24 * 2**20),
        name="match",
    )(plan, aligned, frames, from_across, *tables, start)


def solution(mesh):
    in_specs = (
        P(("grp", "visit"), None),
        P(("grp", "visit"), None, None),
        P("grp", None),
        P(None, ("grp", "visit")),
        P("grp"),
    )
    out_specs = P(("grp", "visit"), None, None)
    return jax.shard_map(step, mesh=mesh, in_specs=in_specs, out_specs=out_specs, check_vma=False)
```
